32 devices in a mesh: ctx: 8 (over z, y), head: 4 (over x, core).
Axes of the slice: x: 2, y: 2, z: 4, core: 2. Of those that a mesh axis runs over, the one named last changes fastest.
Arguments:
- tokens: bfloat16 [4096, 2048], P('ctx', 'head'), may hold values from -6 to 6
- value_weight: bfloat16 [2048, 4096], P('ctx', 'head'), may hold values from -0.125 to 0.125
- queries: bfloat16 [4096, 128], P('ctx'), may hold values from -2.390625 to 2.390625
- key_vectors: bfloat16 [4096, 128], P('ctx'), may hold values from -2.390625 to 2.390625
- level_weight: float32 [13, 64, 4096], P(None, 'head', 'ctx'), may hold values from 0.2 to 1
Outputs:
- attended: bfloat16 [4096, 4096], P('ctx', 'head')
The draws below stay inside these ranges and needn't reach their ends.
All inputs are finite; a program needn't handle non-finite values.
Results may differ from the reference program's by a relative error of at most 0.006.
Values may be sent and summed in bfloat16 or wider, within the bound.
No kernel may reach another device: no remote copies, remote signals or barrier semaphores. Data moves between devices by JAX's collectives and lax.ppermute only.
A program may use at most 64 MiB of HBM per device.

```python
import math
import jax
import jax.numpy as jnp
from jax import lax

D = 2048
HEADS = 64
P_SIZE = 64
N = 128
TOK_DEV = 512
STRETCH_BITS = 9
DEV_BITS = 3
LEVELS = 13
TOKENS = 4096


def block_scale(rng, extent, shards, smallest, high):
    def one(position, blocks):
        draws = jax.random.uniform(jax.random.fold_in(jax.random.fold_in(rng, 6), position), (blocks,), jnp.float32, smallest / len(shards), high / len(shards))
        return jnp.repeat(jnp.exp(draws), extent[position] // blocks).reshape((-1,) + (1,) * (len(extent) - position - 1))

    loudness = one(*shards[0])
    for cut in shards[1:]:
        loudness = loudness * one(*cut)
    return loudness


def normal_values(own_key, extent, scale, limit, split=(), dtype=jnp.bfloat16):
    array = jax.random.normal(own_key, extent, jnp.float32) * scale
    if len(split) > 0:
        array = block_scale(own_key, extent, split, -0.22, 0.18) * array
    return jnp.clip(array, min=-limit, max=limit).astype(dtype)


def setup_inputs(seed: int = 0) -> dict:
    seeds = jax.random.split(jax.random.key(seed), 6)
    return {
        "tokens": normal_values(seeds[0], (TOKENS, D), 1.0, 6.0, ((0, 8), (1, 4))),
        "value_weight": normal_values(seeds[1], (D, HEADS * P_SIZE), D ** -0.5, 0.125, ((0, 8), (1, 4))),
        "queries": normal_values(seeds[2], (TOKENS, N), 0.3, 2.390625, ((0, 8),)),
        "key_vectors": normal_values(seeds[3], (TOKENS, N), 0.3, 2.390625, ((0, 8),)),
        "level_weight": jnp.clip(jnp.exp(math.log(1.0) - 1.609438 * jax.random.uniform(seeds[4], (LEVELS, HEADS, TOKENS), jnp.float32) ** block_scale(seeds[4], (LEVELS, HEADS, TOKENS), ((1, 4), (2, 8)), -0.2, 0.2)), 0.2, 1.0),
    }


def reference(tokens, value_weight, queries, key_vectors, level_weight):
    values = jnp.dot(tokens, value_weight, preferred_element_type=jnp.float32).astype(jnp.bfloat16)
    total_len = tokens.shape[0]
    width_all = value_weight.shape[1]
    head_size = width_all // HEADS
    query_wide = queries.astype(jnp.float32)
    key_wide = key_vectors.astype(jnp.float32)
    value_wide = values.astype(jnp.float32)
    diagonal = lax.optimization_barrier(jnp.sum(query_wide * key_wide, axis=1).astype(jnp.bfloat16)).astype(jnp.float32)
    term = diagonal[:, None] * value_wide
    result = level_weight[0].T[:, :, None] * term.reshape(total_len, HEADS, head_size)
    for level_num in range(1, STRETCH_BITS + 1):
        half_len = 2 ** (level_num - 1)
        groups = total_len // (2 * half_len)
        scale = 2.0 ** (-(level_num - 1) / 2.0)
        q_right = query_wide.reshape(groups, 2, half_len, N)[:, 1]
        k_left = key_wide.reshape(groups, 2, half_len, N)[:, 0]
        v_left = value_wide.reshape(groups, 2, half_len, width_all)[:, 0]
        scores = jnp.einsum("bin,bjn->bij", q_right, k_left)
        scores = lax.optimization_barrier(scores.astype(jnp.bfloat16)).astype(jnp.float32)
        mixed = jnp.einsum("bij,bjc->bic", scores, v_left)
        weights = level_weight[level_num].T.reshape(groups, 2, half_len, HEADS)[:, 1] * scale
        addend = weights[..., None] * mixed.reshape(groups, half_len, HEADS, head_size)
        result = result.reshape(groups, 2, half_len, HEADS, head_size).at[:, 1].add(addend)
        result = result.reshape(total_len, HEADS, head_size)
    stretch_count = total_len // TOK_DEV
    states = jnp.einsum("gtn,gtc->gnc", key_wide.reshape(stretch_count, TOK_DEV, N),
                        value_wide.reshape(stretch_count, TOK_DEV, width_all), precision=lax.Precision.HIGHEST)
    for section_bit in range(DEV_BITS):
        level_num = STRETCH_BITS + 1 + section_bit
        scale = 2.0 ** (-(level_num - 1) / 2.0)
        span = 2 ** section_bit
        groups = stretch_count // (2 * span)
        left_sum = states.reshape(groups, 2, span, N, width_all)[:, 0].sum(axis=1)
        state_high = left_sum.astype(jnp.bfloat16)
        state_low = (left_sum - state_high.astype(jnp.float32)).astype(jnp.bfloat16)
        q_right = query_wide.reshape(groups, 2, span * TOK_DEV, N)[:, 1]
        reading = jnp.einsum("gtn,gnc->gtc", q_right, state_high.astype(jnp.float32))
        reading = reading + jnp.einsum("gtn,gnc->gtc", q_right, state_low.astype(jnp.float32))
        weights = level_weight[level_num].T.reshape(groups, 2, span * TOK_DEV, HEADS)[:, 1] * scale
        addend = weights[..., None] * reading.reshape(groups, span * TOK_DEV, HEADS, head_size)
        result = result.reshape(groups, 2, span * TOK_DEV, HEADS, head_size).at[:, 1].add(addend)
        result = result.reshape(total_len, HEADS, head_size)
    return result.reshape(total_len, width_all).astype(jnp.bfloat16)
```

```python
import jax
import jax.numpy as jnp
from jax import lax
from jax.sharding import PartitionSpec as P


def from_partner(block, axis, distance):
    count = lax.axis_size(axis)
    route = []
    for low in range(count):
        high = low | 1 << distance
        if high != low and high < count:
            route += [(low, high), (high, low)]
    return lax.ppermute(block, axis, route)


def gather_pieces(block, axis):
    pieces = [block]
    bits = lax.axis_size(axis).bit_length() - 1
    masks = [0]
    for bit in reversed(range(bits)):
        pieces += [from_partner(piece, axis, bit) for piece in pieces]
        masks += [mask | 1 << bit for mask in masks]
    ordered = [None] * len(pieces)
    for mask, piece in zip(masks, pieces):
        ordered[mask] = piece
    return jnp.stack(ordered)


def body(tokens, value_weight, queries, key_vectors, level_weight):
    length, width_feat = tokens.shape
    depth, width_local = value_weight.shape
    head_local = level_weight.shape[1]
    head_size = width_local // head_local
    state_rows = queries.shape[1]
    stretch_bits = length.bit_length() - 1
    ctx_count = lax.axis_size("ctx")
    dev_bits = ctx_count.bit_length() - 1
    my_index = lax.axis_index("ctx")
    my_head = lax.axis_index("head")

    order = list(range(0, ctx_count, 2)) + list(range(1, ctx_count, 2))[::-1]
    ahead = [(order[i], order[(i + 1) % ctx_count]) for i in range(ctx_count)]
    back = [(b, a) for a, b in ahead]
    half_count = ctx_count // 2
    my_pos = jnp.where(my_index % 2 == 0, my_index // 2, ctx_count - 1 - my_index // 2)

    def origin(offset):
        pos = (my_pos + offset) % ctx_count
        return jnp.where(pos < half_count, 2 * pos, 2 * (ctx_count - 1 - pos) + 1)

    running = jnp.einsum("tn,tf->nf", key_vectors, tokens, preferred_element_type=jnp.float32)
    level_sums = []
    for section_bit in range(dev_bits):
        partner = from_partner(running.astype(jnp.bfloat16), "ctx", section_bit)
        is_right = my_index // 2**section_bit % 2 == 1
        level_sums.append(jnp.where(is_right, partner, jnp.zeros_like(partner)))
        running = running + partner.astype(jnp.float32)
    level_sums = jnp.concatenate(level_sums, axis=0)

    if depth < 128:
        features = lax.all_gather(tokens, "head", axis=1, tiled=True)
        sums = lax.all_gather(level_sums, "head", axis=1, tiled=True)
        weight = lax.all_gather(value_weight, "ctx", axis=0, tiled=True)
        values = jnp.dot(features, weight, preferred_element_type=jnp.float32)
        states = jnp.dot(sums, weight, preferred_element_type=jnp.float32)
    else:
        token_pieces = gather_pieces(tokens, "head")
        sum_pieces = gather_pieces(level_sums, "head")
        blocks = [(0, 0, value_weight)]
        cw = ccw = value_weight
        for step in range(1, half_count):
            cw = lax.ppermute(cw, "ctx", ahead)
            ccw = lax.ppermute(ccw, "ctx", back)
            blocks += [(-step, 0, cw), (step, 0, ccw)]
        half = depth // 2
        blocks += [
            (half_count, 0, lax.ppermute(cw[:half], "ctx", ahead)),
            (half_count, half, lax.ppermute(ccw[half:], "ctx", back)),
        ]

        def product(pieces, block_index, rows_from, weight_rows):
            start = block_index * depth + rows_from
            piece = start // width_feat ^ my_head
            cols = start % width_feat
            part = lax.dynamic_slice(
                pieces, (piece, 0, cols), (1, pieces.shape[1], weight_rows.shape[0])
            )[0]
            return jnp.dot(part, weight_rows, preferred_element_type=jnp.float32)

        values = 0.0
        states = 0.0
        for offset, rows_from, rows in blocks:
            index = origin(offset)
            values = values + product(token_pieces, index, rows_from, rows)
            states = states + product(sum_pieces, index, rows_from, rows)
    values = values.astype(jnp.bfloat16)

    tile_len = min(128, length)
    tile_count = length // tile_len
    tile_bits = tile_len.bit_length() - 1
    q_tiles = queries.reshape(tile_count, tile_len, state_rows)
    k_tiles = key_vectors.reshape(tile_count, tile_len, state_rows)
    v_tiles = values.reshape(tile_count, tile_len, width_local)
    tile_scores = jnp.einsum(
        "bin,bjn->bij", q_tiles, k_tiles, preferred_element_type=jnp.float32
    ).astype(jnp.bfloat16)
    row_pos = lax.broadcasted_iota(jnp.int32, (tile_len, tile_len), 0)
    col_pos = lax.broadcasted_iota(jnp.int32, (tile_len, tile_len), 1)
    differ = jnp.bitwise_xor(row_pos, col_pos)
    pair_level = jnp.zeros((tile_len, tile_len), jnp.int32)
    for bit_num in range(tile_bits):
        pair_level = pair_level + (jnp.right_shift(differ, bit_num) > 0).astype(jnp.int32)
    causal = col_pos <= row_pos
    result = jnp.zeros((length, head_local, head_size), jnp.float32)
    for level_num in range(0, tile_bits + 1):
        scale = 1.0 if level_num == 0 else 2.0 ** (-(level_num - 1) / 2.0)
        chosen = causal & (pair_level == level_num)
        masked = jnp.where(chosen[None], tile_scores, jnp.zeros_like(tile_scores))
        mixed = jnp.einsum("bij,bjc->bic", masked, v_tiles, preferred_element_type=jnp.float32)
        weights = level_weight[level_num].T * scale
        result = result + weights[..., None] * mixed.reshape(length, head_local, head_size)
    for level_num in range(tile_bits + 1, stretch_bits + 1):
        half_len = 2 ** (level_num - 1)
        groups = length // (2 * half_len)
        scale = 2.0 ** (-(level_num - 1) / 2.0)
        q_right = queries.reshape(groups, 2, half_len, state_rows)[:, 1]
        k_left = key_vectors.reshape(groups, 2, half_len, state_rows)[:, 0]
        v_left = values.reshape(groups, 2, half_len, width_local)[:, 0]
        scores = jnp.einsum(
            "bin,bjn->bij", q_right, k_left, preferred_element_type=jnp.float32
        ).astype(jnp.bfloat16)
        mixed = jnp.einsum("bij,bjc->bic", scores, v_left, preferred_element_type=jnp.float32)
        weights = level_weight[level_num].T.reshape(groups, 2, half_len, head_local)[:, 1] * scale
        addend = weights[..., None] * mixed.reshape(groups, half_len, head_local, head_size)
        result = result.reshape(groups, 2, half_len, head_local, head_size).at[:, 1].add(addend)
        result = result.reshape(length, head_local, head_size)
    level_states = states.reshape(dev_bits, state_rows, width_local)
    for section_bit in range(dev_bits):
        level_num = stretch_bits + 1 + section_bit
        scale = 2.0 ** (-(level_num - 1) / 2.0)
        state_high = level_states[section_bit].astype(jnp.bfloat16)
        state_low = (level_states[section_bit] - state_high.astype(jnp.float32)).astype(
            jnp.bfloat16
        )
        reading = jnp.dot(queries, state_high, preferred_element_type=jnp.float32)
        reading = reading + jnp.dot(queries, state_low, preferred_element_type=jnp.float32)
        weights = level_weight[level_num].T * scale
        result = result + weights[..., None] * reading.reshape(length, head_local, head_size)
    return result.reshape(length, width_local).astype(jnp.bfloat16)


def solution(mesh):
    return jax.shard_map(
        body,
        mesh=mesh,
        in_specs=(
            P("ctx", "head"),
            P("ctx", "head"),
            P("ctx", None),
            P("ctx", None),
            P(None, "head", "ctx"),
        ),
        out_specs=P("ctx", "head"),
        check_vma=False,
    )
```

```python
import functools

import jax
import jax.numpy as jnp
from jax import lax
from jax.experimental import pallas as pl
from jax.experimental.pallas import tpu as pltpu
from jax.sharding import PartitionSpec as P

F32 = jnp.float32
BF16 = jnp.bfloat16


def from_partner(block, axis, distance):
    count = lax.axis_size(axis)
    route = []
    for low in range(count):
        high = low | 1 << distance
        if high != low and high < count:
            route += [(low, high), (high, low)]
    return lax.ppermute(block, axis, route)


def gather_pieces(block, axis):
    pieces = [block]
    masks = [0]
    for bit in reversed(range(lax.axis_size(axis).bit_length() - 1)):
        pieces += [from_partner(piece, axis, bit) for piece in pieces]
        masks += [mask | 1 << bit for mask in masks]
    ordered = [None] * len(pieces)
    for mask, piece in zip(masks, pieces):
        ordered[mask] = piece
    return jnp.stack(ordered)


def level_scale(level_num):
    return 1.0 if level_num == 0 else 2.0 ** (-(level_num - 1) / 2.0)


def row_block(length):
    return min(256, length)


def prepare_kernel(near_levels, far_levels, head_size, q_ref, k_ref, w_ref, far_ref, *rest):
    near_refs, (score_ref,) = rest[:-1], rest[-1:]
    length = q_ref.shape[0]
    heads = w_ref.shape[0]
    rows = row_block(length)
    tile = min(128, length)

    @pl.when(pl.program_id(0) == 0)
    def _():
        score_ref[...] = lax.dot_general(
            q_ref[...], k_ref[...], (((1,), (1,)), ((), ())), preferred_element_type=F32
        ).astype(BF16).astype(F32)

    t_pos = lax.broadcasted_iota(jnp.int32, (tile, tile), 0)
    s_pos = lax.broadcasted_iota(jnp.int32, (tile, tile), 1)
    differ = jnp.bitwise_xor(t_pos, s_pos)
    tile_levels = tile.bit_length() - 1
    level = jnp.zeros((tile, tile), jnp.int32)
    for bit in range(tile_levels):
        level = level + (jnp.right_shift(differ, bit) > 0).astype(jnp.int32)
    level = jnp.where(s_pos <= t_pos, level, -1)
    for head in range(heads):
        for t_tile in range(length // tile):
            block = t_tile * tile // rows
            depth = (block + 1) * rows
            near_ref = near_refs[block]
            r0 = t_tile * tile - block * rows
            w = w_ref[head, t_tile * tile : (t_tile + 1) * tile, :]
            for s_tile in range(depth // tile):
                c0 = head * depth + s_tile * tile
                if s_tile > t_tile:
                    near_ref[0, r0 : r0 + tile, c0 : c0 + tile] = jnp.zeros((tile, tile), BF16)
                    continue
                if s_tile == t_tile:
                    weight = jnp.zeros((tile, tile), F32)
                    for num in range(tile_levels + 1):
                        weight = jnp.where(level == num, w[:, num : num + 1], weight)
                else:
                    num = tile_levels + (s_tile ^ t_tile).bit_length()
                    weight = w[:, num : num + 1]
                score = score_ref[
                    t_tile * tile : (t_tile + 1) * tile, s_tile * tile : (s_tile + 1) * tile
                ]
                near_ref[0, r0 : r0 + tile, c0 : c0 + tile] = (weight * score).astype(BF16)
    owner = lax.broadcasted_iota(jnp.int32, (length, heads * head_size), 1) // head_size
    for num in range(far_levels):
        lane = near_levels + num
        spread = jnp.broadcast_to(w_ref[0, :, lane : lane + 1], owner.shape)
        for head in range(1, heads):
            spread = jnp.where(owner == head, w_ref[head, :, lane : lane + 1], spread)
        far_ref[num] = spread.astype(BF16)


def prepare(queries, key_vectors, weights, head_size, group, near_levels):
    head_local, length, levels = weights.shape
    far_levels = levels - near_levels
    rows = row_block(length)
    depths = [(block + 1) * rows for block in range(length // rows)]
    whole = pl.BlockSpec(queries.shape, lambda i: (0, 0))
    return pl.pallas_call(
        functools.partial(prepare_kernel, near_levels, far_levels, head_size),
        grid=(head_local // group,),
        in_specs=[whole, whole, pl.BlockSpec((group, length, levels), lambda i: (i, 0, 0))],
        out_specs=[pl.BlockSpec((far_levels, length, group * head_size), lambda i: (0, 0, i))]
        + [pl.BlockSpec((1, rows, group * depth), lambda i: (i, 0, 0)) for depth in depths],
        out_shape=[jax.ShapeDtypeStruct((far_levels, length, head_local * head_size), BF16)]
        + [
            jax.ShapeDtypeStruct((head_local // group, rows, group * depth), BF16)
            for depth in depths
        ],
        scratch_shapes=[pltpu.VMEM((length, length), F32)],
        name="prepare",
    )(queries, key_vectors, weights)


def extend_kernel(count, started, where_ref, *refs):
    out_ref = refs[-1]
    total = refs[2 * count][...] if started else None
    for num in range(count):
        term = jnp.dot(refs[num][0], refs[count + num][...], preferred_element_type=F32)
        total = term if total is None else total + term
    out_ref[...] = total


def extend(total, pieces, where, blocks):
    count = len(blocks)
    rows = pieces.shape[1]
    width = blocks[0].shape[1]
    cols = min(512, width)
    in_specs = [
        pl.BlockSpec(
            (1, rows, block.shape[0]),
            functools.partial(lambda num, i, w: (w[2 * num], 0, w[2 * num + 1]), num),
        )
        for num, block in enumerate(blocks)
    ]
    in_specs += [pl.BlockSpec((block.shape[0], cols), lambda i, w: (0, i)) for block in blocks]
    operands = [pieces] * count + list(blocks)
    if total is not None:
        in_specs.append(pl.BlockSpec((rows, cols), lambda i, w: (0, i)))
        operands.append(total)
    return pl.pallas_call(
        functools.partial(extend_kernel, count, total is not None),
        grid_spec=pltpu.PrefetchScalarGridSpec(
            num_scalar_prefetch=1,
            grid=(width // cols,),
            in_specs=in_specs,
            out_specs=pl.BlockSpec((rows, cols), lambda i, w: (0, i)),
        ),
        out_shape=jax.ShapeDtypeStruct((rows, width), F32),
        input_output_aliases={} if total is None else {2 * count + 1: 0},
        name="extend",
    )(jnp.stack(where), *operands)


def finish_kernel(count, head_size, where_ref, *refs):
    token_refs, sum_refs = refs[:count], refs[count : 2 * count]
    weight_refs = refs[2 * count : 3 * count]
    value_ref, state_ref, q_ref, far_ref = refs[3 * count : 3 * count + 4]
    near_refs, out_ref = refs[3 * count + 4 : -1], refs[-1]
    values, states = value_ref[...], state_ref[...]
    for num in range(count):
        rows = weight_refs[num][...]
        values = values + jnp.dot(token_refs[num][0], rows, preferred_element_type=F32)
        states = states + jnp.dot(sum_refs[num][0], rows, preferred_element_type=F32)
    values = values.astype(BF16)
    length, width = values.shape
    heads = width // head_size
    queries = q_ref[...]
    state_rows = queries.shape[1]
    twice = jnp.concatenate([queries, queries], axis=1)
    owner = lax.broadcasted_iota(jnp.int32, (length, width), 1) // head_size
    masked = [jnp.where(owner == head, values, jnp.zeros_like(values)) for head in range(heads)]
    far = None
    for num in range(far_ref.shape[0]):
        state = states[num * state_rows : (num + 1) * state_rows]
        high = state.astype(BF16)
        low = (state - high.astype(F32)).astype(BF16)
        reading = jnp.dot(twice, jnp.concatenate([high, low], axis=0), preferred_element_type=F32)
        addend = far_ref[num].astype(F32) * reading
        far = addend if far is None else far + addend
    rows = row_block(length)
    for block, near_ref in enumerate(near_refs):
        depth = (block + 1) * rows
        stacked = jnp.concatenate([part[:depth] for part in masked], axis=0)
        near = jnp.dot(near_ref[0], stacked, preferred_element_type=F32)
        low, high = block * rows, (block + 1) * rows
        out_ref[low:high, :] = (near + far[low:high]).astype(BF16)


def finish(values, states, last, token_pieces, sum_pieces, queries, far, near, head_size, group, first):
    length, width = values.shape
    state_rows = states.shape[0]
    cols = group * head_size
    count = len(last)
    where = jnp.stack([num for pair, _ in last for num in pair] or [jnp.int32(0)])
    skip = first // cols

    def part(pieces, num, block):
        return pl.BlockSpec(
            (1, pieces.shape[1], block.shape[0]),
            lambda i, w: (w[2 * num], 0, w[2 * num + 1]),
        )

    in_specs = [part(token_pieces, num, block) for num, (_, block) in enumerate(last)]
    in_specs += [part(sum_pieces, num, block) for num, (_, block) in enumerate(last)]
    in_specs += [pl.BlockSpec((block.shape[0], cols), lambda i, w: (0, i)) for _, block in last]
    in_specs += [
        pl.BlockSpec((length, cols), lambda i, w: (0, i)),
        pl.BlockSpec((state_rows, cols), lambda i, w: (0, i)),
        pl.BlockSpec(queries.shape, lambda i, w: (0, 0)),
        pl.BlockSpec((far.shape[0], length, cols), lambda i, w: (0, 0, skip + i)),
    ]
    in_specs += [pl.BlockSpec((1,) + part.shape[1:], lambda i, w: (skip + i, 0, 0)) for part in near]
    return pl.pallas_call(
        functools.partial(finish_kernel, count, head_size),
        grid_spec=pltpu.PrefetchScalarGridSpec(
            num_scalar_prefetch=1,
            grid=(width // cols,),
            in_specs=in_specs,
            out_specs=pl.BlockSpec((length, cols), lambda i, w: (0, i)),
        ),
        out_shape=jax.ShapeDtypeStruct((length, width), BF16),
        name="finish",
    )(
        where,
        *[token_pieces] * count,
        *[sum_pieces] * count,
        *[block for _, block in last],
        values,
        states,
        queries,
        far,
        *near,
    )


def body(tokens, value_weight, queries, key_vectors, level_weight):
    length, width_feat = tokens.shape
    depth, width_local = value_weight.shape
    levels, head_local = level_weight.shape[:2]
    head_size = width_local // head_local
    near_levels = length.bit_length()
    ctx_count = lax.axis_size("ctx")
    dev_bits = ctx_count.bit_length() - 1
    my_index = lax.axis_index("ctx")
    my_head = lax.axis_index("head")
    group = min(head_local, max(1, 256 // head_size))
    scales = jnp.array([level_scale(num) for num in range(levels)], F32)
    spread = jnp.transpose(level_weight * scales[:, None, None], (1, 2, 0))
    far, *near = prepare(queries, key_vectors, spread, head_size, group, near_levels)

    running = jnp.einsum("tn,tf->nf", key_vectors, tokens, preferred_element_type=F32)
    level_sums = []
    for section_bit in range(dev_bits):
        partner = from_partner(running.astype(BF16), "ctx", section_bit)
        is_right = my_index // 2**section_bit % 2 == 1
        level_sums.append(jnp.where(is_right, partner, jnp.zeros_like(partner)))
        running = running + partner.astype(F32)
    level_sums = jnp.concatenate(level_sums, axis=0)

    if depth % 256 or width_feat % depth:
        features = lax.all_gather(tokens, "head", axis=1, tiled=True)
        sums = lax.all_gather(level_sums, "head", axis=1, tiled=True)
        weight = lax.all_gather(value_weight, "ctx", axis=0, tiled=True)
        values = jnp.dot(features, weight, preferred_element_type=F32)
        states = jnp.dot(sums, weight, preferred_element_type=F32)
        return finish(values, states, [], None, None, queries, far, near, head_size, group, 0)

    order = list(range(0, ctx_count, 2)) + list(range(1, ctx_count, 2))[::-1]
    ahead = [(order[i], order[(i + 1) % ctx_count]) for i in range(ctx_count)]
    back = [(b, a) for a, b in ahead]
    half_count = ctx_count // 2
    my_pos = jnp.where(my_index % 2 == 0, my_index // 2, ctx_count - 1 - my_index // 2)

    def place(offset, rows_from, block):
        pos = (my_pos + offset) % ctx_count
        index = jnp.where(pos < half_count, 2 * pos, 2 * (ctx_count - 1 - pos) + 1)
        start = index * depth + rows_from
        return start // width_feat ^ my_head, start % width_feat // block.shape[0]

    token_pieces = gather_pieces(tokens, "head")
    sum_pieces = gather_pieces(level_sums, "head")
    cw = ccw = value_weight
    steps = [[(place(0, 0, cw), cw)]]
    for step in range(1, half_count):
        cw = lax.ppermute(cw, "ctx", ahead)
        ccw = lax.ppermute(ccw, "ctx", back)
        steps.append([(place(-step, 0, cw), cw), (place(step, 0, ccw), ccw)])
    half = depth // 2
    cw = lax.ppermute(cw[:half], "ctx", ahead)
    ccw = lax.ppermute(ccw[half:], "ctx", back)
    last = [(place(half_count, 0, cw), cw), (place(half_count, half, ccw), ccw)]
    values = states = None

    def more(total, pieces, parts):
        return extend(
            total, pieces, [num for pair, _ in parts for num in pair], [rows for _, rows in parts]
        )

    values = more(None, token_pieces, steps[0] + steps[1])
    for parts in steps[2:]:
        values = more(values, token_pieces, parts)
    states = more(None, sum_pieces, [part for parts in steps[:-1] for part in parts])
    states = more(states, sum_pieces, steps[-1])
    return finish(
        values, states, last, token_pieces, sum_pieces, queries, far, near, head_size, group, 0
    )


def solution(mesh):
    return jax.shard_map(
        body,
        mesh=mesh,
        in_specs=(
            P("ctx", "head"),
            P("ctx", "head"),
            P("ctx", None),
            P("ctx", None),
            P(None, "head", "ctx"),
        ),
        out_specs=P("ctx", "head"),
        check_vma=False,
    )
```

```python
import functools

import jax
import jax.numpy as jnp
from jax import lax
from jax.experimental import pallas as pl
from jax.experimental.pallas import tpu as pltpu
from jax.sharding import PartitionSpec as P

F32 = jnp.float32
BF16 = jnp.bfloat16


def from_partner(block, axis, distance):
    count = lax.axis_size(axis)
    route = []
    for low in range(count):
        high = low | 1 << distance
        if high != low and high < count:
            route += [(low, high), (high, low)]
    return lax.ppermute(block, axis, route)


def gather_pieces(block, axis):
    pieces = [block]
    masks = [0]
    for bit in reversed(range(lax.axis_size(axis).bit_length() - 1)):
        pieces += [from_partner(piece, axis, bit) for piece in pieces]
        masks += [mask | 1 << bit for mask in masks]
    return [piece for _, piece in sorted(zip(masks, pieces), key=lambda pair: pair[0])]


def level_scale(level_num):
    return 1.0 if level_num == 0 else 2.0 ** (-(level_num - 1) / 2.0)


def on_chip(*arrays):
    return [pltpu.with_memory_space_constraint(array, pltpu.VMEM) for array in arrays]


def dot_last(left, right):
    return lax.dot_general(left, right, (((1,), (1,)), ((), ())), preferred_element_type=F32)


def spread_rows(row, count):
    return jnp.broadcast_to(row, (count, row.shape[1]))


def prepare_kernel(q_ref, k_ref, w_ref, *rest):
    near_refs, (score_ref, row_ref) = rest[:-2], rest[-2:]
    length = q_ref.shape[0]
    heads = w_ref.shape[1]
    rows = near_refs[0].shape[2]
    tile = min(128, length)
    sub = 8
    tile_levels = tile.bit_length() - 1
    sub_levels = sub.bit_length() - 1
    score_ref[...] = dot_last(k_ref[...], q_ref[...]).astype(BF16).astype(F32)

    for num in range(length.bit_length()):
        for head in range(heads):
            row_ref[head, num : num + 1, :] = w_ref[num, head : head + 1, :] * level_scale(num)

    def grid_level(shape, shift):
        s_pos = lax.broadcasted_iota(jnp.int32, shape, 0)
        t_pos = jnp.right_shift(lax.broadcasted_iota(jnp.int32, shape, 1), shift)
        if shift == 0:
            t_pos = jnp.bitwise_and(t_pos, sub - 1)
        differ = jnp.bitwise_xor(s_pos, t_pos)
        level = jnp.zeros(shape, jnp.int32)
        for bit in range(tile_levels):
            level = level + (jnp.right_shift(differ, bit) > 0).astype(jnp.int32)
        return jnp.where(s_pos <= t_pos, level, -1)

    fine = grid_level((sub, tile), 0)
    coarse = grid_level((tile // sub, tile), sub_levels)
    near_diag = lax.broadcasted_iota(jnp.int32, (tile, tile), 0) // sub == (
        lax.broadcasted_iota(jnp.int32, (tile, tile), 1) // sub
    )

    def one_head(head, carry):
        for t_tile in range(length // tile):
            t0 = t_tile * tile
            block = t0 // rows
            near_ref = near_refs[block]
            c0 = t0 - block * rows
            weight_rows = [
                row_ref[head, num : num + 1, t0 : t0 + tile]
                for num in range(length.bit_length())
            ]
            for s_tile in range((block + 1) * rows // tile):
                s0 = s_tile * tile
                if s_tile > t_tile:
                    near_ref[head, s0 : s0 + tile, c0 : c0 + tile] = jnp.zeros((tile, tile), BF16)
                    continue
                if s_tile == t_tile:
                    small = jnp.zeros((sub, tile), F32)
                    for num in range(sub_levels + 1):
                        small = jnp.where(fine == num, spread_rows(weight_rows[num], sub), small)
                    big = jnp.zeros((tile // sub, tile), F32)
                    for num in range(sub_levels + 1, tile_levels + 1):
                        big = jnp.where(
                            coarse == num - sub_levels,
                            spread_rows(weight_rows[num], tile // sub),
                            big,
                        )
                    big = jnp.concatenate(
                        [spread_rows(big[row : row + 1], sub) for row in range(tile // sub)], axis=0
                    )
                    weight = jnp.where(near_diag, jnp.concatenate([small] * (tile // sub), 0), big)
                else:
                    num = tile_levels + (s_tile ^ t_tile).bit_length()
                    weight = spread_rows(weight_rows[num], tile)
                score = score_ref[s0 : s0 + tile, t0 : t0 + tile]
                near_ref[head, s0 : s0 + tile, c0 : c0 + tile] = (weight * score).astype(BF16)
        return carry

    lax.fori_loop(0, heads, one_head, 0)


def prepare(queries, key_vectors, level_weight):
    length = queries.shape[0]
    heads = level_weight.shape[1]
    rows = min(256, length)
    return pl.pallas_call(
        prepare_kernel,
        out_shape=[
            pltpu.VMEM((heads, (block + 1) * rows, rows), BF16) for block in range(length // rows)
        ],
        scratch_shapes=[
            pltpu.VMEM((length, length), F32),
            pltpu.VMEM((heads, length.bit_length(), length), F32),
        ],
        compiler_params=pltpu.CompilerParams(vmem_limit_bytes=16 << 20),
        name="prepare",
    )(queries, key_vectors, level_weight)


def choose(where_ref, pieces, depth, chosen_ref, first, count):
    for num in range(count):
        piece = where_ref[2 * (first + num)]
        start = pl.multiple_of(where_ref[2 * (first + num) + 1], 128)
        for index, ref in enumerate(pieces):

            @pl.when(piece == index)
            def _():
                chosen_ref[:, num * depth : (num + 1) * depth] = ref[:, pl.ds(start, depth)]


def extend_kernel(piece_count, count, started, where_ref, *refs):
    pieces = refs[:piece_count]
    blocks = refs[piece_count : piece_count + count]
    out_ref, chosen_ref = refs[-2], refs[-1]
    depth = blocks[0].shape[1]
    choose(where_ref, pieces, depth, chosen_ref, 0, count)
    width = out_ref.shape[0]
    step = min(256, width)
    for c0 in range(0, width, step):
        left = jnp.concatenate([block[c0 : c0 + step, :] for block in blocks], axis=1)
        total = dot_last(left, chosen_ref[...])
        if started:
            total = total + refs[piece_count + count][c0 : c0 + step, :]
        out_ref[c0 : c0 + step, :] = total


def extend(total, pieces, parts):
    where = jnp.stack([num for pair, _ in parts for num in pair])
    blocks = [block for _, block in parts]
    rows = pieces[0].shape[0]
    width, depth = blocks[0].shape
    arrays = on_chip(*pieces, *blocks, *([] if total is None else [total]))
    return pl.pallas_call(
        functools.partial(extend_kernel, len(pieces), len(blocks), total is not None),
        in_specs=[pl.BlockSpec(memory_space=pltpu.SMEM)]
        + [pl.BlockSpec(memory_space=pltpu.VMEM)] * len(arrays),
        out_shape=pltpu.VMEM((width, rows), F32),
        scratch_shapes=[pltpu.VMEM((rows, depth * len(blocks)), BF16)],
        compiler_params=pltpu.CompilerParams(vmem_limit_bytes=12 << 20),
        name="extend",
    )(where, *arrays)


def finish_kernel(piece_count, last_count, near_count, head_size, where_ref, *refs):
    refs = list(refs)
    take = lambda count: [refs.pop(0) for _ in range(count)]
    token_refs, sum_refs = take(piece_count), take(piece_count)
    last_refs = take(last_count)
    value_ref, state_ref, q_ref, w_ref = take(4)
    near_refs = take(near_count)
    out_ref = refs.pop(0)
    length, state_rows = q_ref.shape
    width = value_ref.shape[0]
    near_levels = length.bit_length()
    far_levels = w_ref.shape[0] - near_levels
    rows = length // near_count
    if last_count:
        token_chosen, sum_chosen = refs
        depth = token_chosen.shape[1]
        choose(where_ref, token_refs, depth, token_chosen, 0, 1)
        choose(where_ref, sum_refs, depth, sum_chosen, 0, 1)
    queries = q_ref[...]
    twice = jnp.concatenate([queries, queries], axis=1)
    step = min(256, width)
    unit = (
        lax.broadcasted_iota(jnp.int32, (rows, rows), 0)
        == lax.broadcasted_iota(jnp.int32, (rows, rows), 1)
    ).astype(BF16)
    for c0 in range(0, width, step):
        values, states = value_ref[c0 : c0 + step, :], state_ref[c0 : c0 + step, :]
        if last_count:
            share = width // last_count
            left = last_refs[c0 // share][c0 % share : c0 % share + step, :]
            values = values + dot_last(left, token_chosen[...])
            states = states + dot_last(left, sum_chosen[...])
        values = values.astype(BF16)
        heads = range(c0 // head_size, (c0 + step) // head_size)
        far = None
        for num in range(far_levels):
            state = states[:, num * state_rows : (num + 1) * state_rows]
            high = state.astype(BF16)
            low = (state - high.astype(F32)).astype(BF16)
            reading = dot_last(jnp.concatenate([high, low], axis=1), twice)
            level = near_levels + num
            weight = jnp.concatenate(
                [
                    spread_rows(w_ref[level, head : head + 1, :] * level_scale(level), head_size)
                    for head in heads
                ],
                axis=0,
            )
            far = weight * reading if far is None else far + weight * reading
        for block, near_ref in enumerate(near_refs):
            near = jnp.concatenate(
                [
                    jnp.dot(
                        values[
                            head * head_size - c0 : (head + 1) * head_size - c0,
                            : (block + 1) * rows,
                        ],
                        near_ref[head],
                        preferred_element_type=F32,
                    )
                    for head in heads
                ],
                axis=0,
            )
            total = (near + far[:, block * rows : (block + 1) * rows]).astype(BF16)
            out_ref[block * rows : (block + 1) * rows, c0 : c0 + step] = dot_last(
                unit, total
            ).astype(BF16)


def finish(values, states, where, last, token_pieces, sum_pieces, queries, level_weight, near, head_size):
    width, length = values.shape
    arrays = on_chip(*token_pieces, *sum_pieces, *last, values, states, queries, level_weight, *near)
    scratch = []
    if last:
        depth = last[0].shape[1]
        scratch = [pltpu.VMEM((length, depth), BF16), pltpu.VMEM((states.shape[1], depth), BF16)]
    return pl.pallas_call(
        functools.partial(finish_kernel, len(token_pieces), len(last), len(near), head_size),
        in_specs=[pl.BlockSpec(memory_space=pltpu.SMEM)]
        + [pl.BlockSpec(memory_space=pltpu.VMEM)] * len(arrays),
        out_shape=jax.ShapeDtypeStruct((length, width), BF16),
        scratch_shapes=scratch,
        compiler_params=pltpu.CompilerParams(vmem_limit_bytes=24 << 20),
        name="finish",
    )(where, *arrays)


def body(tokens, value_weight, queries, key_vectors, level_weight):
    length, width_feat = tokens.shape
    depth, width_local = value_weight.shape
    head_local = level_weight.shape[1]
    head_size = width_local // head_local
    ctx_count = lax.axis_size("ctx")
    dev_bits = ctx_count.bit_length() - 1
    my_index = lax.axis_index("ctx")
    my_head = lax.axis_index("head")
    near = prepare(queries, key_vectors, level_weight)

    running = jnp.einsum("tn,tf->nf", key_vectors, tokens, preferred_element_type=F32)
    level_sums = []
    for section_bit in range(dev_bits):
        partner = from_partner(running.astype(BF16), "ctx", section_bit)
        is_right = my_index // 2**section_bit % 2 == 1
        level_sums.append(jnp.where(is_right, partner, jnp.zeros_like(partner)))
        running = running + partner.astype(F32)
    level_sums = jnp.concatenate(level_sums, axis=0)

    if depth % 256 or width_feat % depth:
        features = lax.all_gather(tokens, "head", axis=1, tiled=True)
        sums = lax.all_gather(level_sums, "head", axis=1, tiled=True)
        weight = lax.all_gather(value_weight, "ctx", axis=0, tiled=True)
        values = jnp.einsum("fc,tf->ct", weight, features, preferred_element_type=F32)
        states = jnp.einsum("fc,nf->cn", weight, sums, preferred_element_type=F32)
        where = jnp.zeros((2,), jnp.int32)
        return finish(values, states, where, [], [], [], queries, level_weight, near, head_size)

    order = list(range(0, ctx_count, 2)) + list(range(1, ctx_count, 2))[::-1]
    ahead = [(order[i], order[(i + 1) % ctx_count]) for i in range(ctx_count)]
    back = [(b, a) for a, b in ahead]
    half_count = ctx_count // 2
    my_pos = jnp.where(my_index % 2 == 0, my_index // 2, ctx_count - 1 - my_index // 2)

    def place(offset):
        pos = (my_pos + offset) % ctx_count
        index = jnp.where(pos < half_count, 2 * pos, 2 * (ctx_count - 1 - pos) + 1)
        start = index * depth
        return start // width_feat ^ my_head, start % width_feat

    token_pieces = gather_pieces(tokens, "head")
    sum_pieces = gather_pieces(level_sums, "head")
    cw = ccw = value_weight.T
    steps = [[(place(0), cw)]]
    for step in range(1, half_count):
        cw = lax.ppermute(cw, "ctx", ahead)
        ccw = lax.ppermute(ccw, "ctx", back)
        steps.append([(place(-step), cw), (place(step), ccw)])
    half = width_local // 2
    last = [
        lax.ppermute(cw[:half], "ctx", ahead),
        lax.ppermute(ccw[half:], "ctx", back),
    ]
    values = extend(None, token_pieces, steps[0] + steps[1])
    for parts in steps[2:]:
        values = extend(values, token_pieces, parts)
    states = extend(None, sum_pieces, [part for parts in steps for part in parts])
    return finish(
        values,
        states,
        jnp.stack(place(half_count)),
        last,
        token_pieces,
        sum_pieces,
        queries,
        level_weight,
        near,
        head_size,
    )


def solution(mesh):
    return jax.shard_map(
        body,
        mesh=mesh,
        in_specs=(
            P("ctx", "head"),
            P("ctx", "head"),
            P("ctx", None),
            P("ctx", None),
            P(None, "head", "ctx"),
        ),
        out_specs=P("ctx", "head"),
        check_vma=False,
    )
```

```python
import functools

import jax
import jax.numpy as jnp
from jax import lax
from jax.experimental import pallas as pl
from jax.experimental.pallas import tpu as pltpu
from jax.sharding import PartitionSpec as P


F32 = jnp.float32
BF16 = jnp.bfloat16


def from_partner(block, axis, distance):
    count = lax.axis_size(axis)
    route = []
    for low in range(count):
        high = low | 1 << distance
        if high != low and high < count:
            route += [(low, high), (high, low)]
    return lax.ppermute(block, axis, route)


def gather_pieces(block, axis):
    pieces = [block]
    masks = [0]
    for bit in reversed(range(lax.axis_size(axis).bit_length() - 1)):
        for mask, piece in zip(list(masks), list(pieces)):
            pieces.append(from_partner(piece, axis, bit))
            masks.append(mask | 1 << bit)
    return [piece for _, piece in sorted(zip(masks, pieces), key=lambda pair: pair[0])]


def level_scale(level_num):
    return 1.0 if level_num == 0 else 2.0 ** (-(level_num - 1) / 2.0)


def on_chip(*arrays):
    return [pltpu.with_memory_space_constraint(array, pltpu.VMEM) for array in arrays]


def dot_last(left, right):
    return lax.dot_general(left, right, (((1,), (1,)), ((), ())), preferred_element_type=F32)


def spread_rows(row, count):
    return jnp.broadcast_to(row, (count, row.shape[1]))


def prepare_kernel(q_ref, k_ref, w_ref, *rest):
    near_refs, (score_ref, row_ref) = rest[:-2], rest[-2:]
    length = q_ref.shape[0]
    heads = w_ref.shape[1]
    rows = near_refs[0].shape[2]
    tile = min(128, length)
    sub = 8
    tile_levels = tile.bit_length() - 1
    sub_levels = sub.bit_length() - 1
    score_ref[...] = dot_last(k_ref[...], q_ref[...]).astype(BF16).astype(F32)

    for num in range(length.bit_length()):
        for head in range(heads):
            row_ref[head, num : num + 1, :] = w_ref[num, head : head + 1, :] * level_scale(num)

    def grid_level(shape, shift):
        s_pos = lax.broadcasted_iota(jnp.int32, shape, 0)
        t_pos = jnp.right_shift(lax.broadcasted_iota(jnp.int32, shape, 1), shift)
        if shift == 0:
            t_pos = jnp.bitwise_and(t_pos, sub - 1)
        differ = jnp.bitwise_xor(s_pos, t_pos)
        level = jnp.zeros(shape, jnp.int32)
        for bit in range(tile_levels):
            level = level + (jnp.right_shift(differ, bit) > 0).astype(jnp.int32)
        return jnp.where(s_pos <= t_pos, level, -1)

    fine = grid_level((sub, tile), 0)
    coarse = grid_level((tile // sub, tile), sub_levels)
    near_diag = lax.broadcasted_iota(jnp.int32, (tile, tile), 0) // sub == (
        lax.broadcasted_iota(jnp.int32, (tile, tile), 1) // sub
    )

    def one_head(head, carry):
        for t_tile in range(length // tile):
            t0 = t_tile * tile
            block = t0 // rows
            near_ref = near_refs[block]
            c0 = t0 - block * rows
            weight_rows = [
                row_ref[head, num : num + 1, t0 : t0 + tile]
                for num in range(length.bit_length())
            ]
            for s_tile in range((block + 1) * rows // tile):
                s0 = s_tile * tile
                if s_tile > t_tile:
                    near_ref[head, s0 : s0 + tile, c0 : c0 + tile] = jnp.zeros((tile, tile), BF16)
                    continue
                if s_tile == t_tile:
                    small = jnp.zeros((sub, tile), F32)
                    for num in range(sub_levels + 1):
                        small = jnp.where(fine == num, spread_rows(weight_rows[num], sub), small)
                    big = jnp.zeros((tile // sub, tile), F32)
                    for num in range(sub_levels + 1, tile_levels + 1):
                        big = jnp.where(
                            coarse == num - sub_levels,
                            spread_rows(weight_rows[num], tile // sub),
                            big,
                        )
                    big = jnp.concatenate(
                        [spread_rows(big[row : row + 1], sub) for row in range(tile // sub)], axis=0
                    )
                    weight = jnp.where(near_diag, jnp.concatenate([small] * (tile // sub), 0), big)
                else:
                    num = tile_levels + (s_tile ^ t_tile).bit_length()
                    weight = spread_rows(weight_rows[num], tile)
                score = score_ref[s0 : s0 + tile, t0 : t0 + tile]
                near_ref[head, s0 : s0 + tile, c0 : c0 + tile] = (weight * score).astype(BF16)
        return carry

    lax.fori_loop(0, heads, one_head, 0)


def prepare(queries, key_vectors, level_weight):
    length = queries.shape[0]
    heads = level_weight.shape[1]
    rows = min(256, length)
    return pl.pallas_call(
        prepare_kernel,
        out_shape=[
            pltpu.VMEM((heads, (block + 1) * rows, rows), BF16) for block in range(length // rows)
        ],
        scratch_shapes=[
            pltpu.VMEM((length, length), F32),
            pltpu.VMEM((heads, length.bit_length(), length), F32),
        ],
        compiler_params=pltpu.CompilerParams(vmem_limit_bytes=16 << 20),
        name="prepare",
    )(queries, key_vectors, level_weight)


def choose(where_ref, pieces, depth, chosen_ref, first, count):
    for num in range(count):
        piece = where_ref[2 * (first + num)]
        start = pl.multiple_of(where_ref[2 * (first + num) + 1], 128)
        for index, ref in enumerate(pieces):

            @pl.when(piece == index)
            def _():
                chosen_ref[:, num * depth : (num + 1) * depth] = ref[:, pl.ds(start, depth)]


def extend_kernel(piece_count, count, started, where_ref, *refs):
    pieces = refs[:piece_count]
    blocks = refs[piece_count : piece_count + count]
    out_ref, chosen_ref = refs[-2], refs[-1]
    depth = blocks[0].shape[1]
    choose(where_ref, pieces, depth, chosen_ref, 0, count)
    width = out_ref.shape[0]
    step = min(256, width)
    for c0 in range(0, width, step):
        left = jnp.concatenate([block[c0 : c0 + step, :] for block in blocks], axis=1)
        total = dot_last(left, chosen_ref[...])
        if started:
            total = total + refs[piece_count + count][c0 : c0 + step, :]
        out_ref[c0 : c0 + step, :] = total


def extend(total, pieces, parts):
    where = jnp.stack([num for pair, _ in parts for num in pair])
    blocks = [block for _, block in parts]
    rows = pieces[0].shape[0]
    width, depth = blocks[0].shape
    arrays = on_chip(*pieces, *blocks, *([] if total is None else [total]))
    return pl.pallas_call(
        functools.partial(extend_kernel, len(pieces), len(blocks), total is not None),
        in_specs=[pl.BlockSpec(memory_space=pltpu.SMEM)]
        + [pl.BlockSpec(memory_space=pltpu.VMEM)] * len(arrays),
        out_shape=pltpu.VMEM((width, rows), F32),
        scratch_shapes=[pltpu.VMEM((rows, depth * len(blocks)), BF16)],
        compiler_params=pltpu.CompilerParams(vmem_limit_bytes=12 << 20),
    )(where, *arrays)


def finish_kernel(piece_count, last_count, near_count, head_size, where_ref, *refs):
    refs = list(refs)
    take = lambda count: [refs.pop(0) for _ in range(count)]
    token_refs, sum_refs = take(piece_count), take(piece_count)
    last_refs = take(last_count)
    value_ref, state_ref, q_ref, w_ref = take(4)
    near_refs = take(near_count)
    out_ref = refs.pop(0)
    length, state_rows = q_ref.shape
    width = value_ref.shape[0]
    near_levels = length.bit_length()
    far_levels = w_ref.shape[0] - near_levels
    rows = length // near_count
    if last_count:
        token_chosen, sum_chosen = refs
        depth = token_chosen.shape[1]
        choose(where_ref, token_refs, depth, token_chosen, 0, 1)
        choose(where_ref, sum_refs, depth, sum_chosen, 0, 1)
    queries = q_ref[...]
    twice = jnp.concatenate([queries, queries], axis=1)
    step = min(256, width)
    unit = (
        lax.broadcasted_iota(jnp.int32, (rows, rows), 0)
        == lax.broadcasted_iota(jnp.int32, (rows, rows), 1)
    ).astype(BF16)
    for c0 in range(0, width, step):
        values, states = value_ref[c0 : c0 + step, :], state_ref[c0 : c0 + step, :]
        if last_count:
            share = width // last_count
            left = last_refs[c0 // share][c0 % share : c0 % share + step, :]
            values = values + dot_last(left, token_chosen[...])
            states = states + dot_last(left, sum_chosen[...])
        values = values.astype(BF16)
        heads = range(c0 // head_size, (c0 + step) // head_size)
        far = None
        for num in range(far_levels):
            state = states[:, num * state_rows : (num + 1) * state_rows]
            high = state.astype(BF16)
            low = (state - high.astype(F32)).astype(BF16)
            reading = dot_last(jnp.concatenate([high, low], axis=1), twice)
            level = near_levels + num
            weight = jnp.concatenate(
                [
                    spread_rows(w_ref[level, head : head + 1, :] * level_scale(level), head_size)
                    for head in heads
                ],
                axis=0,
            )
            far = weight * reading if far is None else far + weight * reading
        for block, near_ref in enumerate(near_refs):
            near = jnp.concatenate(
                [
                    jnp.dot(
                        values[
                            head * head_size - c0 : (head + 1) * head_size - c0,
                            : (block + 1) * rows,
                        ],
                        near_ref[head],
                        preferred_element_type=F32,
                    )
                    for head in heads
                ],
                axis=0,
            )
            total = (near + far[:, block * rows : (block + 1) * rows]).astype(BF16)
            out_ref[block * rows : (block + 1) * rows, c0 : c0 + step] = dot_last(
                unit, total
            ).astype(BF16)


def finish(values, states, where, last, token_pieces, sum_pieces, queries, level_weight, near, head_size):
    width, length = values.shape
    arrays = on_chip(*token_pieces, *sum_pieces, *last, values, states, queries, level_weight, *near)
    scratch = []
    if last:
        depth = last[0].shape[1]
        scratch = [pltpu.VMEM((length, depth), BF16), pltpu.VMEM((states.shape[1], depth), BF16)]
    return pl.pallas_call(
        functools.partial(finish_kernel, len(token_pieces), len(last), len(near), head_size),
        in_specs=[pl.BlockSpec(memory_space=pltpu.SMEM)]
        + [pl.BlockSpec(memory_space=pltpu.VMEM)] * len(arrays),
        out_shape=jax.ShapeDtypeStruct((length, width), BF16),
        scratch_shapes=scratch,
        compiler_params=pltpu.CompilerParams(vmem_limit_bytes=24 << 20),
        name="finish",
    )(where, *arrays)


def body(tokens, value_weight, queries, key_vectors, level_weight):
    _, width_feat = tokens.shape
    depth, width_local = value_weight.shape
    head_local = level_weight.shape[1]
    head_size = width_local // head_local
    ctx_count = lax.axis_size("ctx")
    dev_bits = ctx_count.bit_length() - 1
    my_index = lax.axis_index("ctx")
    my_head = lax.axis_index("head")
    near = prepare(queries, key_vectors, level_weight)

    running = jnp.einsum("tn,tf->nf", key_vectors, tokens, preferred_element_type=F32)
    level_sums = []
    for section_bit in range(dev_bits):
        partner = from_partner(running.astype(BF16), "ctx", section_bit)
        is_right = my_index // 2**section_bit % 2 == 1
        level_sums.append(jnp.where(is_right, partner, jnp.zeros_like(partner)))
        running = running + partner.astype(F32)
    level_sums = jnp.concatenate(level_sums, axis=0)

    if depth % 256 or width_feat % depth:
        features = lax.all_gather(tokens, "head", axis=1, tiled=True)
        sums = lax.all_gather(level_sums, "head", axis=1, tiled=True)
        weight = lax.all_gather(value_weight, "ctx", axis=0, tiled=True)
        values = jnp.einsum("fc,tf->ct", weight, features, preferred_element_type=F32)
        states = jnp.einsum("fc,nf->cn", weight, sums, preferred_element_type=F32)
        where = jnp.zeros((2,), jnp.int32)
        return finish(values, states, where, [], [], [], queries, level_weight, near, head_size)

    order = list(range(0, ctx_count, 2)) + list(range(1, ctx_count, 2))[::-1]
    ahead = [(order[i], order[(i + 1) % ctx_count]) for i in range(ctx_count)]
    back = [(b, a) for a, b in ahead]
    half_count = ctx_count // 2
    my_pos = jnp.where(my_index % 2 == 0, my_index // 2, ctx_count - 1 - my_index // 2)

    def place(offset):
        pos = (my_pos + offset) % ctx_count
        index = jnp.where(pos < half_count, 2 * pos, 2 * (ctx_count - 1 - pos) + 1)
        start = index * depth
        return start // width_feat ^ my_head, start % width_feat

    token_pieces = gather_pieces(tokens, "head")
    sum_pieces = gather_pieces(level_sums, "head")
    cw = ccw = value_weight.T
    steps = [[(place(0), cw)]]
    for step in range(1, half_count):
        cw = lax.ppermute(cw, "ctx", ahead)
        ccw = lax.ppermute(ccw, "ctx", back)
        steps.append([(place(-step), cw), (place(step), ccw)])
    half = width_local // 2
    cw = lax.ppermute(cw[:half], "ctx", ahead)
    ccw = lax.ppermute(ccw[half:], "ctx", back)
    last = [cw, ccw]
    values = extend(None, token_pieces, steps[0] + steps[1])
    for step in range(2, half_count):
        values = extend(values, token_pieces, steps[step])
    states = extend(None, sum_pieces, [part for parts in steps for part in parts])
    return finish(
        values,
        states,
        jnp.stack(place(half_count)),
        last,
        token_pieces,
        sum_pieces,
        queries,
        level_weight,
        near,
        head_size,
    )


def solution(mesh):
    return jax.shard_map(
        body,
        mesh=mesh,
        in_specs=(
            P("ctx", "head"),
            P("ctx", "head"),
            P("ctx", None),
            P("ctx", None),
            P(None, "head", "ctx"),
        ),
        out_specs=P("ctx", "head"),
        check_vma=False,
    )
```

```python
import functools

import jax
import jax.numpy as jnp
from jax import lax
from jax.experimental import pallas as pl
from jax.experimental.pallas import tpu as pltpu
from jax.sharding import PartitionSpec as P


F32 = jnp.float32
BF16 = jnp.bfloat16


def from_partner(block, axis, distance):
    count = lax.axis_size(axis)
    route = []
    for low in range(count):
        high = low | 1 << distance
        if high != low and high < count:
            route += [(low, high), (high, low)]
    return lax.ppermute(block, axis, route)


def gather_pieces(block, axis):
    pieces = [block]
    masks = [0]
    for bit in reversed(range(lax.axis_size(axis).bit_length() - 1)):
        for mask, piece in zip(list(masks), list(pieces)):
            pieces.append(from_partner(piece, axis, bit))
            masks.append(mask | 1 << bit)
    return [piece for _, piece in sorted(zip(masks, pieces), key=lambda pair: pair[0])]


def level_scale(level_num):
    return 1.0 if level_num == 0 else 2.0 ** (-(level_num - 1) / 2.0)


def on_chip(*arrays):
    return [pltpu.with_memory_space_constraint(array, pltpu.VMEM) for array in arrays]


def dot_last(left, right):
    return lax.dot_general(left, right, (((1,), (1,)), ((), ())), preferred_element_type=F32)


def spread_rows(row, count):
    return jnp.broadcast_to(row, (count, row.shape[1]))


def prepare_kernel(q_ref, k_ref, w_ref, *rest):
    near_refs, (score_ref, row_ref) = rest[:-2], rest[-2:]
    length = q_ref.shape[0]
    heads = w_ref.shape[1]
    rows = near_refs[0].shape[2]
    tile = min(128, length)
    sub = 8
    tile_levels = tile.bit_length() - 1
    sub_levels = sub.bit_length() - 1
    score_ref[...] = dot_last(k_ref[...], q_ref[...]).astype(BF16).astype(F32)

    for num in range(length.bit_length()):
        for head in range(heads):
            row_ref[head, num : num + 1, :] = w_ref[num, head : head + 1, :] * level_scale(num)

    def grid_level(shape, shift):
        s_pos = lax.broadcasted_iota(jnp.int32, shape, 0)
        t_pos = jnp.right_shift(lax.broadcasted_iota(jnp.int32, shape, 1), shift)
        if shift == 0:
            t_pos = jnp.bitwise_and(t_pos, sub - 1)
        differ = jnp.bitwise_xor(s_pos, t_pos)
        level = jnp.zeros(shape, jnp.int32)
        for bit in range(tile_levels):
            level = level + (jnp.right_shift(differ, bit) > 0).astype(jnp.int32)
        return jnp.where(s_pos <= t_pos, level, -1)

    fine = grid_level((sub, tile), 0)
    coarse = grid_level((tile // sub, tile), sub_levels)
    near_diag = lax.broadcasted_iota(jnp.int32, (tile, tile), 0) // sub == (
        lax.broadcasted_iota(jnp.int32, (tile, tile), 1) // sub
    )

    def one_head(head, carry):
        for t_tile in range(length // tile):
            t0 = t_tile * tile
            block = t0 // rows
            near_ref = near_refs[block]
            c0 = t0 - block * rows
            weight_rows = [
                row_ref[head, num : num + 1, t0 : t0 + tile]
                for num in range(length.bit_length())
            ]
            for s_tile in range((block + 1) * rows // tile):
                s0 = s_tile * tile
                if s_tile > t_tile:
                    near_ref[head, s0 : s0 + tile, c0 : c0 + tile] = jnp.zeros((tile, tile), BF16)
                    continue
                if s_tile == t_tile:
                    small = jnp.zeros((sub, tile), F32)
                    for num in range(sub_levels + 1):
                        small = jnp.where(fine == num, spread_rows(weight_rows[num], sub), small)
                    big = jnp.zeros((tile // sub, tile), F32)
                    for num in range(sub_levels + 1, tile_levels + 1):
                        big = jnp.where(
                            coarse == num - sub_levels,
                            spread_rows(weight_rows[num], tile // sub),
                            big,
                        )
                    big = jnp.concatenate(
                        [spread_rows(big[row : row + 1], sub) for row in range(tile // sub)], axis=0
                    )
                    weight = jnp.where(near_diag, jnp.concatenate([small] * (tile // sub), 0), big)
                else:
                    num = tile_levels + (s_tile ^ t_tile).bit_length()
                    weight = spread_rows(weight_rows[num], tile)
                score = score_ref[s0 : s0 + tile, t0 : t0 + tile]
                near_ref[head, s0 : s0 + tile, c0 : c0 + tile] = (weight * score).astype(BF16)
        return carry

    lax.fori_loop(0, heads, one_head, 0)


def prepare(queries, key_vectors, level_weight):
    length = queries.shape[0]
    heads = level_weight.shape[1]
    rows = min(256, length)
    return pl.pallas_call(
        prepare_kernel,
        out_shape=[
            pltpu.VMEM((heads, (block + 1) * rows, rows), BF16) for block in range(length // rows)
        ],
        scratch_shapes=[
            pltpu.VMEM((length, length), F32),
            pltpu.VMEM((heads, length.bit_length(), length), F32),
        ],
        compiler_params=pltpu.CompilerParams(vmem_limit_bytes=16 << 20),
        name="prepare",
    )(queries, key_vectors, level_weight)


def choose(where_ref, pieces, depth, chosen_ref, first, count):
    for num in range(count):
        piece = where_ref[2 * (first + num)]
        start = pl.multiple_of(where_ref[2 * (first + num) + 1], 128)
        for index, ref in enumerate(pieces):

            @pl.when(piece == index)
            def _():
                chosen_ref[:, num * depth : (num + 1) * depth] = ref[:, pl.ds(start, depth)]


def extend_kernel(piece_count, count, split, started, where_ref, *refs):
    pieces = refs[:piece_count]
    blocks = [refs[piece_count + num * split :][:split] for num in range(count)]
    out_ref, chosen_ref = refs[-2], refs[-1]
    share, depth = blocks[0][0].shape
    choose(where_ref, pieces, depth, chosen_ref, 0, count)
    width = out_ref.shape[0]
    step = min(256, share)
    for c0 in range(0, width, step):
        at = c0 % share
        left = jnp.concatenate(
            [block[c0 // share][at : at + step, :] for block in blocks], axis=1
        )
        total = dot_last(left, chosen_ref[...])
        if started:
            total = total + refs[piece_count + count * split][c0 : c0 + step, :]
        out_ref[c0 : c0 + step, :] = total


def extend(total, pieces, parts):
    where = jnp.stack([num for pair, _ in parts for num in pair])
    blocks = [half for _, block in parts for half in block]
    split = len(parts[0][1])
    rows = pieces[0].shape[0]
    share, depth = blocks[0].shape
    arrays = [*pieces, *blocks, *([] if total is None else [total])]
    return pl.pallas_call(
        functools.partial(extend_kernel, len(pieces), len(parts), split, total is not None),
        in_specs=[pl.BlockSpec(memory_space=pltpu.SMEM)]
        + [pl.BlockSpec(memory_space=pltpu.VMEM)] * len(arrays),
        out_shape=pltpu.VMEM((share * split, rows), F32),
        scratch_shapes=[pltpu.VMEM((rows, depth * len(parts)), BF16)],
        compiler_params=pltpu.CompilerParams(vmem_limit_bytes=12 << 20),
    )(where, *arrays)


def finish_kernel(piece_count, last_count, near_count, head_size, where_ref, *refs):
    refs = list(refs)
    take = lambda count: [refs.pop(0) for _ in range(count)]
    token_refs, sum_refs = take(piece_count), take(piece_count)
    last_refs = take(last_count)
    value_ref, state_ref, q_ref, w_ref = take(4)
    near_refs = take(near_count)
    out_ref = refs.pop(0)
    length, state_rows = q_ref.shape
    width = value_ref.shape[0]
    near_levels = length.bit_length()
    far_levels = w_ref.shape[0] - near_levels
    rows = length // near_count
    if last_count:
        token_chosen, sum_chosen = refs
        depth = token_chosen.shape[1]
        choose(where_ref, token_refs, depth, token_chosen, 0, 1)
        choose(where_ref, sum_refs, depth, sum_chosen, 0, 1)
    queries = q_ref[...]
    twice = jnp.concatenate([queries, queries], axis=1)
    step = min(256, width)
    unit = (
        lax.broadcasted_iota(jnp.int32, (rows, rows), 0)
        == lax.broadcasted_iota(jnp.int32, (rows, rows), 1)
    ).astype(BF16)
    for c0 in range(0, width, step):
        values, states = value_ref[c0 : c0 + step, :], state_ref[c0 : c0 + step, :]
        if last_count:
            share = width // last_count
            left = last_refs[c0 // share][c0 % share : c0 % share + step, :]
            values = values + dot_last(left, token_chosen[...])
            states = states + dot_last(left, sum_chosen[...])
        values = values.astype(BF16)
        heads = range(c0 // head_size, (c0 + step) // head_size)
        far = None
        for num in range(far_levels):
            state = states[:, num * state_rows : (num + 1) * state_rows]
            high = state.astype(BF16)
            low = (state - high.astype(F32)).astype(BF16)
            reading = dot_last(jnp.concatenate([high, low], axis=1), twice)
            level = near_levels + num
            weight = jnp.concatenate(
                [
                    spread_rows(w_ref[level, head : head + 1, :] * level_scale(level), head_size)
                    for head in heads
                ],
                axis=0,
            )
            far = weight * reading if far is None else far + weight * reading
        for block, near_ref in enumerate(near_refs):
            near = jnp.concatenate(
                [
                    jnp.dot(
                        values[
                            head * head_size - c0 : (head + 1) * head_size - c0,
                            : (block + 1) * rows,
                        ],
                        near_ref[head],
                        preferred_element_type=F32,
                    )
                    for head in heads
                ],
                axis=0,
            )
            total = (near + far[:, block * rows : (block + 1) * rows]).astype(BF16)
            out_ref[block * rows : (block + 1) * rows, c0 : c0 + step] = dot_last(
                unit, total
            ).astype(BF16)


def finish(values, states, where, last, token_pieces, sum_pieces, queries, level_weight, near, head_size):
    width, length = values.shape
    arrays = [*token_pieces, *sum_pieces, *last, values, states, queries, level_weight, *near]
    scratch = []
    if last:
        depth = last[0].shape[1]
        scratch = [pltpu.VMEM((length, depth), BF16), pltpu.VMEM((states.shape[1], depth), BF16)]
    return pl.pallas_call(
        functools.partial(finish_kernel, len(token_pieces), len(last), len(near), head_size),
        in_specs=[pl.BlockSpec(memory_space=pltpu.SMEM)]
        + [pl.BlockSpec(memory_space=pltpu.VMEM)] * len(arrays),
        out_shape=jax.ShapeDtypeStruct((length, width), BF16),
        scratch_shapes=scratch,
        compiler_params=pltpu.CompilerParams(vmem_limit_bytes=24 << 20),
        name="finish",
    )(where, *arrays)


def body(tokens, value_weight, queries, key_vectors, level_weight):
    _, width_feat = tokens.shape
    depth, width_local = value_weight.shape
    head_local = level_weight.shape[1]
    head_size = width_local // head_local
    ctx_count = lax.axis_size("ctx")
    dev_bits = ctx_count.bit_length() - 1
    my_index = lax.axis_index("ctx")
    my_head = lax.axis_index("head")
    near = prepare(queries, key_vectors, level_weight)

    running = jnp.einsum("tn,tf->nf", key_vectors, tokens, preferred_element_type=F32)
    level_sums = []
    for section_bit in range(dev_bits):
        partner = from_partner(running.astype(BF16), "ctx", section_bit)
        is_right = my_index // 2**section_bit % 2 == 1
        level_sums.append(jnp.where(is_right, partner, jnp.zeros_like(partner)))
        running = running + partner.astype(F32)
    level_sums = jnp.concatenate(level_sums, axis=0)

    if depth % 256 or width_feat % depth:
        features = lax.all_gather(tokens, "head", axis=1, tiled=True)
        sums = lax.all_gather(level_sums, "head", axis=1, tiled=True)
        weight = lax.all_gather(value_weight, "ctx", axis=0, tiled=True)
        values = jnp.einsum("fc,tf->ct", weight, features, preferred_element_type=F32)
        states = jnp.einsum("fc,nf->cn", weight, sums, preferred_element_type=F32)
        where = jnp.zeros((2,), jnp.int32)
        return finish(values, states, where, [], [], [], queries, level_weight, near, head_size)

    order = list(range(0, ctx_count, 2)) + list(range(1, ctx_count, 2))[::-1]
    ahead = [(order[i], order[(i + 1) % ctx_count]) for i in range(ctx_count)]
    back = [(b, a) for a, b in ahead]
    half_count = ctx_count // 2
    my_pos = jnp.where(my_index % 2 == 0, my_index // 2, ctx_count - 1 - my_index // 2)

    def place(offset):
        pos = (my_pos + offset) % ctx_count
        index = jnp.where(pos < half_count, 2 * pos, 2 * (ctx_count - 1 - pos) + 1)
        start = index * depth
        return start // width_feat ^ my_head, start % width_feat

    token_pieces = on_chip(*gather_pieces(tokens, "head"))
    sum_pieces = on_chip(*gather_pieces(level_sums, "head"))
    half = width_local // 2
    first = value_weight.T
    cw = ccw = (first[:half], first[half:])
    steps = [[(place(0), on_chip(*cw))]]

    def move(part, route):
        return lax.ppermute(part, "ctx", route)

    for step in range(1, half_count):
        cw = tuple(move(part, ahead) for part in cw)
        ccw = tuple(move(part, back) for part in ccw)
        steps.append([(place(-step), on_chip(*cw)), (place(step), on_chip(*ccw))])
    last = on_chip(move(cw[0], ahead), move(ccw[1], back))
    values = extend(None, token_pieces, steps[0] + steps[1])
    for step in range(2, half_count):
        values = extend(values, token_pieces, steps[step])
    states = extend(None, sum_pieces, [part for parts in steps for part in parts])
    return finish(
        values,
        states,
        jnp.stack(place(half_count)),
        last,
        token_pieces,
        sum_pieces,
        queries,
        level_weight,
        near,
        head_size,
    )


def solution(mesh):
    return jax.shard_map(
        body,
        mesh=mesh,
        in_specs=(
            P("ctx", "head"),
            P("ctx", "head"),
            P("ctx", None),
            P("ctx", None),
            P(None, "head", "ctx"),
        ),
        out_specs=P("ctx", "head"),
        check_vma=False,
    )
```

```python
import functools

import jax
import jax.numpy as jnp
from jax import lax
from jax.experimental import pallas as pl
from jax.experimental.pallas import tpu as pltpu
from jax.sharding import PartitionSpec as P


F32 = jnp.float32
BF16 = jnp.bfloat16


def from_partner(block, axis, distance):
    count = lax.axis_size(axis)
    route = []
    for low in range(count):
        high = low | 1 << distance
        if high != low and high < count:
            route += [(low, high), (high, low)]
    return lax.ppermute(block, axis, route)


def gather_pieces(block, axis):
    pieces = [block]
    masks = [0]
    for bit in reversed(range(lax.axis_size(axis).bit_length() - 1)):
        for mask, piece in zip(list(masks), list(pieces)):
            pieces.append(from_partner(piece, axis, bit))
            masks.append(mask | 1 << bit)
    return [piece for _, piece in sorted(zip(masks, pieces), key=lambda pair: pair[0])]


def level_scale(level_num):
    return 1.0 if level_num == 0 else 2.0 ** (-(level_num - 1) / 2.0)


def on_chip(*arrays):
    return [pltpu.with_memory_space_constraint(array, pltpu.VMEM) for array in arrays]


def dot_last(left, right):
    return lax.dot_general(left, right, (((1,), (1,)), ((), ())), preferred_element_type=F32)


def spread_rows(row, count):
    return jnp.broadcast_to(row, (count, row.shape[1]))


def prepare_kernel(q_ref, k_ref, w_ref, *rest):
    near_refs, (score_ref, row_ref) = rest[:-2], rest[-2:]
    length = q_ref.shape[0]
    heads = w_ref.shape[1]
    rows = near_refs[0].shape[2]
    tile = min(128, length)
    sub = 8
    tile_levels = tile.bit_length() - 1
    sub_levels = sub.bit_length() - 1
    score_ref[...] = dot_last(k_ref[...], q_ref[...]).astype(BF16).astype(F32)

    for num in range(length.bit_length()):
        for head in range(heads):
            row_ref[head, num : num + 1, :] = w_ref[num, head : head + 1, :] * level_scale(num)

    def grid_level(shape, shift):
        s_pos = lax.broadcasted_iota(jnp.int32, shape, 0)
        t_pos = jnp.right_shift(lax.broadcasted_iota(jnp.int32, shape, 1), shift)
        if shift == 0:
            t_pos = jnp.bitwise_and(t_pos, sub - 1)
        differ = jnp.bitwise_xor(s_pos, t_pos)
        level = jnp.zeros(shape, jnp.int32)
        for bit in range(tile_levels):
            level = level + (jnp.right_shift(differ, bit) > 0).astype(jnp.int32)
        return jnp.where(s_pos <= t_pos, level, -1)

    fine = grid_level((sub, tile), 0)
    coarse = grid_level((tile // sub, tile), sub_levels)
    near_diag = lax.broadcasted_iota(jnp.int32, (tile, tile), 0) // sub == (
        lax.broadcasted_iota(jnp.int32, (tile, tile), 1) // sub
    )

    def one_head(head, carry):
        for t_tile in range(length // tile):
            t0 = t_tile * tile
            block = t0 // rows
            near_ref = near_refs[block]
            c0 = t0 - block * rows
            weight_rows = [
                row_ref[head, num : num + 1, t0 : t0 + tile]
                for num in range(length.bit_length())
            ]
            for s_tile in range((block + 1) * rows // tile):
                s0 = s_tile * tile
                if s_tile > t_tile:
                    near_ref[head, s0 : s0 + tile, c0 : c0 + tile] = jnp.zeros((tile, tile), BF16)
                    continue
                if s_tile == t_tile:
                    small = jnp.zeros((sub, tile), F32)
                    for num in range(sub_levels + 1):
                        small = jnp.where(fine == num, spread_rows(weight_rows[num], sub), small)
                    big = jnp.zeros((tile // sub, tile), F32)
                    for num in range(sub_levels + 1, tile_levels + 1):
                        big = jnp.where(
                            coarse == num - sub_levels,
                            spread_rows(weight_rows[num], tile // sub),
                            big,
                        )
                    big = jnp.concatenate(
                        [spread_rows(big[row : row + 1], sub) for row in range(tile // sub)], axis=0
                    )
                    weight = jnp.where(near_diag, jnp.concatenate([small] * (tile // sub), 0), big)
                else:
                    num = tile_levels + (s_tile ^ t_tile).bit_length()
                    weight = spread_rows(weight_rows[num], tile)
                score = score_ref[s0 : s0 + tile, t0 : t0 + tile]
                near_ref[head, s0 : s0 + tile, c0 : c0 + tile] = (weight * score).astype(BF16)
        return carry

    lax.fori_loop(0, heads, one_head, 0)


def prepare(queries, key_vectors, level_weight):
    length = queries.shape[0]
    heads = level_weight.shape[1]
    rows = min(256, length)
    return pl.pallas_call(
        prepare_kernel,
        out_shape=[
            pltpu.VMEM((heads, (block + 1) * rows, rows), BF16) for block in range(length // rows)
        ],
        scratch_shapes=[
            pltpu.VMEM((length, length), F32),
            pltpu.VMEM((heads, length.bit_length(), length), F32),
        ],
        compiler_params=pltpu.CompilerParams(vmem_limit_bytes=16 << 20),
        name="prepare",
    )(queries, key_vectors, level_weight)


def turn_kernel(weight_ref, *half_refs):
    share = half_refs[0].shape[0]
    for num, half_ref in enumerate(half_refs):
        half_ref[...] = weight_ref[:, num * share : (num + 1) * share].T


def turn(weight, split):
    depth, width = weight.shape
    return pl.pallas_call(
        turn_kernel,
        out_shape=[pltpu.VMEM((width // split, depth), weight.dtype)] * split,
        compiler_params=pltpu.CompilerParams(vmem_limit_bytes=8 << 20),
        name="turn",
    )(weight)


def ring_order(count):
    return list(range(0, count, 2)) + list(range(1, count, 2))[::-1]


def place(offset, depth, piece_width):
    count = lax.axis_size("ctx")
    mine = lax.axis_index("ctx")
    pos = jnp.where(mine % 2 == 0, mine // 2, count - 1 - mine // 2)
    pos = (pos + offset + count) % count
    index = jnp.where(pos < count // 2, 2 * pos, 2 * (count - 1 - pos) + 1)
    per_piece = piece_width // depth
    return jnp.bitwise_xor(index // per_piece, lax.axis_index("head")), index % per_piece * depth


def choose(offsets, pieces, depth, chosen_ref):
    for num, offset in enumerate(offsets):
        piece, start = place(offset, depth, pieces[0].shape[1])
        start = pl.multiple_of(start, 128)
        for index, ref in enumerate(pieces):

            @pl.when(piece == index)
            def _():
                chosen_ref[:, num * depth : (num + 1) * depth] = ref[:, pl.ds(start, depth)]


def extend_kernel(piece_count, offsets, split, started, *refs):
    count = len(offsets)
    pieces = refs[:piece_count]
    blocks = [refs[piece_count + num * split :][:split] for num in range(count)]
    out_ref, chosen_ref = refs[-2], refs[-1]
    share, depth = blocks[0][0].shape
    choose(offsets, pieces, depth, chosen_ref)
    width = out_ref.shape[0]
    step = min(256, share)
    for c0 in range(0, width, step):
        at = c0 % share
        left = jnp.concatenate(
            [block[c0 // share][at : at + step, :] for block in blocks], axis=1
        )
        total = dot_last(left, chosen_ref[...])
        if started:
            total = total + refs[piece_count + count * split][c0 : c0 + step, :]
        out_ref[c0 : c0 + step, :] = total


def extend(total, pieces, parts):
    offsets = tuple(offset for offset, _ in parts)
    blocks = [half for _, block in parts for half in block]
    split = len(parts[0][1])
    rows = pieces[0].shape[0]
    share, depth = blocks[0].shape
    arrays = [*pieces, *blocks, *([] if total is None else [total])]
    return pl.pallas_call(
        functools.partial(extend_kernel, len(pieces), offsets, split, total is not None),
        in_specs=[pl.BlockSpec(memory_space=pltpu.VMEM)] * len(arrays),
        out_shape=pltpu.VMEM((share * split, rows), F32),
        scratch_shapes=[pltpu.VMEM((rows, depth * len(parts)), BF16)],
        compiler_params=pltpu.CompilerParams(vmem_limit_bytes=12 << 20),
    )(*arrays)


def finish_kernel(piece_count, offset, last_count, near_count, head_size, *refs):
    refs = list(refs)
    take = lambda count: [refs.pop(0) for _ in range(count)]
    token_refs, sum_refs = take(piece_count), take(piece_count)
    last_refs = take(last_count)
    value_ref, state_ref, q_ref, w_ref = take(4)
    near_refs = take(near_count)
    out_ref = refs.pop(0)
    length, state_rows = q_ref.shape
    width = value_ref.shape[0]
    near_levels = length.bit_length()
    far_levels = w_ref.shape[0] - near_levels
    rows = length // near_count
    if last_count:
        token_chosen, sum_chosen = refs
        depth = token_chosen.shape[1]
        choose([offset], token_refs, depth, token_chosen)
        choose([offset], sum_refs, depth, sum_chosen)
    mine = lax.axis_index("ctx")
    queries = q_ref[...]
    twice = jnp.concatenate([queries, queries], axis=1)
    step = min(256, width)
    unit = (
        lax.broadcasted_iota(jnp.int32, (rows, rows), 0)
        == lax.broadcasted_iota(jnp.int32, (rows, rows), 1)
    ).astype(BF16)
    for c0 in range(0, width, step):
        values, states = value_ref[c0 : c0 + step, :], state_ref[c0 : c0 + step, :]
        if last_count:
            share = width // last_count
            left = last_refs[c0 // share][c0 % share : c0 % share + step, :]
            values = values + dot_last(left, token_chosen[...])
            states = states + dot_last(left, sum_chosen[...])
        values = values.astype(BF16)
        heads = range(c0 // head_size, (c0 + step) // head_size)
        far = None
        for num in range(far_levels):
            state = states[:, num * state_rows : (num + 1) * state_rows]
            state = jnp.where(jnp.right_shift(mine, num) % 2 == 1, state, jnp.zeros_like(state))
            high = state.astype(BF16)
            low = (state - high.astype(F32)).astype(BF16)
            reading = dot_last(jnp.concatenate([high, low], axis=1), twice)
            level = near_levels + num
            weight = jnp.concatenate(
                [
                    spread_rows(w_ref[level, head : head + 1, :] * level_scale(level), head_size)
                    for head in heads
                ],
                axis=0,
            )
            far = weight * reading if far is None else far + weight * reading
        for block, near_ref in enumerate(near_refs):
            near = jnp.concatenate(
                [
                    jnp.dot(
                        values[
                            head * head_size - c0 : (head + 1) * head_size - c0,
                            : (block + 1) * rows,
                        ],
                        near_ref[head],
                        preferred_element_type=F32,
                    )
                    for head in heads
                ],
                axis=0,
            )
            total = (near + far[:, block * rows : (block + 1) * rows]).astype(BF16)
            out_ref[block * rows : (block + 1) * rows, c0 : c0 + step] = dot_last(
                unit, total
            ).astype(BF16)


def finish(values, states, offset, last, token_pieces, sum_pieces, queries, level_weight, near, head_size):
    width, length = values.shape
    arrays = [*token_pieces, *sum_pieces, *last, values, states, queries, level_weight, *near]
    scratch = []
    if last:
        depth = last[0].shape[1]
        scratch = [pltpu.VMEM((length, depth), BF16), pltpu.VMEM((states.shape[1], depth), BF16)]
    return pl.pallas_call(
        functools.partial(finish_kernel, len(token_pieces), offset, len(last), len(near), head_size),
        in_specs=[pl.BlockSpec(memory_space=pltpu.VMEM)] * len(arrays),
        out_shape=jax.ShapeDtypeStruct((length, width), BF16),
        scratch_shapes=scratch,
        compiler_params=pltpu.CompilerParams(vmem_limit_bytes=24 << 20),
        name="finish",
    )(*arrays)


def body(tokens, value_weight, queries, key_vectors, level_weight):
    _, width_feat = tokens.shape
    depth, width_local = value_weight.shape
    head_local = level_weight.shape[1]
    head_size = width_local // head_local
    ctx_count = lax.axis_size("ctx")
    dev_bits = ctx_count.bit_length() - 1
    near = prepare(queries, key_vectors, level_weight)

    running = jnp.einsum("tn,tf->nf", key_vectors, tokens, preferred_element_type=F32)
    level_sums = []
    for section_bit in range(dev_bits):
        partner = from_partner(running.astype(BF16), "ctx", section_bit)
        level_sums.append(partner)
        running = running + partner.astype(F32)
    level_sums = jnp.concatenate(level_sums, axis=0)

    if depth % 256 or width_feat % depth:
        features = lax.all_gather(tokens, "head", axis=1, tiled=True)
        sums = lax.all_gather(level_sums, "head", axis=1, tiled=True)
        weight = lax.all_gather(value_weight, "ctx", axis=0, tiled=True)
        values = jnp.einsum("fc,tf->ct", weight, features, preferred_element_type=F32)
        states = jnp.einsum("fc,nf->cn", weight, sums, preferred_element_type=F32)
        return finish(values, states, 0, [], [], [], queries, level_weight, near, head_size)

    order = ring_order(ctx_count)
    ahead = [(order[i], order[(i + 1) % ctx_count]) for i in range(ctx_count)]
    back = [(b, a) for a, b in ahead]
    half_count = ctx_count // 2
    token_pieces = on_chip(*gather_pieces(tokens, "head"))
    sum_pieces = on_chip(*gather_pieces(level_sums, "head"))
    cw = ccw = tuple(turn(value_weight, 2))
    steps = [[(0, cw)]]

    def move(part, route):
        return lax.ppermute(part, "ctx", route)

    for step in range(1, half_count):
        cw = tuple(move(part, ahead) for part in cw)
        ccw = tuple(move(part, back) for part in ccw)
        steps.append([(-step, on_chip(*cw)), (step, on_chip(*ccw))])
    last = on_chip(move(cw[0], ahead), move(ccw[1], back))
    values = extend(None, token_pieces, steps[0] + steps[1])
    for step in range(2, half_count):
        values = extend(values, token_pieces, steps[step])
    states = extend(None, sum_pieces, [part for parts in steps for part in parts])
    return finish(
        values,
        states,
        half_count,
        last,
        token_pieces,
        sum_pieces,
        queries,
        level_weight,
        near,
        head_size,
    )


def solution(mesh):
    return jax.shard_map(
        body,
        mesh=mesh,
        in_specs=(
            P("ctx", "head"),
            P("ctx", "head"),
            P("ctx", None),
            P("ctx", None),
            P(None, "head", "ctx"),
        ),
        out_specs=P("ctx", "head"),
        check_vma=False,
    )
```

```python
import functools

import jax
import jax.numpy as jnp
from jax import lax
from jax.experimental import pallas as pl
from jax.experimental.pallas import tpu as pltpu
from jax.sharding import PartitionSpec as P


F32 = jnp.float32
BF16 = jnp.bfloat16


def from_partner(block, axis, distance):
    count = lax.axis_size(axis)
    route = []
    for low in range(count):
        high = low | 1 << distance
        if high != low and high < count:
            route += [(low, high), (high, low)]
    return lax.ppermute(block, axis, route)


def gather_pieces(block, axis):
    pieces = [block]
    masks = [0]
    for bit in reversed(range(lax.axis_size(axis).bit_length() - 1)):
        for mask, piece in zip(list(masks), list(pieces)):
            pieces.append(from_partner(piece, axis, bit))
            masks.append(mask | 1 << bit)
    return [piece for _, piece in sorted(zip(masks, pieces), key=lambda pair: pair[0])]


def level_scale(level_num):
    return 1.0 if level_num == 0 else 2.0 ** (-(level_num - 1) / 2.0)


def on_chip(*arrays):
    return [pltpu.with_memory_space_constraint(array, pltpu.VMEM) for array in arrays]


def dot_last(left, right):
    return lax.dot_general(left, right, (((1,), (1,)), ((), ())), preferred_element_type=F32)


def spread_rows(row, count):
    return jnp.broadcast_to(row, (count, row.shape[1]))


def prepare_kernel(q_ref, k_ref, w_ref, near_ref, score_ref, row_ref):
    length = q_ref.shape[0]
    heads, _, rows = near_ref.shape
    tile = min(128, length)
    sub = 8
    tile_levels = tile.bit_length() - 1
    sub_levels = sub.bit_length() - 1
    score_ref[...] = dot_last(k_ref[...], q_ref[...]).astype(BF16)
    for num in range(rows.bit_length()):
        for head in range(heads):
            row_ref[head, num : num + 1, :] = w_ref[num, head : head + 1, :] * level_scale(num)

    def grid_level(shape, shift):
        s_pos = lax.broadcasted_iota(jnp.int32, shape, 0)
        t_pos = jnp.right_shift(lax.broadcasted_iota(jnp.int32, shape, 1), shift)
        if shift == 0:
            t_pos = jnp.bitwise_and(t_pos, sub - 1)
        differ = jnp.bitwise_xor(s_pos, t_pos)
        level = jnp.zeros(shape, jnp.int32)
        for bit in range(tile_levels):
            level = level + (jnp.right_shift(differ, bit) > 0).astype(jnp.int32)
        return jnp.where(s_pos <= t_pos, level, -1)

    fine = grid_level((sub, tile), 0)
    coarse = grid_level((tile // sub, tile), sub_levels)
    near_diag = lax.broadcasted_iota(jnp.int32, (tile, tile), 0) // sub == (
        lax.broadcasted_iota(jnp.int32, (tile, tile), 1) // sub
    )

    def one_head(head, carry):
        for t0 in range(0, length, tile):
            base = t0 // rows * rows
            weight_rows = [
                row_ref[head, num : num + 1, t0 : t0 + tile] for num in range(rows.bit_length())
            ]
            for s0 in range(base, base + rows, tile):
                place_at = (head, pl.ds(s0, tile), pl.ds(t0 - base, tile))
                if s0 > t0:
                    near_ref[place_at] = jnp.zeros((tile, tile), BF16)
                    continue
                if s0 == t0:
                    small = jnp.zeros((sub, tile), F32)
                    for num in range(sub_levels + 1):
                        small = jnp.where(fine == num, spread_rows(weight_rows[num], sub), small)
                    big = jnp.zeros((tile // sub, tile), F32)
                    for num in range(sub_levels + 1, tile_levels + 1):
                        big = jnp.where(
                            coarse == num - sub_levels,
                            spread_rows(weight_rows[num], tile // sub),
                            big,
                        )
                    big = jnp.concatenate(
                        [spread_rows(big[row : row + 1], sub) for row in range(tile // sub)], axis=0
                    )
                    weight = jnp.where(near_diag, jnp.concatenate([small] * (tile // sub), 0), big)
                else:
                    num = tile_levels + (s0 // tile ^ t0 // tile).bit_length()
                    weight = spread_rows(weight_rows[num], tile)
                score = score_ref[s0 : s0 + tile, t0 : t0 + tile].astype(F32)
                near_ref[place_at] = (weight * score).astype(BF16)
        return carry

    lax.fori_loop(0, heads, one_head, 0)


def prepare(queries, key_vectors, level_weight):
    length = queries.shape[0]
    heads = level_weight.shape[1]
    rows = min(256, length)
    return pl.pallas_call(
        prepare_kernel,
        out_shape=[
            pltpu.VMEM((heads, length, rows), BF16),
            pltpu.VMEM((length, length), BF16),
        ],
        scratch_shapes=[pltpu.VMEM((heads, rows.bit_length(), length), F32)],
        compiler_params=pltpu.CompilerParams(vmem_limit_bytes=16 << 20),
        name="prepare",
    )(queries, key_vectors, level_weight)


def begin_kernel(k_ref, token_ref, weight_ref, sum_ref, sent_ref, *part_refs):
    total = lax.dot_general(
        k_ref[...], token_ref[...], (((0,), (0,)), ((), ())), preferred_element_type=F32
    )
    sum_ref[...] = total
    sent_ref[...] = total.astype(BF16)
    share = part_refs[0].shape[0]
    for num, part_ref in enumerate(part_refs):
        part_ref[...] = weight_ref[:, num * share : (num + 1) * share].T


def begin(key_vectors, tokens, weight, split):
    depth, width = weight.shape
    shape = (key_vectors.shape[1], tokens.shape[1])
    return pl.pallas_call(
        begin_kernel,
        out_shape=[pltpu.VMEM(shape, F32), pltpu.VMEM(shape, BF16)]
        + [pltpu.VMEM((width // split, depth), weight.dtype)] * split,
        compiler_params=pltpu.CompilerParams(vmem_limit_bytes=8 << 20),
        name="begin",
    )(key_vectors, tokens, weight)


def ring_order(count):
    return list(range(0, count, 2)) + list(range(1, count, 2))[::-1]


def place(offset, depth, piece_width):
    count = lax.axis_size("ctx")
    mine = lax.axis_index("ctx")
    pos = jnp.where(mine % 2 == 0, mine // 2, count - 1 - mine // 2)
    pos = (pos + offset + count) % count
    index = jnp.where(pos < count // 2, 2 * pos, 2 * (count - 1 - pos) + 1)
    per_piece = piece_width // depth
    return jnp.bitwise_xor(index // per_piece, lax.axis_index("head")), index % per_piece * depth


def choose(offsets, pieces, depth, chosen_ref):
    for num, offset in enumerate(offsets):
        piece, start = place(offset, depth, pieces[0][0].shape[1])
        start = pl.multiple_of(start, 128)
        for index, parts in enumerate(pieces):

            @pl.when(piece == index)
            def _():
                row = 0
                for ref in parts:
                    rows = ref.shape[0]
                    chosen_ref[row : row + rows, num * depth : (num + 1) * depth] = ref[
                        :, pl.ds(start, depth)
                    ]
                    row += rows


def in_parts(refs, count):
    return [refs[num : num + count] for num in range(0, len(refs), count)]


def extend_kernel(piece_count, parts, offsets, split, started, *refs):
    count = len(offsets)
    pieces = in_parts(refs[:piece_count], parts)
    blocks = [refs[piece_count + num * split :][:split] for num in range(count)]
    out_ref, chosen_ref = refs[-2], refs[-1]
    share, depth = blocks[0][0].shape
    choose(offsets, pieces, depth, chosen_ref)
    width = out_ref.shape[0]
    step = min(256, share)
    for c0 in range(0, width, step):
        at = c0 % share
        left = jnp.concatenate(
            [block[c0 // share][at : at + step, :] for block in blocks], axis=1
        )
        total = dot_last(left, chosen_ref[...])
        if started:
            total = total + refs[piece_count + count * split][c0 : c0 + step, :]
        out_ref[c0 : c0 + step, :] = total


def extend(total, pieces, parts):
    offsets = tuple(offset for offset, _ in parts)
    blocks = [half for _, block in parts for half in block]
    split = len(parts[0][1])
    rows = sum(part.shape[0] for part in pieces[0])
    share, depth = blocks[0].shape
    flat = [part for piece in pieces for part in piece]
    arrays = [*flat, *blocks, *([] if total is None else [total])]
    return pl.pallas_call(
        functools.partial(
            extend_kernel, len(flat), len(pieces[0]), offsets, split, total is not None
        ),
        in_specs=[pl.BlockSpec(memory_space=pltpu.VMEM)] * len(arrays),
        out_shape=pltpu.VMEM((share * split, rows), F32),
        scratch_shapes=[pltpu.VMEM((rows, depth * len(parts)), BF16)],
        compiler_params=pltpu.CompilerParams(vmem_limit_bytes=12 << 20),
    )(*arrays)


def finish_kernel(piece_count, sum_parts, offset, last_count, head_size, *refs):
    refs = list(refs)
    take = lambda count: [refs.pop(0) for _ in range(count)]
    token_refs, sum_refs = take(piece_count), take(piece_count * sum_parts)
    last_refs = take(last_count)
    value_ref, state_ref, q_ref, w_ref, near_ref, score_ref, out_ref = take(7)
    length, state_rows = q_ref.shape
    width = value_ref.shape[0]
    near_levels = length.bit_length()
    far_levels = w_ref.shape[0] - near_levels
    rows = near_ref.shape[2]
    if last_count:
        token_chosen, sum_chosen = refs
        depth = token_chosen.shape[1]
        choose([offset], in_parts(token_refs, 1), depth, token_chosen)
        choose([offset], in_parts(sum_refs, sum_parts), depth, sum_chosen)
    mine = lax.axis_index("ctx")
    queries = q_ref[...]
    twice = jnp.concatenate([queries, queries], axis=1)
    step = min(256, width)
    unit = (
        lax.broadcasted_iota(jnp.int32, (rows, rows), 0)
        == lax.broadcasted_iota(jnp.int32, (rows, rows), 1)
    ).astype(BF16)
    for c0 in range(0, width, step):
        values, states = value_ref[c0 : c0 + step, :], state_ref[c0 : c0 + step, :]
        if last_count:
            share = width // last_count
            left = last_refs[c0 // share][c0 % share : c0 % share + step, :]
            values = values + dot_last(left, token_chosen[...])
            states = states + dot_last(left, sum_chosen[...])
        values = values.astype(BF16)
        heads = range(c0 // head_size, (c0 + step) // head_size)

        def weight(level, low, high):
            return jnp.concatenate(
                [
                    spread_rows(
                        w_ref[level, head : head + 1, low:high] * level_scale(level), head_size
                    )
                    for head in heads
                ],
                axis=0,
            )

        far = None
        for num in range(far_levels):
            state = states[:, num * state_rows : (num + 1) * state_rows]
            state = jnp.where(jnp.right_shift(mine, num) % 2 == 1, state, jnp.zeros_like(state))
            high = state.astype(BF16)
            low = (state - high.astype(F32)).astype(BF16)
            reading = dot_last(jnp.concatenate([high, low], axis=1), twice)
            reading = weight(near_levels + num, 0, length) * reading
            far = reading if far is None else far + reading
        for t0 in range(0, length, rows):
            total = far[:, t0 : t0 + rows] + jnp.concatenate(
                [
                    jnp.dot(
                        values[head * head_size - c0 : (head + 1) * head_size - c0, t0 : t0 + rows],
                        near_ref[head, t0 : t0 + rows, :],
                        preferred_element_type=F32,
                    )
                    for head in heads
                ],
                axis=0,
            )
            for level in range(rows.bit_length(), near_levels):
                span = 1 << level - 1
                if t0 & span:
                    s0 = t0 // span * span - span
                    mixed = jnp.dot(
                        values[:, s0 : s0 + span],
                        score_ref[s0 : s0 + span, t0 : t0 + rows],
                        preferred_element_type=F32,
                    )
                    total = total + weight(level, t0, t0 + rows) * mixed
            out_ref[t0 : t0 + rows, c0 : c0 + step] = dot_last(unit, total.astype(BF16)).astype(
                BF16
            )


def finish(values, states, offset, last, token_pieces, sum_pieces, queries, level_weight, near, head_size):
    width, length = values.shape
    sum_parts = len(sum_pieces[0]) if sum_pieces else 1
    flat_sums = [part for piece in sum_pieces for part in piece]
    flat_tokens = [piece[0] for piece in token_pieces]
    arrays = [*flat_tokens, *flat_sums, *last, values, states, queries, level_weight, *near]
    scratch = []
    if last:
        depth = last[0].shape[1]
        scratch = [pltpu.VMEM((length, depth), BF16), pltpu.VMEM((states.shape[1], depth), BF16)]
    return pl.pallas_call(
        functools.partial(
            finish_kernel, len(flat_tokens), sum_parts, offset, len(last), head_size
        ),
        in_specs=[pl.BlockSpec(memory_space=pltpu.VMEM)] * len(arrays),
        out_shape=jax.ShapeDtypeStruct((length, width), BF16),
        scratch_shapes=scratch,
        compiler_params=pltpu.CompilerParams(vmem_limit_bytes=24 << 20),
        name="finish",
    )(*arrays)


def body(tokens, value_weight, queries, key_vectors, level_weight):
    _, width_feat = tokens.shape
    depth, width_local = value_weight.shape
    head_local = level_weight.shape[1]
    head_size = width_local // head_local
    ctx_count = lax.axis_size("ctx")
    dev_bits = ctx_count.bit_length() - 1
    near = prepare(queries, key_vectors, level_weight)

    running, sent, *turned = begin(key_vectors, tokens, value_weight, 2)
    level_sums = []
    for section_bit in range(dev_bits):
        if section_bit > 0:
            sent = running.astype(BF16)
        if section_bit == dev_bits - 1 and dev_bits > 1:
            break
        partner = from_partner(sent, "ctx", section_bit)
        level_sums.append(partner)
        running = running + partner.astype(F32)
    if dev_bits > 1:
        unit = ctx_count // 4
        for hop in range(2):
            route = [((1 + hop) * unit + num, (2 + hop) * unit + num) for num in range(unit)]
            sent = lax.ppermute(sent, "ctx", route)
            top = sent if hop == 0 else top + sent
        level_sums.append(top)
    low_sums = jnp.concatenate(level_sums[:-1] or level_sums, axis=0)
    top_sums = level_sums[-1:] if dev_bits > 1 else []

    if depth % 256 or width_feat % depth:
        features = lax.all_gather(tokens, "head", axis=1, tiled=True)
        level_sums = jnp.concatenate([low_sums, *top_sums], axis=0)
        sums = lax.all_gather(level_sums, "head", axis=1, tiled=True)
        weight = lax.all_gather(value_weight, "ctx", axis=0, tiled=True)
        values = jnp.einsum("fc,tf->ct", weight, features, preferred_element_type=F32)
        states = jnp.einsum("fc,nf->cn", weight, sums, preferred_element_type=F32)
        return finish(values, states, 0, [], [], [], queries, level_weight, near, head_size)

    order = ring_order(ctx_count)
    ahead = [(order[i], order[(i + 1) % ctx_count]) for i in range(ctx_count)]
    back = [(b, a) for a, b in ahead]
    half_count = ctx_count // 2
    token_pieces = [[piece] for piece in on_chip(*gather_pieces(tokens, "head"))]
    low_pieces = on_chip(*gather_pieces(low_sums, "head"))
    top_pieces = [on_chip(*gather_pieces(sums, "head")) for sums in top_sums]
    sum_pieces = list(zip(low_pieces, *top_pieces))
    cw = ccw = tuple(turned)
    steps = [[(0, cw)]]

    def move(part, route):
        return lax.ppermute(part, "ctx", route)

    for step in range(1, half_count):
        cw = tuple(move(part, ahead) for part in cw)
        ccw = tuple(move(part, back) for part in ccw)
        steps.append([(-step, on_chip(*cw)), (step, on_chip(*ccw))])
    last = on_chip(move(cw[0], ahead), move(ccw[1], back))
    values = extend(None, token_pieces, steps[0] + steps[1])
    for step in range(2, half_count):
        values = extend(values, token_pieces, steps[step])
    states = extend(None, sum_pieces, [part for parts in steps for part in parts])
    return finish(
        values,
        states,
        half_count,
        last,
        token_pieces,
        sum_pieces,
        queries,
        level_weight,
        near,
        head_size,
    )


def solution(mesh):
    return jax.shard_map(
        body,
        mesh=mesh,
        in_specs=(
            P("ctx", "head"),
            P("ctx", "head"),
            P("ctx", None),
            P("ctx", None),
            P(None, "head", "ctx"),
        ),
        out_specs=P("ctx", "head"),
        check_vma=False,
    )
```

```python
import functools

import jax
import jax.numpy as jnp
from jax import lax
from jax.experimental import pallas as pl
from jax.experimental.pallas import tpu as pltpu
from jax.sharding import PartitionSpec as P


F32 = jnp.float32
BF16 = jnp.bfloat16


def from_partner(block, axis, distance):
    count = lax.axis_size(axis)
    route = []
    for low in range(count):
        high = low | 1 << distance
        if high != low and high < count:
            route += [(low, high), (high, low)]
    return lax.ppermute(block, axis, route)


def gather_pieces(block, axis):
    pieces = [block]
    masks = [0]
    for bit in reversed(range(lax.axis_size(axis).bit_length() - 1)):
        for mask, piece in zip(list(masks), list(pieces)):
            pieces.append(from_partner(piece, axis, bit))
            masks.append(mask | 1 << bit)
    return [piece for _, piece in sorted(zip(masks, pieces), key=lambda pair: pair[0])]


def level_scale(level_num):
    return 1.0 if level_num == 0 else 2.0 ** (-(level_num - 1) / 2.0)


def on_chip(*arrays):
    return [pltpu.with_memory_space_constraint(array, pltpu.VMEM) for array in arrays]


def dot_last(left, right):
    return lax.dot_general(left, right, (((1,), (1,)), ((), ())), preferred_element_type=F32)


def spread_rows(row, count):
    return jnp.broadcast_to(row, (count, row.shape[1]))


def prepare_kernel(q_ref, k_ref, w_ref, near_ref, score_ref, row_ref):
    length = q_ref.shape[0]
    heads, _, rows = near_ref.shape
    tile = min(128, length)
    sub = 8
    tile_levels = tile.bit_length() - 1
    sub_levels = sub.bit_length() - 1
    score_ref[...] = dot_last(k_ref[...], q_ref[...]).astype(BF16)
    for num in range(rows.bit_length()):
        for head in range(heads):
            row_ref[head, num : num + 1, :] = w_ref[num, head : head + 1, :] * level_scale(num)

    def grid_level(shape, shift):
        s_pos = lax.broadcasted_iota(jnp.int32, shape, 0)
        t_pos = jnp.right_shift(lax.broadcasted_iota(jnp.int32, shape, 1), shift)
        if shift == 0:
            t_pos = jnp.bitwise_and(t_pos, sub - 1)
        differ = jnp.bitwise_xor(s_pos, t_pos)
        level = jnp.zeros(shape, jnp.int32)
        for bit in range(tile_levels):
            level = level + (jnp.right_shift(differ, bit) > 0).astype(jnp.int32)
        return jnp.where(s_pos <= t_pos, level, -1)

    fine = grid_level((sub, tile), 0)
    coarse = grid_level((tile // sub, tile), sub_levels)
    near_diag = lax.broadcasted_iota(jnp.int32, (tile, tile), 0) // sub == (
        lax.broadcasted_iota(jnp.int32, (tile, tile), 1) // sub
    )

    def one_head(head, carry):
        for t0 in range(0, length, tile):
            base = t0 // rows * rows
            weight_rows = [
                row_ref[head, num : num + 1, t0 : t0 + tile] for num in range(rows.bit_length())
            ]
            for s0 in range(base, base + rows, tile):
                place_at = (head, pl.ds(s0, tile), pl.ds(t0 - base, tile))
                if s0 > t0:
                    near_ref[place_at] = jnp.zeros((tile, tile), BF16)
                    continue
                if s0 == t0:
                    small = jnp.zeros((sub, tile), F32)
                    for num in range(sub_levels + 1):
                        small = jnp.where(fine == num, spread_rows(weight_rows[num], sub), small)
                    big = jnp.zeros((tile // sub, tile), F32)
                    for num in range(sub_levels + 1, tile_levels + 1):
                        big = jnp.where(
                            coarse == num - sub_levels,
                            spread_rows(weight_rows[num], tile // sub),
                            big,
                        )
                    big = jnp.concatenate(
                        [spread_rows(big[row : row + 1], sub) for row in range(tile // sub)], axis=0
                    )
                    weight = jnp.where(near_diag, jnp.concatenate([small] * (tile // sub), 0), big)
                else:
                    num = tile_levels + (s0 // tile ^ t0 // tile).bit_length()
                    weight = spread_rows(weight_rows[num], tile)
                score = score_ref[s0 : s0 + tile, t0 : t0 + tile].astype(F32)
                near_ref[place_at] = (weight * score).astype(BF16)
        return carry

    lax.fori_loop(0, heads, one_head, 0)


def prepare(queries, key_vectors, level_weight):
    length = queries.shape[0]
    heads = level_weight.shape[1]
    rows = min(256, length)
    return pl.pallas_call(
        prepare_kernel,
        out_shape=[
            pltpu.VMEM((heads, length, rows), BF16),
            pltpu.VMEM((length, length), BF16),
        ],
        scratch_shapes=[pltpu.VMEM((heads, rows.bit_length(), length), F32)],
        compiler_params=pltpu.CompilerParams(vmem_limit_bytes=16 << 20),
        name="prepare",
    )(queries, key_vectors, level_weight)


def turn_kernel(weight_ref, *part_refs):
    share = part_refs[0].shape[0]
    for num, part_ref in enumerate(part_refs):
        part_ref[...] = weight_ref[:, num * share : (num + 1) * share].T


def turn(weight, split):
    depth, width = weight.shape
    return pl.pallas_call(
        turn_kernel,
        out_shape=[pltpu.VMEM((width // split, depth), weight.dtype)] * split,
        compiler_params=pltpu.CompilerParams(vmem_limit_bytes=8 << 20),
        name="turn",
    )(weight)


def begin_kernel(k_ref, token_ref, sum_ref, sent_ref, held_ref):
    tokens = token_ref[...]
    total = lax.dot_general(
        k_ref[...], tokens, (((0,), (0,)), ((), ())), preferred_element_type=F32
    )
    sum_ref[...] = total
    sent_ref[...] = total.astype(BF16)
    held_ref[...] = tokens


def begin(key_vectors, tokens):
    shape = (key_vectors.shape[1], tokens.shape[1])
    return pl.pallas_call(
        begin_kernel,
        out_shape=[
            pltpu.VMEM(shape, F32),
            pltpu.VMEM(shape, BF16),
            pltpu.VMEM(tokens.shape, tokens.dtype),
        ],
        compiler_params=pltpu.CompilerParams(vmem_limit_bytes=8 << 20),
        name="begin",
    )(key_vectors, tokens)


def ring_order(count):
    return list(range(0, count, 2)) + list(range(1, count, 2))[::-1]


def place(offset, depth, piece_width):
    count = lax.axis_size("ctx")
    mine = lax.axis_index("ctx")
    pos = jnp.where(mine % 2 == 0, mine // 2, count - 1 - mine // 2)
    pos = (pos + offset + count) % count
    index = jnp.where(pos < count // 2, 2 * pos, 2 * (count - 1 - pos) + 1)
    per_piece = piece_width // depth
    return jnp.bitwise_xor(index // per_piece, lax.axis_index("head")), index % per_piece * depth


def choose(offsets, pieces, depth, chosen_ref):
    for num, offset in enumerate(offsets):
        piece, start = place(offset, depth, pieces[0].shape[1])
        start = pl.multiple_of(start, 128)
        for index, ref in enumerate(pieces):

            @pl.when(piece == index)
            def _():
                chosen_ref[:, num * depth : (num + 1) * depth] = ref[:, pl.ds(start, depth)]


def extend_kernel(piece_count, offsets, split, started, *refs):
    count = len(offsets)
    pieces = refs[:piece_count]
    blocks = [refs[piece_count + num * split :][:split] for num in range(count)]
    out_ref, chosen_ref = refs[-2], refs[-1]
    share, depth = blocks[0][0].shape
    choose(offsets, pieces, depth, chosen_ref)
    width = out_ref.shape[0]
    step = min(256, share)
    for c0 in range(0, width, step):
        at = c0 % share
        left = jnp.concatenate(
            [block[c0 // share][at : at + step, :] for block in blocks], axis=1
        )
        total = dot_last(left, chosen_ref[...])
        if started:
            total = total + refs[piece_count + count * split][c0 : c0 + step, :]
        out_ref[c0 : c0 + step, :] = total


def extend(total, pieces, parts):
    offsets = tuple(offset for offset, _ in parts)
    blocks = [half for _, block in parts for half in block]
    split = len(parts[0][1])
    rows = pieces[0].shape[0]
    share, depth = blocks[0].shape
    arrays = [*pieces, *blocks, *([] if total is None else [total])]
    return pl.pallas_call(
        functools.partial(
            extend_kernel, len(pieces), offsets, split, total is not None
        ),
        in_specs=[pl.BlockSpec(memory_space=pltpu.VMEM)] * len(arrays),
        out_shape=pltpu.VMEM((share * split, rows), F32),
        scratch_shapes=[pltpu.VMEM((rows, depth * len(parts)), BF16)],
        compiler_params=pltpu.CompilerParams(vmem_limit_bytes=12 << 20),
    )(*arrays)


def finish_kernel(piece_count, groups, offset, last_count, head_size, *refs):
    refs = list(refs)
    take = lambda count: [refs.pop(0) for _ in range(count)]
    token_refs, sum_refs = take(piece_count), [take(piece_count) for _ in range(groups)]
    last_refs = take(last_count)
    value_ref, state_refs = refs.pop(0), take(groups)
    q_ref, w_ref, near_ref, score_ref, out_ref = take(5)
    length, state_rows = q_ref.shape
    width = value_ref.shape[0]
    near_levels = length.bit_length()
    far_levels = w_ref.shape[0] - near_levels
    rows = near_ref.shape[2]
    if last_count:
        token_chosen, *sum_chosen = refs
        depth = token_chosen.shape[1]
        choose([offset], token_refs, depth, token_chosen)
        for pieces, chosen in zip(sum_refs, sum_chosen):
            choose([offset], pieces, depth, chosen)
    mine = lax.axis_index("ctx")
    queries = q_ref[...]
    twice = jnp.concatenate([queries, queries], axis=1)
    step = min(256, width)
    unit = (
        lax.broadcasted_iota(jnp.int32, (rows, rows), 0)
        == lax.broadcasted_iota(jnp.int32, (rows, rows), 1)
    ).astype(BF16)
    for c0 in range(0, width, step):
        values = value_ref[c0 : c0 + step, :]
        states = [ref[c0 : c0 + step, :] for ref in state_refs]
        if last_count:
            share = width // last_count
            left = last_refs[c0 // share][c0 % share : c0 % share + step, :]
            values = values + dot_last(left, token_chosen[...])
            states = [
                part + dot_last(left, chosen[...]) for part, chosen in zip(states, sum_chosen)
            ]
        values = values.astype(BF16)
        heads = range(c0 // head_size, (c0 + step) // head_size)

        def weight(level, low, high):
            return jnp.concatenate(
                [
                    spread_rows(
                        w_ref[level, head : head + 1, low:high] * level_scale(level), head_size
                    )
                    for head in heads
                ],
                axis=0,
            )

        far = None
        states = jnp.concatenate(states, axis=1)
        for num in range(far_levels):
            state = states[:, num * state_rows : (num + 1) * state_rows]
            state = jnp.where(jnp.right_shift(mine, num) % 2 == 1, state, jnp.zeros_like(state))
            high = state.astype(BF16)
            low = (state - high.astype(F32)).astype(BF16)
            reading = dot_last(jnp.concatenate([high, low], axis=1), twice)
            reading = weight(near_levels + num, 0, length) * reading
            far = reading if far is None else far + reading
        for t0 in range(0, length, rows):
            total = far[:, t0 : t0 + rows] + jnp.concatenate(
                [
                    jnp.dot(
                        values[head * head_size - c0 : (head + 1) * head_size - c0, t0 : t0 + rows],
                        near_ref[head, t0 : t0 + rows, :],
                        preferred_element_type=F32,
                    )
                    for head in heads
                ],
                axis=0,
            )
            for level in range(rows.bit_length(), near_levels):
                span = 1 << level - 1
                if t0 & span:
                    s0 = t0 // span * span - span
                    mixed = jnp.dot(
                        values[:, s0 : s0 + span],
                        score_ref[s0 : s0 + span, t0 : t0 + rows],
                        preferred_element_type=F32,
                    )
                    total = total + weight(level, t0, t0 + rows) * mixed
            out_ref[t0 : t0 + rows, c0 : c0 + step] = dot_last(unit, total.astype(BF16)).astype(
                BF16
            )


def finish(values, states, offset, last, token_pieces, sum_pieces, queries, level_weight, near, head_size):
    width, length = values.shape
    flat_sums = [piece for pieces in sum_pieces for piece in pieces]
    arrays = [*token_pieces, *flat_sums, *last, values, *states, queries, level_weight, *near]
    scratch = []
    if last:
        depth = last[0].shape[1]
        scratch = [pltpu.VMEM((rows, depth), BF16) for rows in [length, *(s.shape[1] for s in states)]]
    return pl.pallas_call(
        functools.partial(
            finish_kernel, len(token_pieces), len(states), offset, len(last), head_size
        ),
        in_specs=[pl.BlockSpec(memory_space=pltpu.VMEM)] * len(arrays),
        out_shape=jax.ShapeDtypeStruct((length, width), BF16),
        scratch_shapes=scratch,
        compiler_params=pltpu.CompilerParams(vmem_limit_bytes=24 << 20),
        name="finish",
    )(*arrays)


def body(tokens, value_weight, queries, key_vectors, level_weight):
    _, width_feat = tokens.shape
    depth, width_local = value_weight.shape
    head_local = level_weight.shape[1]
    head_size = width_local // head_local
    ctx_count = lax.axis_size("ctx")
    dev_bits = ctx_count.bit_length() - 1
    near = prepare(queries, key_vectors, level_weight)

    running, sent, held = begin(key_vectors, tokens)
    level_sums = []
    for section_bit in range(dev_bits):
        if section_bit > 0:
            sent = running.astype(BF16)
        if section_bit == dev_bits - 1 and dev_bits > 1:
            break
        partner = from_partner(sent, "ctx", section_bit)
        level_sums.append(partner)
        running = running + partner.astype(F32)
    if dev_bits > 1:
        unit = ctx_count // 4
        for hop in range(2):
            route = [((1 + hop) * unit + num, (2 + hop) * unit + num) for num in range(unit)]
            sent = lax.ppermute(sent, "ctx", route)
            top = sent if hop == 0 else top + sent
        level_sums.append(top)
    low_sums = jnp.concatenate(level_sums[:-1] or level_sums, axis=0)
    top_sums = level_sums[-1:] if dev_bits > 1 else []

    if depth % 256 or width_feat % depth:
        features = lax.all_gather(tokens, "head", axis=1, tiled=True)
        level_sums = jnp.concatenate([low_sums, *top_sums], axis=0)
        sums = lax.all_gather(level_sums, "head", axis=1, tiled=True)
        weight = lax.all_gather(value_weight, "ctx", axis=0, tiled=True)
        values = jnp.einsum("fc,tf->ct", weight, features, preferred_element_type=F32)
        states = jnp.einsum("fc,nf->cn", weight, sums, preferred_element_type=F32)
        return finish(values, [states], 0, [], [], [[]], queries, level_weight, near, head_size)

    order = ring_order(ctx_count)
    ahead = [(order[i], order[(i + 1) % ctx_count]) for i in range(ctx_count)]
    back = [(b, a) for a, b in ahead]
    half_count = ctx_count // 2
    token_pieces = on_chip(*gather_pieces(held, "head"))
    sum_pieces = [on_chip(*gather_pieces(low_sums, "head"))]
    sum_pieces += [on_chip(*gather_pieces(sums, "head")) for sums in top_sums]
    cw = ccw = tuple(turn(value_weight, 2))
    steps = [[(0, cw)]]

    def move(part, route):
        return lax.ppermute(part, "ctx", route)

    for step in range(1, half_count):
        cw = tuple(move(part, ahead) for part in cw)
        ccw = tuple(move(part, back) for part in ccw)
        steps.append([(-step, on_chip(*cw)), (step, on_chip(*ccw))])
    last = on_chip(move(cw[0], ahead), move(ccw[1], back))
    values = extend(None, token_pieces, steps[0] + steps[1])
    for step in range(2, half_count):
        values = extend(values, token_pieces, steps[step])
    every = [part for parts in steps for part in parts]
    states = [extend(None, pieces, every) for pieces in sum_pieces]
    return finish(
        values,
        states,
        half_count,
        last,
        token_pieces,
        sum_pieces,
        queries,
        level_weight,
        near,
        head_size,
    )


def solution(mesh):
    return jax.shard_map(
        body,
        mesh=mesh,
        in_specs=(
            P("ctx", "head"),
            P("ctx", "head"),
            P("ctx", None),
            P("ctx", None),
            P(None, "head", "ctx"),
        ),
        out_specs=P("ctx", "head"),
        check_vma=False,
    )
```

```python
import functools

import jax
import jax.numpy as jnp
from jax import lax
from jax.experimental import pallas as pl
from jax.experimental.pallas import tpu as pltpu
from jax.sharding import PartitionSpec as P


F32 = jnp.float32
BF16 = jnp.bfloat16


def from_partner(block, axis, distance):
    count = lax.axis_size(axis)
    route = []
    for low in range(count):
        high = low | 1 << distance
        if high != low and high < count:
            route += [(low, high), (high, low)]
    return lax.ppermute(block, axis, route)


def gather_pieces(block, axis):
    pieces = [block]
    masks = [0]
    for bit in reversed(range(lax.axis_size(axis).bit_length() - 1)):
        for mask, piece in zip(list(masks), list(pieces)):
            pieces.append(from_partner(piece, axis, bit))
            masks.append(mask | 1 << bit)
    return [piece for _, piece in sorted(zip(masks, pieces), key=lambda pair: pair[0])]


def level_scale(level_num):
    return 1.0 if level_num == 0 else 2.0 ** (-(level_num - 1) / 2.0)


def on_chip(*arrays):
    return [pltpu.with_memory_space_constraint(array, pltpu.VMEM) for array in arrays]


def off_chip(*arrays):
    return [pltpu.with_memory_space_constraint(array, pltpu.HBM) for array in arrays]


def dot_last(left, right):
    return lax.dot_general(left, right, (((1,), (1,)), ((), ())), preferred_element_type=F32)


def spread_rows(row, count):
    return jnp.broadcast_to(row, (count, row.shape[1]))


def prepare_kernel(q_hbm, k_hbm, w_hbm, near_ref, score_ref, row_ref, q_ref, k_ref, w_ref, sems):
    loads = [
        pltpu.make_async_copy(source, target, sems.at[num])
        for num, (source, target) in enumerate([(q_hbm, q_ref), (k_hbm, k_ref), (w_hbm, w_ref)])
    ]
    for load in loads:
        load.start()
    for load in loads:
        load.wait()
    length = q_ref.shape[0]
    heads, _, rows = near_ref.shape
    tile = min(128, length)
    sub = 8
    tile_levels = tile.bit_length() - 1
    sub_levels = sub.bit_length() - 1
    score_ref[...] = dot_last(k_ref[...], q_ref[...]).astype(BF16)
    for num in range(rows.bit_length()):
        for head in range(heads):
            row_ref[head, num : num + 1, :] = w_ref[num, head : head + 1, :] * level_scale(num)

    def grid_level(shape, shift):
        s_pos = lax.broadcasted_iota(jnp.int32, shape, 0)
        t_pos = jnp.right_shift(lax.broadcasted_iota(jnp.int32, shape, 1), shift)
        if shift == 0:
            t_pos = jnp.bitwise_and(t_pos, sub - 1)
        differ = jnp.bitwise_xor(s_pos, t_pos)
        level = jnp.zeros(shape, jnp.int32)
        for bit in range(tile_levels):
            level = level + (jnp.right_shift(differ, bit) > 0).astype(jnp.int32)
        return jnp.where(s_pos <= t_pos, level, -1)

    fine = grid_level((sub, tile), 0)
    coarse = grid_level((tile // sub, tile), sub_levels)
    near_diag = lax.broadcasted_iota(jnp.int32, (tile, tile), 0) // sub == (
        lax.broadcasted_iota(jnp.int32, (tile, tile), 1) // sub
    )

    def one_head(head, carry):
        for t0 in range(0, length, tile):
            base = t0 // rows * rows
            weight_rows = [
                row_ref[head, num : num + 1, t0 : t0 + tile] for num in range(rows.bit_length())
            ]
            for s0 in range(base, base + rows, tile):
                place_at = (head, pl.ds(s0, tile), pl.ds(t0 - base, tile))
                if s0 > t0:
                    near_ref[place_at] = jnp.zeros((tile, tile), BF16)
                    continue
                if s0 == t0:
                    small = jnp.zeros((sub, tile), F32)
                    for num in range(sub_levels + 1):
                        small = jnp.where(fine == num, spread_rows(weight_rows[num], sub), small)
                    big = jnp.zeros((tile // sub, tile), F32)
                    for num in range(sub_levels + 1, tile_levels + 1):
                        big = jnp.where(
                            coarse == num - sub_levels,
                            spread_rows(weight_rows[num], tile // sub),
                            big,
                        )
                    big = jnp.concatenate(
                        [spread_rows(big[row : row + 1], sub) for row in range(tile // sub)], axis=0
                    )
                    weight = jnp.where(near_diag, jnp.concatenate([small] * (tile // sub), 0), big)
                else:
                    num = tile_levels + (s0 // tile ^ t0 // tile).bit_length()
                    weight = spread_rows(weight_rows[num], tile)
                score = score_ref[s0 : s0 + tile, t0 : t0 + tile].astype(F32)
                near_ref[place_at] = (weight * score).astype(BF16)
        return carry

    lax.fori_loop(0, heads, one_head, 0)


def prepare(queries, key_vectors, level_weight):
    length = queries.shape[0]
    heads = level_weight.shape[1]
    rows = min(256, length)
    return pl.pallas_call(
        prepare_kernel,
        in_specs=[pl.BlockSpec(memory_space=pltpu.HBM)] * 3,
        out_shape=[
            pltpu.VMEM((heads, length, rows), BF16),
            pltpu.VMEM((length, length), BF16),
        ],
        scratch_shapes=[
            pltpu.VMEM((heads, rows.bit_length(), length), F32),
            pltpu.VMEM(queries.shape, queries.dtype),
            pltpu.VMEM(key_vectors.shape, key_vectors.dtype),
            pltpu.VMEM(level_weight.shape, level_weight.dtype),
            pltpu.SemaphoreType.DMA((3,)),
        ],
        compiler_params=pltpu.CompilerParams(vmem_limit_bytes=16 << 20),
        name="prepare",
    )(*off_chip(queries, key_vectors, level_weight))


def begin_kernel(k_hbm, token_hbm, weight_hbm, sum_ref, sent_ref, held_ref, *rest):
    part_refs, (k_ref, weight_ref, sems) = rest[:-3], rest[-3:]
    loads = [
        pltpu.make_async_copy(source, target, sems.at[num])
        for num, (source, target) in enumerate(
            [(k_hbm, k_ref), (token_hbm, held_ref), (weight_hbm, weight_ref)]
        )
    ]
    for load in loads:
        load.start()
    loads[0].wait()
    loads[1].wait()
    total = lax.dot_general(
        k_ref[...], held_ref[...], (((0,), (0,)), ((), ())), preferred_element_type=F32
    )
    sum_ref[...] = total
    sent_ref[...] = total.astype(BF16)
    loads[2].wait()
    share = part_refs[0].shape[0]
    for num, part_ref in enumerate(part_refs):
        part_ref[...] = weight_ref[:, num * share : (num + 1) * share].T


def begin(key_vectors, tokens, weight, split):
    depth, width = weight.shape
    shape = (key_vectors.shape[1], tokens.shape[1])
    return pl.pallas_call(
        begin_kernel,
        in_specs=[pl.BlockSpec(memory_space=pltpu.HBM)] * 3,
        out_shape=[
            pltpu.VMEM(shape, F32),
            pltpu.VMEM(shape, BF16),
            pltpu.VMEM(tokens.shape, tokens.dtype),
        ]
        + [pltpu.VMEM((width // split, depth), weight.dtype)] * split,
        scratch_shapes=[
            pltpu.VMEM(key_vectors.shape, key_vectors.dtype),
            pltpu.VMEM(weight.shape, weight.dtype),
            pltpu.SemaphoreType.DMA((3,)),
        ],
        compiler_params=pltpu.CompilerParams(vmem_limit_bytes=8 << 20),
        name="begin",
    )(*off_chip(key_vectors, tokens, weight))


def ring_order(count):
    return list(range(0, count, 2)) + list(range(1, count, 2))[::-1]


def place(offset, depth, piece_width):
    count = lax.axis_size("ctx")
    mine = lax.axis_index("ctx")
    pos = jnp.where(mine % 2 == 0, mine // 2, count - 1 - mine // 2)
    pos = (pos + offset + count) % count
    index = jnp.where(pos < count // 2, 2 * pos, 2 * (count - 1 - pos) + 1)
    per_piece = piece_width // depth
    return jnp.bitwise_xor(index // per_piece, lax.axis_index("head")), index % per_piece * depth


def choose(offsets, pieces, depth, chosen_ref):
    for num, offset in enumerate(offsets):
        piece, start = place(offset, depth, pieces[0].shape[1])
        start = pl.multiple_of(start, 128)
        for index, ref in enumerate(pieces):

            @pl.when(piece == index)
            def _():
                chosen_ref[:, num * depth : (num + 1) * depth] = ref[:, pl.ds(start, depth)]


def extend_kernel(piece_count, offsets, split, started, *refs):
    count = len(offsets)
    pieces = refs[:piece_count]
    blocks = [refs[piece_count + num * split :][:split] for num in range(count)]
    out_ref, chosen_ref = refs[-2], refs[-1]
    share, depth = blocks[0][0].shape
    choose(offsets, pieces, depth, chosen_ref)
    width = out_ref.shape[0]
    step = min(256, share)
    for c0 in range(0, width, step):
        at = c0 % share
        left = jnp.concatenate(
            [block[c0 // share][at : at + step, :] for block in blocks], axis=1
        )
        total = dot_last(left, chosen_ref[...])
        if started:
            total = total + refs[piece_count + count * split][c0 : c0 + step, :]
        out_ref[c0 : c0 + step, :] = total


def extend(total, pieces, parts):
    offsets = tuple(offset for offset, _ in parts)
    blocks = [half for _, block in parts for half in block]
    split = len(parts[0][1])
    rows = pieces[0].shape[0]
    share, depth = blocks[0].shape
    arrays = [*pieces, *blocks, *([] if total is None else [total])]
    return pl.pallas_call(
        functools.partial(
            extend_kernel, len(pieces), offsets, split, total is not None
        ),
        in_specs=[pl.BlockSpec(memory_space=pltpu.VMEM)] * len(arrays),
        out_shape=pltpu.VMEM((share * split, rows), F32),
        scratch_shapes=[pltpu.VMEM((rows, depth * len(parts)), BF16)],
        compiler_params=pltpu.CompilerParams(vmem_limit_bytes=12 << 20),
    )(*arrays)


def finish_kernel(piece_count, groups, offset, last_count, head_size, *refs):
    refs = list(refs)
    take = lambda count: [refs.pop(0) for _ in range(count)]
    token_refs, sum_refs = take(piece_count), [take(piece_count) for _ in range(groups)]
    last_refs = take(last_count)
    value_ref, state_refs = refs.pop(0), take(groups)
    q_ref, w_ref, near_ref, score_ref, out_ref = take(5)
    length, state_rows = q_ref.shape
    width = value_ref.shape[0]
    near_levels = length.bit_length()
    far_levels = w_ref.shape[0] - near_levels
    rows = near_ref.shape[2]
    if last_count:
        token_chosen, *sum_chosen = refs
        depth = token_chosen.shape[1]
        choose([offset], token_refs, depth, token_chosen)
        for pieces, chosen in zip(sum_refs, sum_chosen):
            choose([offset], pieces, depth, chosen)
    mine = lax.axis_index("ctx")
    queries = q_ref[...]
    twice = jnp.concatenate([queries, queries], axis=1)
    step = min(256, width)
    unit = (
        lax.broadcasted_iota(jnp.int32, (rows, rows), 0)
        == lax.broadcasted_iota(jnp.int32, (rows, rows), 1)
    ).astype(BF16)
    for c0 in range(0, width, step):
        values = value_ref[c0 : c0 + step, :]
        states = [ref[c0 : c0 + step, :] for ref in state_refs]
        if last_count:
            share = width // last_count
            left = last_refs[c0 // share][c0 % share : c0 % share + step, :]
            values = values + dot_last(left, token_chosen[...])
            states = [
                part + dot_last(left, chosen[...]) for part, chosen in zip(states, sum_chosen)
            ]
        values = values.astype(BF16)
        heads = range(c0 // head_size, (c0 + step) // head_size)

        def weight(level, low, high):
            return jnp.concatenate(
                [
                    spread_rows(
                        w_ref[level, head : head + 1, low:high] * level_scale(level), head_size
                    )
                    for head in heads
                ],
                axis=0,
            )

        far = None
        states = jnp.concatenate(states, axis=1)
        for num in range(far_levels):
            state = states[:, num * state_rows : (num + 1) * state_rows]
            state = jnp.where(jnp.right_shift(mine, num) % 2 == 1, state, jnp.zeros_like(state))
            high = state.astype(BF16)
            low = (state - high.astype(F32)).astype(BF16)
            reading = dot_last(jnp.concatenate([high, low], axis=1), twice)
            reading = weight(near_levels + num, 0, length) * reading
            far = reading if far is None else far + reading
        for t0 in range(0, length, rows):
            total = far[:, t0 : t0 + rows] + jnp.concatenate(
                [
                    jnp.dot(
                        values[head * head_size - c0 : (head + 1) * head_size - c0, t0 : t0 + rows],
                        near_ref[head, t0 : t0 + rows, :],
                        preferred_element_type=F32,
                    )
                    for head in heads
                ],
                axis=0,
            )
            for level in range(rows.bit_length(), near_levels):
                span = 1 << level - 1
                if t0 & span:
                    s0 = t0 // span * span - span
                    mixed = jnp.dot(
                        values[:, s0 : s0 + span],
                        score_ref[s0 : s0 + span, t0 : t0 + rows],
                        preferred_element_type=F32,
                    )
                    total = total + weight(level, t0, t0 + rows) * mixed
            out_ref[t0 : t0 + rows, c0 : c0 + step] = dot_last(unit, total.astype(BF16)).astype(
                BF16
            )


def finish(values, states, offset, last, token_pieces, sum_pieces, queries, level_weight, near, head_size):
    width, length = values.shape
    flat_sums = [piece for pieces in sum_pieces for piece in pieces]
    arrays = [*token_pieces, *flat_sums, *last, values, *states, queries, level_weight, *near]
    scratch = []
    if last:
        depth = last[0].shape[1]
        scratch = [pltpu.VMEM((rows, depth), BF16) for rows in [length, *(s.shape[1] for s in states)]]
    return pl.pallas_call(
        functools.partial(
            finish_kernel, len(token_pieces), len(states), offset, len(last), head_size
        ),
        in_specs=[pl.BlockSpec(memory_space=pltpu.VMEM)] * len(arrays),
        out_shape=jax.ShapeDtypeStruct((length, width), BF16),
        scratch_shapes=scratch,
        compiler_params=pltpu.CompilerParams(vmem_limit_bytes=24 << 20),
        name="finish",
    )(*arrays)


def body(tokens, value_weight, queries, key_vectors, level_weight):
    _, width_feat = tokens.shape
    depth, width_local = value_weight.shape
    head_local = level_weight.shape[1]
    head_size = width_local // head_local
    ctx_count = lax.axis_size("ctx")
    dev_bits = ctx_count.bit_length() - 1
    near = prepare(queries, key_vectors, level_weight)

    running, sent, held, *turned = begin(key_vectors, tokens, value_weight, 2)
    level_sums = []
    for section_bit in range(dev_bits):
        if section_bit > 0:
            sent = running.astype(BF16)
        if section_bit == dev_bits - 1 and dev_bits > 1:
            break
        partner = from_partner(sent, "ctx", section_bit)
        level_sums.append(partner)
        running = running + partner.astype(F32)
    if dev_bits > 1:
        unit = ctx_count // 4
        for hop in range(2):
            route = [((1 + hop) * unit + num, (2 + hop) * unit + num) for num in range(unit)]
            sent = lax.ppermute(sent, "ctx", route)
            top = sent if hop == 0 else top + sent
        level_sums.append(top)
    low_sums = jnp.concatenate(level_sums[:-1] or level_sums, axis=0)
    top_sums = level_sums[-1:] if dev_bits > 1 else []

    if depth % 256 or width_feat % depth:
        features = lax.all_gather(tokens, "head", axis=1, tiled=True)
        level_sums = jnp.concatenate([low_sums, *top_sums], axis=0)
        sums = lax.all_gather(level_sums, "head", axis=1, tiled=True)
        weight = lax.all_gather(value_weight, "ctx", axis=0, tiled=True)
        values = jnp.einsum("fc,tf->ct", weight, features, preferred_element_type=F32)
        states = jnp.einsum("fc,nf->cn", weight, sums, preferred_element_type=F32)
        return finish(values, [states], 0, [], [], [[]], queries, level_weight, near, head_size)

    order = ring_order(ctx_count)
    ahead = [(order[i], order[(i + 1) % ctx_count]) for i in range(ctx_count)]
    back = [(b, a) for a, b in ahead]
    half_count = ctx_count // 2
    token_pieces = on_chip(*gather_pieces(held, "head"))
    sum_pieces = [on_chip(*gather_pieces(low_sums, "head"))]
    sum_pieces += [on_chip(*gather_pieces(sums, "head")) for sums in top_sums]
    cw = ccw = tuple(turned)
    steps = [[(0, cw)]]

    def move(part, route):
        return lax.ppermute(part, "ctx", route)

    for step in range(1, half_count):
        cw = tuple(move(part, ahead) for part in cw)
        ccw = tuple(move(part, back) for part in ccw)
        steps.append([(-step, on_chip(*cw)), (step, on_chip(*ccw))])
    last = on_chip(move(cw[0], ahead), move(ccw[1], back))
    values = extend(None, token_pieces, steps[0] + steps[1])
    for step in range(2, half_count):
        values = extend(values, token_pieces, steps[step])
    every = [part for parts in steps for part in parts]
    states = [extend(None, pieces, every) for pieces in sum_pieces]
    return finish(
        values,
        states,
        half_count,
        last,
        token_pieces,
        sum_pieces,
        queries,
        level_weight,
        near,
        head_size,
    )


def solution(mesh):
    return jax.shard_map(
        body,
        mesh=mesh,
        in_specs=(
            P("ctx", "head"),
            P("ctx", "head"),
            P("ctx", None),
            P("ctx", None),
            P(None, "head", "ctx"),
        ),
        out_specs=P("ctx", "head"),
        check_vma=False,
    )
```

```python
import functools

import jax
import jax.numpy as jnp
from jax import lax
from jax.experimental import pallas as pl
from jax.experimental.pallas import tpu as pltpu
from jax.sharding import PartitionSpec as P


F32 = jnp.float32
BF16 = jnp.bfloat16


def from_partner(block, axis, distance):
    count = lax.axis_size(axis)
    route = []
    for low in range(count):
        high = low | 1 << distance
        if high != low and high < count:
            route += [(low, high), (high, low)]
    return lax.ppermute(block, axis, route)


def gather_pieces(block, axis):
    pieces = [block]
    masks = [0]
    for bit in reversed(range(lax.axis_size(axis).bit_length() - 1)):
        for mask, piece in zip(list(masks), list(pieces)):
            pieces.append(from_partner(piece, axis, bit))
            masks.append(mask | 1 << bit)
    return [piece for _, piece in sorted(zip(masks, pieces), key=lambda pair: pair[0])]


def level_scale(level_num):
    return 1.0 if level_num == 0 else 2.0 ** (-(level_num - 1) / 2.0)


def on_chip(*arrays):
    return [pltpu.with_memory_space_constraint(array, pltpu.VMEM) for array in arrays]


def off_chip(*arrays):
    return [pltpu.with_memory_space_constraint(array, pltpu.HBM) for array in arrays]


def dot_last(left, right):
    return lax.dot_general(left, right, (((1,), (1,)), ((), ())), preferred_element_type=F32)


def spread_rows(row, count):
    return jnp.broadcast_to(row, (count, row.shape[1]))


def prepare_kernel(q_hbm, k_hbm, w_hbm, near_ref, score_ref, row_ref, q_ref, k_ref, w_ref, sems):
    loads = [
        pltpu.make_async_copy(source, target, sems.at[num])
        for num, (source, target) in enumerate([(q_hbm, q_ref), (k_hbm, k_ref), (w_hbm, w_ref)])
    ]
    for load in loads:
        load.start()
    for load in loads:
        load.wait()
    length = q_ref.shape[0]
    heads, _, rows = near_ref.shape
    tile = min(128, length)
    sub = 8
    tile_levels = tile.bit_length() - 1
    sub_levels = sub.bit_length() - 1
    score_ref[...] = dot_last(k_ref[...], q_ref[...]).astype(BF16)
    for num in range(rows.bit_length()):
        for head in range(heads):
            row_ref[head, num : num + 1, :] = w_ref[num, head : head + 1, :] * level_scale(num)

    def grid_level(shape, shift):
        s_pos = lax.broadcasted_iota(jnp.int32, shape, 0)
        t_pos = jnp.right_shift(lax.broadcasted_iota(jnp.int32, shape, 1), shift)
        if shift == 0:
            t_pos = jnp.bitwise_and(t_pos, sub - 1)
        differ = jnp.bitwise_xor(s_pos, t_pos)
        level = jnp.zeros(shape, jnp.int32)
        for bit in range(tile_levels):
            level = level + (jnp.right_shift(differ, bit) > 0).astype(jnp.int32)
        return jnp.where(s_pos <= t_pos, level, -1)

    fine = grid_level((sub, tile), 0)
    coarse = grid_level((tile // sub, tile), sub_levels)
    near_diag = lax.broadcasted_iota(jnp.int32, (tile, tile), 0) // sub == (
        lax.broadcasted_iota(jnp.int32, (tile, tile), 1) // sub
    )

    def one_head(head, carry):
        for t0 in range(0, length, tile):
            base = t0 // rows * rows
            weight_rows = [
                row_ref[head, num : num + 1, t0 : t0 + tile] for num in range(rows.bit_length())
            ]
            for s0 in range(base, base + rows, tile):
                place_at = (head, pl.ds(s0, tile), pl.ds(t0 - base, tile))
                if s0 > t0:
                    near_ref[place_at] = jnp.zeros((tile, tile), BF16)
                    continue
                if s0 == t0:
                    small = jnp.zeros((sub, tile), F32)
                    for num in range(sub_levels + 1):
                        small = jnp.where(fine == num, spread_rows(weight_rows[num], sub), small)
                    big = jnp.zeros((tile // sub, tile), F32)
                    for num in range(sub_levels + 1, tile_levels + 1):
                        big = jnp.where(
                            coarse == num - sub_levels,
                            spread_rows(weight_rows[num], tile // sub),
                            big,
                        )
                    big = jnp.concatenate(
                        [spread_rows(big[row : row + 1], sub) for row in range(tile // sub)], axis=0
                    )
                    weight = jnp.where(near_diag, jnp.concatenate([small] * (tile // sub), 0), big)
                else:
                    num = tile_levels + (s0 // tile ^ t0 // tile).bit_length()
                    weight = spread_rows(weight_rows[num], tile)
                score = score_ref[s0 : s0 + tile, t0 : t0 + tile].astype(F32)
                near_ref[place_at] = (weight * score).astype(BF16)
        return carry

    lax.fori_loop(0, heads, one_head, 0)


def prepare(queries, key_vectors, level_weight):
    length = queries.shape[0]
    heads = level_weight.shape[1]
    rows = min(256, length)
    return pl.pallas_call(
        prepare_kernel,
        in_specs=[pl.BlockSpec(memory_space=pltpu.HBM)] * 3,
        out_shape=[
            pltpu.VMEM((heads, length, rows), BF16),
            pltpu.VMEM((length, length), BF16),
        ],
        scratch_shapes=[
            pltpu.VMEM((heads, rows.bit_length(), length), F32),
            pltpu.VMEM(queries.shape, queries.dtype),
            pltpu.VMEM(key_vectors.shape, key_vectors.dtype),
            pltpu.VMEM(level_weight.shape, level_weight.dtype),
            pltpu.SemaphoreType.DMA((3,)),
        ],
        compiler_params=pltpu.CompilerParams(vmem_limit_bytes=16 << 20),
        name="prepare",
    )(*off_chip(queries, key_vectors, level_weight))


def begin_kernel(k_hbm, token_hbm, weight_hbm, sum_ref, sent_ref, held_ref, *rest):
    part_refs, (k_ref, weight_ref, sems) = rest[:-3], rest[-3:]
    loads = [
        pltpu.make_async_copy(source, target, sems.at[num])
        for num, (source, target) in enumerate(
            [(k_hbm, k_ref), (token_hbm, held_ref), (weight_hbm, weight_ref)]
        )
    ]
    for load in loads:
        load.start()
    loads[0].wait()
    loads[1].wait()
    total = lax.dot_general(
        k_ref[...], held_ref[...], (((0,), (0,)), ((), ())), preferred_element_type=F32
    )
    sum_ref[...] = total
    sent_ref[...] = total.astype(BF16)
    loads[2].wait()
    share = part_refs[0].shape[0]
    for num, part_ref in enumerate(part_refs):
        part_ref[...] = weight_ref[:, num * share : (num + 1) * share].T


def begin(key_vectors, tokens, weight, split):
    depth, width = weight.shape
    shape = (key_vectors.shape[1], tokens.shape[1])
    return pl.pallas_call(
        begin_kernel,
        in_specs=[pl.BlockSpec(memory_space=pltpu.HBM)] * 3,
        out_shape=[
            pltpu.VMEM(shape, F32),
            pltpu.VMEM(shape, BF16),
            pltpu.VMEM(tokens.shape, tokens.dtype),
        ]
        + [pltpu.VMEM((width // split, depth), weight.dtype)] * split,
        scratch_shapes=[
            pltpu.VMEM(key_vectors.shape, key_vectors.dtype),
            pltpu.VMEM(weight.shape, weight.dtype),
            pltpu.SemaphoreType.DMA((3,)),
        ],
        compiler_params=pltpu.CompilerParams(vmem_limit_bytes=8 << 20),
        name="begin",
    )(*off_chip(key_vectors, tokens, weight))


def ring_order(count):
    return list(range(0, count, 2)) + list(range(1, count, 2))[::-1]


def place(offset, depth, piece_width):
    count = lax.axis_size("ctx")
    mine = lax.axis_index("ctx")
    pos = jnp.where(mine % 2 == 0, mine // 2, count - 1 - mine // 2)
    pos = (pos + offset + count) % count
    index = jnp.where(pos < count // 2, 2 * pos, 2 * (count - 1 - pos) + 1)
    per_piece = piece_width // depth
    return jnp.bitwise_xor(index // per_piece, lax.axis_index("head")), index % per_piece * depth


def choose(offsets, pieces, depth, chosen_ref):
    for num, offset in enumerate(offsets):
        piece, start = place(offset, depth, pieces[0].shape[1])
        start = pl.multiple_of(start, 128)
        for index, ref in enumerate(pieces):

            @pl.when(piece == index)
            def _():
                chosen_ref[:, num * depth : (num + 1) * depth] = ref[:, pl.ds(start, depth)]


def extend_kernel(sizes, offsets, split, started, *refs):
    refs = list(refs)
    take = lambda count: [refs.pop(0) for _ in range(count)]
    groups = [take(size) for size in sizes]
    blocks = [take(split) for _ in offsets]
    totals = take(len(sizes)) if started else []
    out_refs, chosen_refs = take(len(sizes)), refs
    share, depth = blocks[0][0].shape
    for pieces, chosen_ref in zip(groups, chosen_refs):
        choose(offsets, pieces, depth, chosen_ref)
    step = min(256, share)
    for c0 in range(0, share * split, step):
        at = c0 % share
        left = jnp.concatenate(
            [block[c0 // share][at : at + step, :] for block in blocks], axis=1
        )
        for num, (out_ref, chosen_ref) in enumerate(zip(out_refs, chosen_refs)):
            total = dot_last(left, chosen_ref[...])
            if started:
                total = total + totals[num][c0 : c0 + step, :]
            out_ref[c0 : c0 + step, :] = total


def extend(totals, groups, parts):
    offsets = tuple(offset for offset, _ in parts)
    blocks = [half for _, block in parts for half in block]
    split = len(parts[0][1])
    share, depth = blocks[0].shape
    arrays = [*(piece for pieces in groups for piece in pieces), *blocks, *totals]
    rows = [pieces[0].shape[0] for pieces in groups]
    return pl.pallas_call(
        functools.partial(
            extend_kernel, [len(pieces) for pieces in groups], offsets, split, len(totals) > 0
        ),
        in_specs=[pl.BlockSpec(memory_space=pltpu.VMEM)] * len(arrays),
        out_shape=[pltpu.VMEM((share * split, count), F32) for count in rows],
        scratch_shapes=[pltpu.VMEM((count, depth * len(parts)), BF16) for count in rows],
        compiler_params=pltpu.CompilerParams(vmem_limit_bytes=12 << 20),
    )(*arrays)


def finish_kernel(piece_count, groups, offset, last_count, head_size, *refs):
    refs = list(refs)
    take = lambda count: [refs.pop(0) for _ in range(count)]
    token_refs, sum_refs = take(piece_count), [take(piece_count) for _ in range(groups)]
    last_refs = take(last_count)
    value_ref, state_refs = refs.pop(0), take(groups)
    q_ref, w_ref, near_ref, score_ref, out_hbm = take(5)
    out_ref, sems = refs.pop(), refs.pop()
    length, state_rows = q_ref.shape
    width = value_ref.shape[0]
    near_levels = length.bit_length()
    far_levels = w_ref.shape[0] - near_levels
    rows = near_ref.shape[2]
    if last_count:
        token_chosen, *sum_chosen = refs
        depth = token_chosen.shape[1]
        choose([offset], token_refs, depth, token_chosen)
        for pieces, chosen in zip(sum_refs, sum_chosen):
            choose([offset], pieces, depth, chosen)
    mine = lax.axis_index("ctx")
    queries = q_ref[...]
    twice = jnp.concatenate([queries, queries], axis=1)
    step = min(256, width)
    stores = []
    for c0 in range(0, width, step):
        values = value_ref[c0 : c0 + step, :]
        states = [ref[c0 : c0 + step, :] for ref in state_refs]
        if last_count:
            share = width // last_count
            left = last_refs[c0 // share][c0 % share : c0 % share + step, :]
            values = values + dot_last(left, token_chosen[...])
            states = [
                part + dot_last(left, chosen[...]) for part, chosen in zip(states, sum_chosen)
            ]
        values = values.astype(BF16)
        heads = range(c0 // head_size, (c0 + step) // head_size)

        def weight(level, low, high):
            return jnp.concatenate(
                [
                    spread_rows(
                        w_ref[level, head : head + 1, low:high] * level_scale(level), head_size
                    )
                    for head in heads
                ],
                axis=0,
            )

        far = None
        states = jnp.concatenate(states, axis=1)
        for num in range(far_levels):
            state = states[:, num * state_rows : (num + 1) * state_rows]
            state = jnp.where(jnp.right_shift(mine, num) % 2 == 1, state, jnp.zeros_like(state))
            high = state.astype(BF16)
            low = (state - high.astype(F32)).astype(BF16)
            reading = dot_last(jnp.concatenate([high, low], axis=1), twice)
            reading = weight(near_levels + num, 0, length) * reading
            far = reading if far is None else far + reading
        for t0 in range(0, length, rows):
            total = far[:, t0 : t0 + rows] + jnp.concatenate(
                [
                    jnp.dot(
                        values[head * head_size - c0 : (head + 1) * head_size - c0, t0 : t0 + rows],
                        near_ref[head, t0 : t0 + rows, :],
                        preferred_element_type=F32,
                    )
                    for head in heads
                ],
                axis=0,
            )
            for level in range(rows.bit_length(), near_levels):
                span = 1 << level - 1
                if t0 & span:
                    s0 = t0 // span * span - span
                    mixed = jnp.dot(
                        values[:, s0 : s0 + span],
                        score_ref[s0 : s0 + span, t0 : t0 + rows],
                        preferred_element_type=F32,
                    )
                    total = total + weight(level, t0, t0 + rows) * mixed
            out_ref[t0 : t0 + rows, c0 : c0 + step] = total.astype(BF16).T
        stores.append(
            pltpu.make_async_copy(
                out_ref.at[:, c0 : c0 + step], out_hbm.at[:, c0 : c0 + step], sems.at[len(stores)]
            )
        )
        stores[-1].start()
    for store in stores:
        store.wait()


def finish(values, states, offset, last, token_pieces, sum_pieces, queries, level_weight, near, head_size):
    width, length = values.shape
    flat_sums = [piece for pieces in sum_pieces for piece in pieces]
    arrays = [*token_pieces, *flat_sums, *last, values, *states, queries, level_weight, *near]
    scratch = []
    if last:
        depth = last[0].shape[1]
        scratch = [pltpu.VMEM((rows, depth), BF16) for rows in [length, *(s.shape[1] for s in states)]]
    scratch += [
        pltpu.SemaphoreType.DMA((max(1, width // 256),)),
        pltpu.VMEM((length, width), BF16),
    ]
    return pl.pallas_call(
        functools.partial(
            finish_kernel, len(token_pieces), len(states), offset, len(last), head_size
        ),
        in_specs=[pl.BlockSpec(memory_space=pltpu.VMEM)] * len(arrays),
        out_shape=jax.ShapeDtypeStruct((length, width), BF16),
        out_specs=pl.BlockSpec(memory_space=pltpu.HBM),
        scratch_shapes=scratch,
        compiler_params=pltpu.CompilerParams(vmem_limit_bytes=24 << 20),
        name="finish",
    )(*arrays)


def body(tokens, value_weight, queries, key_vectors, level_weight):
    _, width_feat = tokens.shape
    depth, width_local = value_weight.shape
    head_local = level_weight.shape[1]
    head_size = width_local // head_local
    ctx_count = lax.axis_size("ctx")
    dev_bits = ctx_count.bit_length() - 1
    near = prepare(queries, key_vectors, level_weight)

    running, sent, held, *turned = begin(key_vectors, tokens, value_weight, 2)
    level_sums = []
    for section_bit in range(dev_bits):
        if section_bit > 0:
            sent = running.astype(BF16)
        if section_bit == dev_bits - 1 and dev_bits > 1:
            break
        partner = from_partner(sent, "ctx", section_bit)
        level_sums.append(partner)
        running = running + partner.astype(F32)
    if dev_bits > 1:
        unit = ctx_count // 4
        for hop in range(2):
            route = [((1 + hop) * unit + num, (2 + hop) * unit + num) for num in range(unit)]
            sent = lax.ppermute(sent, "ctx", route)
            top = sent if hop == 0 else top + sent
        level_sums.append(top)
    low_sums = jnp.concatenate(level_sums[:-1] or level_sums, axis=0)
    top_sums = level_sums[-1:] if dev_bits > 1 else []

    if depth % 256 or width_feat % depth:
        features = lax.all_gather(tokens, "head", axis=1, tiled=True)
        level_sums = jnp.concatenate([low_sums, *top_sums], axis=0)
        sums = lax.all_gather(level_sums, "head", axis=1, tiled=True)
        weight = lax.all_gather(value_weight, "ctx", axis=0, tiled=True)
        values = jnp.einsum("fc,tf->ct", weight, features, preferred_element_type=F32)
        states = jnp.einsum("fc,nf->cn", weight, sums, preferred_element_type=F32)
        return finish(values, [states], 0, [], [], [[]], queries, level_weight, near, head_size)

    order = ring_order(ctx_count)
    ahead = [(order[i], order[(i + 1) % ctx_count]) for i in range(ctx_count)]
    back = [(b, a) for a, b in ahead]
    half_count = ctx_count // 2
    token_pieces = on_chip(*gather_pieces(held, "head"))
    sum_pieces = [on_chip(*gather_pieces(low_sums, "head"))]
    sum_pieces += [on_chip(*gather_pieces(sums, "head")) for sums in top_sums]
    cw = ccw = tuple(turned)
    steps = [[(0, cw)]]

    def move(part, route):
        return lax.ppermute(part, "ctx", route)

    for step in range(1, half_count):
        cw = tuple(move(part, ahead) for part in cw)
        ccw = tuple(move(part, back) for part in ccw)
        steps.append([(-step, on_chip(*cw)), (step, on_chip(*ccw))])
    last = on_chip(move(cw[0], ahead), move(ccw[1], back))
    values = extend([], [token_pieces], steps[0] + steps[1])
    for step in range(2, half_count - 1):
        values = extend(values, [token_pieces], steps[step])
    early = [part for parts in steps[:-1] for part in parts]
    low = extend([], sum_pieces[:1], early)
    values, low = extend([*values, *low], [token_pieces, sum_pieces[0]], steps[-1])
    top = [extend([], [pieces], early + steps[-1])[0] for pieces in sum_pieces[1:]]
    states = [low, *top]
    return finish(
        values,
        states,
        half_count,
        last,
        token_pieces,
        sum_pieces,
        queries,
        level_weight,
        near,
        head_size,
    )


def solution(mesh):
    return jax.shard_map(
        body,
        mesh=mesh,
        in_specs=(
            P("ctx", "head"),
            P("ctx", "head"),
            P("ctx", None),
            P("ctx", None),
            P(None, "head", "ctx"),
        ),
        out_specs=P("ctx", "head"),
        check_vma=False,
    )
```

```python
import functools

import jax
import jax.numpy as jnp
from jax import lax
from jax.experimental import pallas as pl
from jax.experimental.pallas import tpu as pltpu
from jax.sharding import PartitionSpec as P


F32 = jnp.float32
BF16 = jnp.bfloat16


def from_partner(block, axis, distance):
    count = lax.axis_size(axis)
    route = []
    for low in range(count):
        high = low | 1 << distance
        if high != low and high < count:
            route += [(low, high), (high, low)]
    return lax.ppermute(block, axis, route)


def gather_pieces(block, axis):
    pieces = [block]
    masks = [0]
    for bit in reversed(range(lax.axis_size(axis).bit_length() - 1)):
        for mask, piece in zip(list(masks), list(pieces)):
            pieces.append(from_partner(piece, axis, bit))
            masks.append(mask | 1 << bit)
    return [piece for _, piece in sorted(zip(masks, pieces), key=lambda pair: pair[0])]


def level_scale(level_num):
    return 1.0 if level_num == 0 else 2.0 ** (-(level_num - 1) / 2.0)


def on_chip(*arrays):
    return [pltpu.with_memory_space_constraint(array, pltpu.VMEM) for array in arrays]


def off_chip(*arrays):
    return [pltpu.with_memory_space_constraint(array, pltpu.HBM) for array in arrays]


def dot_last(left, right):
    return lax.dot_general(left, right, (((1,), (1,)), ((), ())), preferred_element_type=F32)


def spread_rows(row, count):
    return jnp.broadcast_to(row, (count, row.shape[1]))


def prepare_kernel(q_hbm, k_hbm, w_hbm, near_ref, score_ref, row_ref, q_ref, k_ref, w_ref, sems):
    loads = [
        pltpu.make_async_copy(source, target, sems.at[num])
        for num, (source, target) in enumerate([(q_hbm, q_ref), (k_hbm, k_ref), (w_hbm, w_ref)])
    ]
    for load in loads:
        load.start()
    for load in loads:
        load.wait()
    length = q_ref.shape[0]
    heads, _, rows = near_ref.shape
    tile = min(128, length)
    sub = 8
    tile_levels = tile.bit_length() - 1
    sub_levels = sub.bit_length() - 1
    score_ref[...] = dot_last(k_ref[...], q_ref[...]).astype(BF16)
    for num in range(rows.bit_length()):
        for head in range(heads):
            row_ref[head, num : num + 1, :] = w_ref[num, head : head + 1, :] * level_scale(num)

    def grid_level(shape, shift):
        s_pos = lax.broadcasted_iota(jnp.int32, shape, 0)
        t_pos = jnp.right_shift(lax.broadcasted_iota(jnp.int32, shape, 1), shift)
        if shift == 0:
            t_pos = jnp.bitwise_and(t_pos, sub - 1)
        differ = jnp.bitwise_xor(s_pos, t_pos)
        level = jnp.zeros(shape, jnp.int32)
        for bit in range(tile_levels):
            level = level + (jnp.right_shift(differ, bit) > 0).astype(jnp.int32)
        return jnp.where(s_pos <= t_pos, level, -1)

    fine = grid_level((sub, tile), 0)
    coarse = grid_level((tile // sub, tile), sub_levels)
    near_diag = lax.broadcasted_iota(jnp.int32, (tile, tile), 0) // sub == (
        lax.broadcasted_iota(jnp.int32, (tile, tile), 1) // sub
    )

    def one_head(head, carry):
        for t0 in range(0, length, tile):
            base = t0 // rows * rows
            weight_rows = [
                row_ref[head, num : num + 1, t0 : t0 + tile] for num in range(rows.bit_length())
            ]
            for s0 in range(base, base + rows, tile):
                place_at = (head, pl.ds(s0, tile), pl.ds(t0 - base, tile))
                if s0 > t0:
                    near_ref[place_at] = jnp.zeros((tile, tile), BF16)
                    continue
                if s0 == t0:
                    small = jnp.zeros((sub, tile), F32)
                    for num in range(sub_levels + 1):
                        small = jnp.where(fine == num, spread_rows(weight_rows[num], sub), small)
                    big = jnp.zeros((tile // sub, tile), F32)
                    for num in range(sub_levels + 1, tile_levels + 1):
                        big = jnp.where(
                            coarse == num - sub_levels,
                            spread_rows(weight_rows[num], tile // sub),
                            big,
                        )
                    big = jnp.concatenate(
                        [spread_rows(big[row : row + 1], sub) for row in range(tile // sub)], axis=0
                    )
                    weight = jnp.where(near_diag, jnp.concatenate([small] * (tile // sub), 0), big)
                else:
                    num = tile_levels + (s0 // tile ^ t0 // tile).bit_length()
                    weight = spread_rows(weight_rows[num], tile)
                score = score_ref[s0 : s0 + tile, t0 : t0 + tile].astype(F32)
                near_ref[place_at] = (weight * score).astype(BF16)
        return carry

    lax.fori_loop(0, heads, one_head, 0)


def prepare(queries, key_vectors, level_weight):
    length = queries.shape[0]
    heads = level_weight.shape[1]
    rows = min(256, length)
    return pl.pallas_call(
        prepare_kernel,
        in_specs=[pl.BlockSpec(memory_space=pltpu.HBM)] * 3,
        out_shape=[
            pltpu.VMEM((heads, length, rows), BF16),
            pltpu.VMEM((length, length), BF16),
        ],
        scratch_shapes=[
            pltpu.VMEM((heads, rows.bit_length(), length), F32),
            pltpu.VMEM(queries.shape, queries.dtype),
            pltpu.VMEM(key_vectors.shape, key_vectors.dtype),
            pltpu.VMEM(level_weight.shape, level_weight.dtype),
            pltpu.SemaphoreType.DMA((3,)),
        ],
        compiler_params=pltpu.CompilerParams(vmem_limit_bytes=16 << 20),
        name="prepare",
    )(*off_chip(queries, key_vectors, level_weight))


def begin_kernel(k_hbm, token_hbm, weight_hbm, sum_ref, sent_ref, held_ref, *rest):
    part_refs, (k_ref, weight_ref, sems) = rest[:-3], rest[-3:]
    loads = [
        pltpu.make_async_copy(source, target, sems.at[num])
        for num, (source, target) in enumerate(
            [(k_hbm, k_ref), (token_hbm, held_ref), (weight_hbm, weight_ref)]
        )
    ]
    for load in loads:
        load.start()
    loads[0].wait()
    loads[1].wait()
    total = lax.dot_general(
        k_ref[...], held_ref[...], (((0,), (0,)), ((), ())), preferred_element_type=F32
    )
    sum_ref[...] = total
    sent_ref[...] = total.astype(BF16)
    loads[2].wait()
    share = part_refs[0].shape[0]
    for num, part_ref in enumerate(part_refs):
        part_ref[...] = weight_ref[:, num * share : (num + 1) * share].T


def begin(key_vectors, tokens, weight, split):
    depth, width = weight.shape
    shape = (key_vectors.shape[1], tokens.shape[1])
    return pl.pallas_call(
        begin_kernel,
        in_specs=[pl.BlockSpec(memory_space=pltpu.HBM)] * 3,
        out_shape=[
            pltpu.VMEM(shape, F32),
            pltpu.VMEM(shape, BF16),
            pltpu.VMEM(tokens.shape, tokens.dtype),
        ]
        + [pltpu.VMEM((width // split, depth), weight.dtype)] * split,
        scratch_shapes=[
            pltpu.VMEM(key_vectors.shape, key_vectors.dtype),
            pltpu.VMEM(weight.shape, weight.dtype),
            pltpu.SemaphoreType.DMA((3,)),
        ],
        compiler_params=pltpu.CompilerParams(vmem_limit_bytes=8 << 20),
        name="begin",
    )(*off_chip(key_vectors, tokens, weight))


def cut_kernel(count, *refs):
    for num in range(count):
        block_ref, parts = refs[num], refs[count + 2 * num :][:2]
        rows = parts[0].shape[0]
        parts[0][...] = block_ref[:rows, :]
        parts[1][...] = block_ref[rows:, :]


def cut(blocks):
    return pl.pallas_call(
        functools.partial(cut_kernel, len(blocks)),
        in_specs=[pl.BlockSpec(memory_space=pltpu.VMEM)] * len(blocks),
        out_shape=[
            pltpu.VMEM((block.shape[0] // 2, block.shape[1]), block.dtype)
            for block in blocks
            for _ in range(2)
        ],
        compiler_params=pltpu.CompilerParams(vmem_limit_bytes=4 << 20),
    )(*blocks)


def ring_order(count):
    return list(range(0, count, 2)) + list(range(1, count, 2))[::-1]


def place(offset, depth, piece_width):
    count = lax.axis_size("ctx")
    mine = lax.axis_index("ctx")
    pos = jnp.where(mine % 2 == 0, mine // 2, count - 1 - mine // 2)
    pos = (pos + offset + count) % count
    index = jnp.where(pos < count // 2, 2 * pos, 2 * (count - 1 - pos) + 1)
    per_piece = piece_width // depth
    return jnp.bitwise_xor(index // per_piece, lax.axis_index("head")), index % per_piece * depth


def choose(offsets, pieces, depth, chosen_ref):
    for num, offset in enumerate(offsets):
        piece, start = place(offset, depth, pieces[0].shape[1])
        start = pl.multiple_of(start, 128)
        for index, ref in enumerate(pieces):

            @pl.when(piece == index)
            def _():
                chosen_ref[:, num * depth : (num + 1) * depth] = ref[:, pl.ds(start, depth)]


def extend_kernel(sizes, offsets, split, started, *refs):
    refs = list(refs)
    take = lambda count: [refs.pop(0) for _ in range(count)]
    groups = [take(size) for size in sizes]
    blocks = [take(split) for _ in offsets]
    totals = take(len(sizes)) if started else []
    out_refs, chosen_refs = take(len(sizes)), refs
    share, depth = blocks[0][0].shape
    for pieces, chosen_ref in zip(groups, chosen_refs):
        choose(offsets, pieces, depth, chosen_ref)
    step = min(256, share)
    for c0 in range(0, share * split, step):
        at = c0 % share
        left = jnp.concatenate(
            [block[c0 // share][at : at + step, :] for block in blocks], axis=1
        )
        for num, (out_ref, chosen_ref) in enumerate(zip(out_refs, chosen_refs)):
            total = dot_last(left, chosen_ref[...])
            if started:
                total = total + totals[num][c0 : c0 + step, :]
            out_ref[c0 : c0 + step, :] = total


def extend(totals, groups, parts):
    offsets = tuple(offset for offset, _ in parts)
    blocks = [half for _, block in parts for half in block]
    split = len(parts[0][1])
    share, depth = blocks[0].shape
    arrays = [*(piece for pieces in groups for piece in pieces), *blocks, *totals]
    rows = [pieces[0].shape[0] for pieces in groups]
    return pl.pallas_call(
        functools.partial(
            extend_kernel, [len(pieces) for pieces in groups], offsets, split, len(totals) > 0
        ),
        in_specs=[pl.BlockSpec(memory_space=pltpu.VMEM)] * len(arrays),
        out_shape=[pltpu.VMEM((share * split, count), F32) for count in rows],
        scratch_shapes=[pltpu.VMEM((count, depth * len(parts)), BF16) for count in rows],
        compiler_params=pltpu.CompilerParams(vmem_limit_bytes=12 << 20),
    )(*arrays)


def finish_kernel(piece_count, groups, offset, last_at, head_size, *refs):
    last_count = len(last_at)
    refs = list(refs)
    take = lambda count: [refs.pop(0) for _ in range(count)]
    token_refs, sum_refs = take(piece_count), [take(piece_count) for _ in range(groups)]
    last_refs = take(last_count)
    value_ref, state_refs = refs.pop(0), take(groups)
    q_ref, w_ref, near_ref, score_ref = take(4)
    out_ref, sems, out_hbm = refs.pop(), refs.pop(), refs.pop(-1 - (groups + 1) * (last_count > 0))
    refs = refs[len(refs) - (groups + 1) * (last_count > 0) :]
    length, state_rows = q_ref.shape
    width = value_ref.shape[0]
    near_levels = length.bit_length()
    far_levels = w_ref.shape[0] - near_levels
    rows = near_ref.shape[2]
    if last_count:
        token_chosen, *sum_chosen = refs
        depth = token_chosen.shape[1]
        choose([offset], token_refs, depth, token_chosen)
        for pieces, chosen in zip(sum_refs, sum_chosen):
            choose([offset], pieces, depth, chosen)
    mine = lax.axis_index("ctx")
    queries = q_ref[...]
    twice = jnp.concatenate([queries, queries], axis=1)
    step = min(256, width)
    stores = []
    columns = [(c0, None) for c0 in range(0, width, step)]
    if last_count:
        columns = [
            (start + c0, ref.at[c0 : c0 + step, :])
            for start, ref in zip(last_at, last_refs)
            for c0 in range(0, ref.shape[0], step)
        ]
    for c0, last_ref in columns:
        values = value_ref[c0 : c0 + step, :]
        states = [ref[c0 : c0 + step, :] for ref in state_refs]
        if last_count:
            left = last_ref[...]
            values = values + dot_last(left, token_chosen[...])
            states = [
                part + dot_last(left, chosen[...]) for part, chosen in zip(states, sum_chosen)
            ]
        values = values.astype(BF16)
        heads = range(c0 // head_size, (c0 + step) // head_size)

        def weight(level, low, high):
            return jnp.concatenate(
                [
                    spread_rows(
                        w_ref[level, head : head + 1, low:high] * level_scale(level), head_size
                    )
                    for head in heads
                ],
                axis=0,
            )

        far = None
        states = jnp.concatenate(states, axis=1)
        for num in range(far_levels):
            state = states[:, num * state_rows : (num + 1) * state_rows]
            state = jnp.where(jnp.right_shift(mine, num) % 2 == 1, state, jnp.zeros_like(state))
            high = state.astype(BF16)
            low = (state - high.astype(F32)).astype(BF16)
            reading = dot_last(jnp.concatenate([high, low], axis=1), twice)
            reading = weight(near_levels + num, 0, length) * reading
            far = reading if far is None else far + reading
        for t0 in range(0, length, rows):
            total = far[:, t0 : t0 + rows] + jnp.concatenate(
                [
                    jnp.dot(
                        values[head * head_size - c0 : (head + 1) * head_size - c0, t0 : t0 + rows],
                        near_ref[head, t0 : t0 + rows, :],
                        preferred_element_type=F32,
                    )
                    for head in heads
                ],
                axis=0,
            )
            for level in range(rows.bit_length(), near_levels):
                span = 1 << level - 1
                if t0 & span:
                    s0 = t0 // span * span - span
                    mixed = jnp.dot(
                        values[:, s0 : s0 + span],
                        score_ref[s0 : s0 + span, t0 : t0 + rows],
                        preferred_element_type=F32,
                    )
                    total = total + weight(level, t0, t0 + rows) * mixed
            out_ref[t0 : t0 + rows, c0 : c0 + step] = total.astype(BF16).T
        stores.append(
            pltpu.make_async_copy(
                out_ref.at[:, c0 : c0 + step], out_hbm.at[:, c0 : c0 + step], sems.at[len(stores)]
            )
        )
        stores[-1].start()
    for store in stores:
        store.wait()


def finish(values, states, offset, last, token_pieces, sum_pieces, queries, level_weight, near, head_size, out):
    width, length = values.shape
    flat_sums = [piece for pieces in sum_pieces for piece in pieces]
    parts = [part for _, part in last]
    arrays = [*token_pieces, *flat_sums, *parts, values, *states, queries, level_weight, *near]
    in_specs = [pl.BlockSpec(memory_space=pltpu.VMEM)] * len(arrays)
    aliases = {}
    if out is not None:
        aliases = {len(arrays): 0}
        arrays.append(out)
        in_specs.append(pl.BlockSpec(memory_space=pltpu.HBM))
    scratch = []
    if last:
        depth = parts[0].shape[1]
        scratch = [pltpu.VMEM((rows, depth), BF16) for rows in [length, *(s.shape[1] for s in states)]]
    scratch += [
        pltpu.SemaphoreType.DMA((max(1, width // 256),)),
        pltpu.VMEM((length, width), BF16),
    ]
    return pl.pallas_call(
        functools.partial(
            finish_kernel,
            len(token_pieces),
            len(states),
            offset,
            [start for start, _ in last],
            head_size,
        ),
        in_specs=in_specs,
        out_shape=jax.ShapeDtypeStruct((length, width), BF16),
        out_specs=pl.BlockSpec(memory_space=pltpu.HBM),
        scratch_shapes=scratch,
        input_output_aliases=aliases,
        compiler_params=pltpu.CompilerParams(vmem_limit_bytes=24 << 20),
        name="finish",
    )(*arrays)


def body(tokens, value_weight, queries, key_vectors, level_weight):
    _, width_feat = tokens.shape
    depth, width_local = value_weight.shape
    head_local = level_weight.shape[1]
    head_size = width_local // head_local
    ctx_count = lax.axis_size("ctx")
    dev_bits = ctx_count.bit_length() - 1
    near = prepare(queries, key_vectors, level_weight)

    running, sent, held, *turned = begin(key_vectors, tokens, value_weight, 2)
    level_sums = []
    for section_bit in range(dev_bits):
        if section_bit > 0:
            sent = running.astype(BF16)
        if section_bit == dev_bits - 1 and dev_bits > 1:
            break
        partner = from_partner(sent, "ctx", section_bit)
        level_sums.append(partner)
        running = running + partner.astype(F32)
    if dev_bits > 1:
        unit = ctx_count // 4
        for hop in range(2):
            route = [((1 + hop) * unit + num, (2 + hop) * unit + num) for num in range(unit)]
            sent = lax.ppermute(sent, "ctx", route)
            top = sent if hop == 0 else top + sent
        level_sums.append(top)
    low_sums = jnp.concatenate(level_sums[:-1] or level_sums, axis=0)
    top_sums = level_sums[-1:] if dev_bits > 1 else []

    if depth % 256 or width_feat % depth:
        features = lax.all_gather(tokens, "head", axis=1, tiled=True)
        level_sums = jnp.concatenate([low_sums, *top_sums], axis=0)
        sums = lax.all_gather(level_sums, "head", axis=1, tiled=True)
        weight = lax.all_gather(value_weight, "ctx", axis=0, tiled=True)
        values = jnp.einsum("fc,tf->ct", weight, features, preferred_element_type=F32)
        states = jnp.einsum("fc,nf->cn", weight, sums, preferred_element_type=F32)
        return finish(
            values, [states], 0, [], [], [[]], queries, level_weight, near, head_size, None
        )

    order = ring_order(ctx_count)
    ahead = [(order[i], order[(i + 1) % ctx_count]) for i in range(ctx_count)]
    back = [(b, a) for a, b in ahead]
    half_count = ctx_count // 2
    token_pieces = on_chip(*gather_pieces(held, "head"))
    sum_pieces = [on_chip(*gather_pieces(low_sums, "head"))]
    sum_pieces += [on_chip(*gather_pieces(sums, "head")) for sums in top_sums]
    cw = ccw = tuple(turned)
    steps = [[(0, cw)]]

    def move(part, route):
        return lax.ppermute(part, "ctx", route)

    for step in range(1, half_count):
        cw = tuple(move(part, ahead) for part in cw)
        ccw = tuple(move(part, back) for part in ccw)
        steps.append([(-step, on_chip(*cw)), (step, on_chip(*ccw))])
    share = width_local // 4
    parts = [*cut([cw[0]]), *cut([ccw[1]])]
    last = [
        [(num * share, move(parts[num], ahead)), ((2 + num) * share, move(parts[2 + num], back))]
        for num in range(2)
    ]
    values = extend([], [token_pieces], steps[0] + steps[1])
    for step in range(2, half_count - 1):
        values = extend(values, [token_pieces], steps[step])
    early = [part for parts in steps[:-1] for part in parts]
    low = extend([], sum_pieces[:1], early)
    values, low = extend([*values, *low], [token_pieces, sum_pieces[0]], steps[-1])
    top = [extend([], [pieces], early + steps[-1])[0] for pieces in sum_pieces[1:]]
    states = [low, *top]
    out = None
    for parts in last:
        starts = [start for start, _ in parts]
        parts = list(zip(starts, on_chip(*(part for _, part in parts))))
        out = finish(
            values,
            states,
            half_count,
            parts,
            token_pieces,
            sum_pieces,
            queries,
            level_weight,
            near,
            head_size,
            out,
        )
    return out


def solution(mesh):
    return jax.shard_map(
        body,
        mesh=mesh,
        in_specs=(
            P("ctx", "head"),
            P("ctx", "head"),
            P("ctx", None),
            P("ctx", None),
            P(None, "head", "ctx"),
        ),
        out_specs=P("ctx", "head"),
        check_vma=False,
    )
```

```python
import functools

import jax
import jax.numpy as jnp
from jax import lax
from jax.experimental import pallas as pl
from jax.experimental.pallas import tpu as pltpu
from jax.sharding import PartitionSpec as P


F32 = jnp.float32
BF16 = jnp.bfloat16


def from_partner(block, axis, distance, both=True):
    count = lax.axis_size(axis)
    route = []
    for low in range(count):
        high = low | 1 << distance
        if high != low and high < count:
            route += [(low, high), (high, low)] if both else [(low, high)]
    return lax.ppermute(block, axis, route)


def gather_pieces(block, axis):
    pieces = [block]
    masks = [0]
    for bit in reversed(range(lax.axis_size(axis).bit_length() - 1)):
        for mask, piece in zip(list(masks), list(pieces)):
            pieces.append(from_partner(piece, axis, bit))
            masks.append(mask | 1 << bit)
    return [piece for _, piece in sorted(zip(masks, pieces), key=lambda pair: pair[0])]


def level_scale(level_num):
    return 1.0 if level_num == 0 else 2.0 ** (-(level_num - 1) / 2.0)


def on_chip(*arrays):
    return [pltpu.with_memory_space_constraint(array, pltpu.VMEM) for array in arrays]


def off_chip(*arrays):
    return [pltpu.with_memory_space_constraint(array, pltpu.HBM) for array in arrays]


def dot_last(left, right):
    return lax.dot_general(left, right, (((1,), (1,)), ((), ())), preferred_element_type=F32)


def spread_rows(row, count):
    return jnp.broadcast_to(row, (count, row.shape[1]))


def prepare_kernel(q_hbm, k_hbm, w_hbm, near_ref, score_ref, row_ref, q_ref, k_ref, w_ref, sems):
    loads = [
        pltpu.make_async_copy(source, target, sems.at[num])
        for num, (source, target) in enumerate([(q_hbm, q_ref), (k_hbm, k_ref), (w_hbm, w_ref)])
    ]
    for load in loads:
        load.start()
    for load in loads:
        load.wait()
    length = q_ref.shape[0]
    heads, _, rows = near_ref.shape
    tile = min(128, length)
    sub = 8
    tile_levels = tile.bit_length() - 1
    sub_levels = sub.bit_length() - 1
    score_ref[...] = dot_last(k_ref[...], q_ref[...]).astype(BF16)
    for num in range(rows.bit_length()):
        for head in range(heads):
            row_ref[head, num : num + 1, :] = w_ref[num, head : head + 1, :] * level_scale(num)

    def grid_level(shape, shift):
        s_pos = lax.broadcasted_iota(jnp.int32, shape, 0)
        t_pos = jnp.right_shift(lax.broadcasted_iota(jnp.int32, shape, 1), shift)
        if shift == 0:
            t_pos = jnp.bitwise_and(t_pos, sub - 1)
        differ = jnp.bitwise_xor(s_pos, t_pos)
        level = jnp.zeros(shape, jnp.int32)
        for bit in range(tile_levels):
            level = level + (jnp.right_shift(differ, bit) > 0).astype(jnp.int32)
        return jnp.where(s_pos <= t_pos, level, -1)

    fine = grid_level((sub, tile), 0)
    coarse = grid_level((tile // sub, tile), sub_levels)
    near_diag = lax.broadcasted_iota(jnp.int32, (tile, tile), 0) // sub == (
        lax.broadcasted_iota(jnp.int32, (tile, tile), 1) // sub
    )

    def one_head(head, carry):
        for t0 in range(0, length, tile):
            base = t0 // rows * rows
            weight_rows = [
                row_ref[head, num : num + 1, t0 : t0 + tile] for num in range(rows.bit_length())
            ]
            for s0 in range(base, base + rows, tile):
                place_at = (head, pl.ds(s0, tile), pl.ds(t0 - base, tile))
                if s0 > t0:
                    near_ref[place_at] = jnp.zeros((tile, tile), BF16)
                    continue
                if s0 == t0:
                    small = jnp.zeros((sub, tile), F32)
                    for num in range(sub_levels + 1):
                        small = jnp.where(fine == num, spread_rows(weight_rows[num], sub), small)
                    big = jnp.zeros((tile // sub, tile), F32)
                    for num in range(sub_levels + 1, tile_levels + 1):
                        big = jnp.where(
                            coarse == num - sub_levels,
                            spread_rows(weight_rows[num], tile // sub),
                            big,
                        )
                    big = jnp.concatenate(
                        [spread_rows(big[row : row + 1], sub) for row in range(tile // sub)], axis=0
                    )
                    weight = jnp.where(near_diag, jnp.concatenate([small] * (tile // sub), 0), big)
                else:
                    num = tile_levels + (s0 // tile ^ t0 // tile).bit_length()
                    weight = spread_rows(weight_rows[num], tile)
                score = score_ref[s0 : s0 + tile, t0 : t0 + tile].astype(F32)
                near_ref[place_at] = (weight * score).astype(BF16)
        return carry

    lax.fori_loop(0, heads, one_head, 0)


def prepare(queries, key_vectors, level_weight):
    length = queries.shape[0]
    heads = level_weight.shape[1]
    rows = min(256, length)
    return pl.pallas_call(
        prepare_kernel,
        in_specs=[pl.BlockSpec(memory_space=pltpu.HBM)] * 3,
        out_shape=[
            pltpu.VMEM((heads, length, rows), BF16),
            pltpu.VMEM((length, length), BF16),
        ],
        scratch_shapes=[
            pltpu.VMEM((heads, rows.bit_length(), length), F32),
            pltpu.VMEM(queries.shape, queries.dtype),
            pltpu.VMEM(key_vectors.shape, key_vectors.dtype),
            pltpu.VMEM(level_weight.shape, level_weight.dtype),
            pltpu.SemaphoreType.DMA((3,)),
        ],
        compiler_params=pltpu.CompilerParams(vmem_limit_bytes=16 << 20),
        name="prepare",
    )(*off_chip(queries, key_vectors, level_weight))


def begin_kernel(k_hbm, token_hbm, weight_hbm, sum_ref, sent_ref, held_ref, *rest):
    part_refs, (k_ref, weight_ref, sems) = rest[:-3], rest[-3:]
    loads = [
        pltpu.make_async_copy(source, target, sems.at[num])
        for num, (source, target) in enumerate(
            [(k_hbm, k_ref), (token_hbm, held_ref), (weight_hbm, weight_ref)]
        )
    ]
    for load in loads:
        load.start()
    loads[0].wait()
    loads[1].wait()
    total = lax.dot_general(
        k_ref[...], held_ref[...], (((0,), (0,)), ((), ())), preferred_element_type=F32
    )
    sum_ref[...] = total
    sent_ref[...] = total.astype(BF16)
    loads[2].wait()
    share = part_refs[0].shape[0]
    for num, part_ref in enumerate(part_refs):
        part_ref[...] = weight_ref[:, num * share : (num + 1) * share].T


def begin(key_vectors, tokens, weight, split):
    depth, width = weight.shape
    shape = (key_vectors.shape[1], tokens.shape[1])
    return pl.pallas_call(
        begin_kernel,
        in_specs=[pl.BlockSpec(memory_space=pltpu.HBM)] * 3,
        out_shape=[
            pltpu.VMEM(shape, F32),
            pltpu.VMEM(shape, BF16),
            pltpu.VMEM(tokens.shape, tokens.dtype),
        ]
        + [pltpu.VMEM((width // split, depth), weight.dtype)] * split,
        scratch_shapes=[
            pltpu.VMEM(key_vectors.shape, key_vectors.dtype),
            pltpu.VMEM(weight.shape, weight.dtype),
            pltpu.SemaphoreType.DMA((3,)),
        ],
        compiler_params=pltpu.CompilerParams(vmem_limit_bytes=8 << 20),
        name="begin",
    )(*off_chip(key_vectors, tokens, weight))


def cut_kernel(count, *refs):
    for num in range(count):
        block_ref, parts = refs[num], refs[count + 2 * num :][:2]
        rows = parts[0].shape[0]
        parts[0][...] = block_ref[:rows, :]
        parts[1][...] = block_ref[rows:, :]


def cut(blocks):
    return pl.pallas_call(
        functools.partial(cut_kernel, len(blocks)),
        in_specs=[pl.BlockSpec(memory_space=pltpu.VMEM)] * len(blocks),
        out_shape=[
            pltpu.VMEM((block.shape[0] // 2, block.shape[1]), block.dtype)
            for block in blocks
            for _ in range(2)
        ],
        compiler_params=pltpu.CompilerParams(vmem_limit_bytes=4 << 20),
    )(*blocks)


def ring_order(count):
    return list(range(0, count, 2)) + list(range(1, count, 2))[::-1]


def place(offset, depth, piece_width):
    count = lax.axis_size("ctx")
    mine = lax.axis_index("ctx")
    pos = jnp.where(mine % 2 == 0, mine // 2, count - 1 - mine // 2)
    pos = (pos + offset + count) % count
    index = jnp.where(pos < count // 2, 2 * pos, 2 * (count - 1 - pos) + 1)
    per_piece = piece_width // depth
    return jnp.bitwise_xor(index // per_piece, lax.axis_index("head")), index % per_piece * depth


def choose(offsets, pieces, depth, chosen_ref):
    for num, offset in enumerate(offsets):
        piece, start = place(offset, depth, pieces[0].shape[1])
        start = pl.multiple_of(start, 128)
        for index, ref in enumerate(pieces):

            @pl.when(piece == index)
            def _():
                chosen_ref[:, num * depth : (num + 1) * depth] = ref[:, pl.ds(start, depth)]


def extend_kernel(sizes, offsets, split, started, *refs):
    refs = list(refs)
    take = lambda count: [refs.pop(0) for _ in range(count)]
    groups = [take(size) for size in sizes]
    blocks = [take(split) for _ in offsets]
    totals = take(len(sizes)) if started else []
    out_refs, chosen_refs = take(len(sizes)), refs
    share, depth = blocks[0][0].shape
    for pieces, chosen_ref in zip(groups, chosen_refs):
        choose(offsets, pieces, depth, chosen_ref)
    step = min(256, share)
    for c0 in range(0, share * split, step):
        at = c0 % share
        left = jnp.concatenate(
            [block[c0 // share][at : at + step, :] for block in blocks], axis=1
        )
        for num, (out_ref, chosen_ref) in enumerate(zip(out_refs, chosen_refs)):
            total = dot_last(left, chosen_ref[...])
            if started:
                total = total + totals[num][c0 : c0 + step, :]
            out_ref[c0 : c0 + step, :] = total


def extend(totals, groups, parts):
    offsets = tuple(offset for offset, _ in parts)
    blocks = [half for _, block in parts for half in block]
    split = len(parts[0][1])
    share, depth = blocks[0].shape
    arrays = [*(piece for pieces in groups for piece in pieces), *blocks, *totals]
    rows = [pieces[0].shape[0] for pieces in groups]
    return pl.pallas_call(
        functools.partial(
            extend_kernel, [len(pieces) for pieces in groups], offsets, split, len(totals) > 0
        ),
        in_specs=[pl.BlockSpec(memory_space=pltpu.VMEM)] * len(arrays),
        out_shape=[pltpu.VMEM((share * split, count), F32) for count in rows],
        scratch_shapes=[pltpu.VMEM((count, depth * len(parts)), BF16) for count in rows],
        compiler_params=pltpu.CompilerParams(vmem_limit_bytes=12 << 20),
    )(*arrays)


def finish_kernel(piece_count, groups, offset, last_at, carried_at, final, head_size, *refs):
    last_count = len(last_at)
    refs = list(refs)
    take = lambda count: [refs.pop(0) for _ in range(count)]
    token_refs, sum_refs = take(piece_count), [take(piece_count) for _ in range(groups)]
    last_refs = take(last_count)
    value_ref, state_refs = refs.pop(0), take(groups)
    q_ref, w_ref, near_ref, score_ref = take(4)
    carried_refs = take(len(carried_at))
    width = value_ref.shape[0]
    step = min(256, width)
    columns = [(c0, None) for c0 in range(0, width, step)]
    if last_count:
        columns = [
            (start + c0, ref.at[c0 : c0 + step, :])
            for start, ref in zip(last_at, last_refs)
            for c0 in range(0, ref.shape[0], step)
        ]
    out_refs = take(1 if final else len(columns))
    stores = []
    if final:
        held_ref, sems = refs.pop(), refs.pop()

        def store(source, start, low):
            stores.append(
                pltpu.make_async_copy(
                    source,
                    out_refs[0].at[low : low + source.shape[0], start : start + step],
                    sems.at[len(stores)],
                )
            )
            stores[-1].start()

        for start, ref in zip(carried_at, carried_refs):
            store(ref, start, 0)
    length, state_rows = q_ref.shape
    near_levels = length.bit_length()
    far_levels = w_ref.shape[0] - near_levels
    rows = near_ref.shape[2]
    if last_count:
        token_chosen, *sum_chosen = refs
        depth = token_chosen.shape[1]
        choose([offset], token_refs, depth, token_chosen)
        for pieces, chosen in zip(sum_refs, sum_chosen):
            choose([offset], pieces, depth, chosen)
    mine = lax.axis_index("ctx")
    queries = q_ref[...]
    twice = jnp.concatenate([queries, queries], axis=1)
    for num, (c0, last_ref) in enumerate(columns):
        out_ref = held_ref.at[:, c0 : c0 + step] if final else out_refs[num]
        values = value_ref[c0 : c0 + step, :]
        states = [ref[c0 : c0 + step, :] for ref in state_refs]
        if last_count:
            left = last_ref[...]
            values = values + dot_last(left, token_chosen[...])
            states = [
                part + dot_last(left, chosen[...]) for part, chosen in zip(states, sum_chosen)
            ]
        values = values.astype(BF16)
        heads = range(c0 // head_size, (c0 + step) // head_size)

        def weight(level, low, high):
            return jnp.concatenate(
                [
                    spread_rows(
                        w_ref[level, head : head + 1, low:high] * level_scale(level), head_size
                    )
                    for head in heads
                ],
                axis=0,
            )

        far = None
        states = jnp.concatenate(states, axis=1)
        for far_num in range(far_levels):
            state = states[:, far_num * state_rows : (far_num + 1) * state_rows]
            state = jnp.where(jnp.right_shift(mine, far_num) % 2 == 1, state, jnp.zeros_like(state))
            high = state.astype(BF16)
            low = (state - high.astype(F32)).astype(BF16)
            reading = dot_last(jnp.concatenate([high, low], axis=1), twice)
            reading = weight(near_levels + far_num, 0, length) * reading
            far = reading if far is None else far + reading
        for t0 in range(0, length, rows):
            total = far[:, t0 : t0 + rows] + jnp.concatenate(
                [
                    jnp.dot(
                        values[head * head_size - c0 : (head + 1) * head_size - c0, t0 : t0 + rows],
                        near_ref[head, t0 : t0 + rows, :],
                        preferred_element_type=F32,
                    )
                    for head in heads
                ],
                axis=0,
            )
            for level in range(rows.bit_length(), near_levels):
                span = 1 << level - 1
                if t0 & span:
                    s0 = t0 // span * span - span
                    mixed = jnp.dot(
                        values[:, s0 : s0 + span],
                        score_ref[s0 : s0 + span, t0 : t0 + rows],
                        preferred_element_type=F32,
                    )
                    total = total + weight(level, t0, t0 + rows) * mixed
            out_ref[t0 : t0 + rows, :] = total.astype(BF16).T
            if final:
                store(out_ref.at[t0 : t0 + rows, :], c0, t0)
    for started in stores:
        started.wait()


def finish(
    values, states, offset, last, token_pieces, sum_pieces, queries, level_weight, near, head_size, carried, final
):
    width, length = values.shape
    step = min(256, width)
    flat_sums = [piece for pieces in sum_pieces for piece in pieces]
    parts = [part for _, part in last]
    held = [array for _, array in carried]
    arrays = [*token_pieces, *flat_sums, *parts, values, *states, queries, level_weight, *near, *held]
    scratch = []
    if last:
        depth = parts[0].shape[1]
        scratch = [pltpu.VMEM((rows, depth), BF16) for rows in [length, *(s.shape[1] for s in states)]]
    starts = [start + c0 for start, part in last for c0 in range(0, part.shape[0], step)]
    if final:
        scratch += [pltpu.SemaphoreType.DMA((width // step * (length // near[0].shape[2]),)), pltpu.VMEM((length, width), BF16)]
        outs = dict(
            out_shape=jax.ShapeDtypeStruct((length, width), BF16),
            out_specs=pl.BlockSpec(memory_space=pltpu.HBM),
        )
    else:
        outs = dict(out_shape=[pltpu.VMEM((length, step), BF16)] * len(starts))
    out = pl.pallas_call(
        functools.partial(
            finish_kernel,
            len(token_pieces),
            len(states),
            offset,
            [start for start, _ in last],
            [start for start, _ in carried],
            final,
            head_size,
        ),
        in_specs=[pl.BlockSpec(memory_space=pltpu.VMEM)] * len(arrays),
        scratch_shapes=scratch,
        compiler_params=pltpu.CompilerParams(vmem_limit_bytes=24 << 20),
        name="finish",
        **outs,
    )(*arrays)
    return out if final else list(zip(starts, out))


def body(tokens, value_weight, queries, key_vectors, level_weight):
    _, width_feat = tokens.shape
    depth, width_local = value_weight.shape
    head_local = level_weight.shape[1]
    head_size = width_local // head_local
    ctx_count = lax.axis_size("ctx")
    dev_bits = ctx_count.bit_length() - 1
    near = prepare(queries, key_vectors, level_weight)

    running, sent, held, *turned = begin(key_vectors, tokens, value_weight, 2)
    level_sums = []
    for section_bit in range(dev_bits):
        if section_bit > 0:
            sent = running.astype(BF16)
        if section_bit == dev_bits - 1 and dev_bits > 1:
            break
        partner = from_partner(sent, "ctx", section_bit, section_bit < dev_bits - 2)
        level_sums.append(partner)
        running = running + partner.astype(F32)
    if dev_bits > 1:
        unit = ctx_count // 4
        for hop in range(2):
            route = [((1 + hop) * unit + num, (2 + hop) * unit + num) for num in range(unit)]
            sent = lax.ppermute(sent, "ctx", route)
            top = sent if hop == 0 else top + sent
        level_sums.append(top)
    low_sums = jnp.concatenate(level_sums[:-1] or level_sums, axis=0)
    top_sums = level_sums[-1:] if dev_bits > 1 else []

    if depth % 256 or width_feat % depth:
        features = lax.all_gather(tokens, "head", axis=1, tiled=True)
        level_sums = jnp.concatenate([low_sums, *top_sums], axis=0)
        sums = lax.all_gather(level_sums, "head", axis=1, tiled=True)
        weight = lax.all_gather(value_weight, "ctx", axis=0, tiled=True)
        values = jnp.einsum("fc,tf->ct", weight, features, preferred_element_type=F32)
        states = jnp.einsum("fc,nf->cn", weight, sums, preferred_element_type=F32)
        return finish(
            values, [states], 0, [], [], [[]], queries, level_weight, near, head_size, [], True
        )

    order = ring_order(ctx_count)
    ahead = [(order[i], order[(i + 1) % ctx_count]) for i in range(ctx_count)]
    back = [(b, a) for a, b in ahead]
    half_count = ctx_count // 2
    token_pieces = on_chip(*gather_pieces(held, "head"))
    sum_pieces = [on_chip(*gather_pieces(low_sums, "head"))]
    sum_pieces += [on_chip(*gather_pieces(sums, "head")) for sums in top_sums]
    cw = ccw = tuple(turned)
    steps = [[(0, cw)]]

    def move(part, route):
        return lax.ppermute(part, "ctx", route)

    for step in range(1, half_count):
        cw = tuple(move(part, ahead) for part in cw)
        ccw = tuple(move(part, back) for part in ccw)
        steps.append([(-step, on_chip(*cw)), (step, on_chip(*ccw))])
    share = width_local // 4
    parts = [*cut([cw[0]]), *cut([ccw[1]])]
    last = [
        [(num * share, move(parts[num], ahead)), ((2 + num) * share, move(parts[2 + num], back))]
        for num in range(2)
    ]
    values = extend([], [token_pieces], steps[0] + steps[1])
    for step in range(2, half_count - 1):
        values = extend(values, [token_pieces], steps[step])
    early = [part for parts in steps[:-1] for part in parts]
    low = extend([], sum_pieces[:1], early)
    values, low = extend([*values, *low], [token_pieces, sum_pieces[0]], steps[-1])
    top = [extend([], [pieces], early + steps[-1])[0] for pieces in sum_pieces[1:]]
    states = [low, *top]
    carried = []
    for num, parts in enumerate(last):
        starts = [start for start, _ in parts]
        done = finish(
            values,
            states,
            half_count,
            list(zip(starts, on_chip(*(part for _, part in parts)))),
            token_pieces,
            sum_pieces,
            queries,
            level_weight,
            near,
            head_size,
            carried,
            num == len(last) - 1,
        )
        carried = done
    return done


def solution(mesh):
    return jax.shard_map(
        body,
        mesh=mesh,
        in_specs=(
            P("ctx", "head"),
            P("ctx", "head"),
            P("ctx", None),
            P("ctx", None),
            P(None, "head", "ctx"),
        ),
        out_specs=P("ctx", "head"),
        check_vma=False,
    )
```

```python
import functools

import jax
import jax.numpy as jnp
from jax import lax
from jax.experimental import pallas as pl
from jax.experimental.pallas import tpu as pltpu
from jax.sharding import PartitionSpec as P


F32 = jnp.float32
BF16 = jnp.bfloat16


def from_partner(block, axis, distance):
    count = lax.axis_size(axis)
    route = []
    for low in range(count):
        high = low | 1 << distance
        if high != low and high < count:
            route += [(low, high), (high, low)]
    return lax.ppermute(block, axis, route)


def gather_pieces(block, axis):
    pieces = [block]
    masks = [0]
    for bit in reversed(range(lax.axis_size(axis).bit_length() - 1)):
        for mask, piece in zip(list(masks), list(pieces)):
            pieces.append(from_partner(piece, axis, bit))
            masks.append(mask | 1 << bit)
    return [piece for _, piece in sorted(zip(masks, pieces), key=lambda pair: pair[0])]


def level_scale(level_num):
    return 1.0 if level_num == 0 else 2.0 ** (-(level_num - 1) / 2.0)


def on_chip(*arrays):
    return [pltpu.with_memory_space_constraint(array, pltpu.VMEM) for array in arrays]


def off_chip(*arrays):
    return [pltpu.with_memory_space_constraint(array, pltpu.HBM) for array in arrays]


def dot_last(left, right):
    return lax.dot_general(left, right, (((1,), (1,)), ((), ())), preferred_element_type=F32)


def spread_rows(row, count):
    return jnp.broadcast_to(row, (count, row.shape[1]))


def prepare_kernel(q_hbm, k_hbm, w_hbm, near_ref, score_ref, row_ref, q_ref, k_ref, w_ref, sems):
    loads = [
        pltpu.make_async_copy(source, target, sems.at[num])
        for num, (source, target) in enumerate([(q_hbm, q_ref), (k_hbm, k_ref), (w_hbm, w_ref)])
    ]
    for load in loads:
        load.start()
    for load in loads:
        load.wait()
    length = q_ref.shape[0]
    heads, _, rows = near_ref.shape
    tile = min(128, length)
    sub = 8
    tile_levels = tile.bit_length() - 1
    sub_levels = sub.bit_length() - 1
    score_ref[...] = dot_last(k_ref[...], q_ref[...]).astype(BF16)
    for num in range(rows.bit_length()):
        for head in range(heads):
            row_ref[head, num : num + 1, :] = w_ref[num, head : head + 1, :] * level_scale(num)

    def grid_level(shape, shift):
        s_pos = lax.broadcasted_iota(jnp.int32, shape, 0)
        t_pos = jnp.right_shift(lax.broadcasted_iota(jnp.int32, shape, 1), shift)
        if shift == 0:
            t_pos = jnp.bitwise_and(t_pos, sub - 1)
        differ = jnp.bitwise_xor(s_pos, t_pos)
        level = jnp.zeros(shape, jnp.int32)
        for bit in range(tile_levels):
            level = level + (jnp.right_shift(differ, bit) > 0).astype(jnp.int32)
        return jnp.where(s_pos <= t_pos, level, -1)

    fine = grid_level((sub, tile), 0)
    coarse = grid_level((tile // sub, tile), sub_levels)
    near_diag = lax.broadcasted_iota(jnp.int32, (tile, tile), 0) // sub == (
        lax.broadcasted_iota(jnp.int32, (tile, tile), 1) // sub
    )

    def one_head(head, carry):
        for t0 in range(0, length, tile):
            base = t0 // rows * rows
            weight_rows = [
                row_ref[head, num : num + 1, t0 : t0 + tile] for num in range(rows.bit_length())
            ]
            for s0 in range(base, base + rows, tile):
                place_at = (head, pl.ds(s0, tile), pl.ds(t0 - base, tile))
                if s0 > t0:
                    near_ref[place_at] = jnp.zeros((tile, tile), BF16)
                    continue
                if s0 == t0:
                    small = jnp.zeros((sub, tile), F32)
                    for num in range(sub_levels + 1):
                        small = jnp.where(fine == num, spread_rows(weight_rows[num], sub), small)
                    big = jnp.zeros((tile // sub, tile), F32)
                    for num in range(sub_levels + 1, tile_levels + 1):
                        big = jnp.where(
                            coarse == num - sub_levels,
                            spread_rows(weight_rows[num], tile // sub),
                            big,
                        )
                    big = jnp.concatenate(
                        [spread_rows(big[row : row + 1], sub) for row in range(tile // sub)], axis=0
                    )
                    weight = jnp.where(near_diag, jnp.concatenate([small] * (tile // sub), 0), big)
                else:
                    num = tile_levels + (s0 // tile ^ t0 // tile).bit_length()
                    weight = spread_rows(weight_rows[num], tile)
                score = score_ref[s0 : s0 + tile, t0 : t0 + tile].astype(F32)
                near_ref[place_at] = (weight * score).astype(BF16)
        return carry

    lax.fori_loop(0, heads, one_head, 0)


def prepare(queries, key_vectors, level_weight):
    length = queries.shape[0]
    heads = level_weight.shape[1]
    rows = min(256, length)
    return pl.pallas_call(
        prepare_kernel,
        in_specs=[pl.BlockSpec(memory_space=pltpu.HBM)] * 3,
        out_shape=[
            pltpu.VMEM((heads, length, rows), BF16),
            pltpu.VMEM((length, length), BF16),
        ],
        scratch_shapes=[
            pltpu.VMEM((heads, rows.bit_length(), length), F32),
            pltpu.VMEM(queries.shape, queries.dtype),
            pltpu.VMEM(key_vectors.shape, key_vectors.dtype),
            pltpu.VMEM(level_weight.shape, level_weight.dtype),
            pltpu.SemaphoreType.DMA((3,)),
        ],
        compiler_params=pltpu.CompilerParams(vmem_limit_bytes=16 << 20),
        name="prepare",
    )(*off_chip(queries, key_vectors, level_weight))


def begin_kernel(k_hbm, token_hbm, weight_hbm, sum_ref, sent_ref, held_ref, *rest):
    part_refs, (k_ref, weight_ref, sems) = rest[:-3], rest[-3:]
    loads = [
        pltpu.make_async_copy(source, target, sems.at[num])
        for num, (source, target) in enumerate(
            [(k_hbm, k_ref), (token_hbm, held_ref), (weight_hbm, weight_ref)]
        )
    ]
    for load in loads:
        load.start()
    loads[0].wait()
    loads[1].wait()
    total = lax.dot_general(
        k_ref[...], held_ref[...], (((0,), (0,)), ((), ())), preferred_element_type=F32
    )
    sum_ref[...] = total
    sent_ref[...] = total.astype(BF16)
    loads[2].wait()
    share = part_refs[0].shape[0]
    for num, part_ref in enumerate(part_refs):
        part_ref[...] = weight_ref[:, num * share : (num + 1) * share].T


def begin(key_vectors, tokens, weight, split):
    depth, width = weight.shape
    shape = (key_vectors.shape[1], tokens.shape[1])
    return pl.pallas_call(
        begin_kernel,
        in_specs=[pl.BlockSpec(memory_space=pltpu.HBM)] * 3,
        out_shape=[
            pltpu.VMEM(shape, F32),
            pltpu.VMEM(shape, BF16),
            pltpu.VMEM(tokens.shape, tokens.dtype),
        ]
        + [pltpu.VMEM((width // split, depth), weight.dtype)] * split,
        scratch_shapes=[
            pltpu.VMEM(key_vectors.shape, key_vectors.dtype),
            pltpu.VMEM(weight.shape, weight.dtype),
            pltpu.SemaphoreType.DMA((3,)),
        ],
        compiler_params=pltpu.CompilerParams(vmem_limit_bytes=8 << 20),
        name="begin",
    )(*off_chip(key_vectors, tokens, weight))


def cut_kernel(count, *refs):
    for num in range(count):
        block_ref, parts = refs[num], refs[count + 2 * num :][:2]
        rows = parts[0].shape[0]
        parts[0][...] = block_ref[:rows, :]
        parts[1][...] = block_ref[rows:, :]


def cut(blocks):
    return pl.pallas_call(
        functools.partial(cut_kernel, len(blocks)),
        in_specs=[pl.BlockSpec(memory_space=pltpu.VMEM)] * len(blocks),
        out_shape=[
            pltpu.VMEM((block.shape[0] // 2, block.shape[1]), block.dtype)
            for block in blocks
            for _ in range(2)
        ],
        compiler_params=pltpu.CompilerParams(vmem_limit_bytes=4 << 20),
    )(*blocks)


def ring_order(count):
    return list(range(0, count, 2)) + list(range(1, count, 2))[::-1]


def place(offset, depth, piece_width):
    count = lax.axis_size("ctx")
    mine = lax.axis_index("ctx")
    pos = jnp.where(mine % 2 == 0, mine // 2, count - 1 - mine // 2)
    pos = (pos + offset + count) % count
    index = jnp.where(pos < count // 2, 2 * pos, 2 * (count - 1 - pos) + 1)
    per_piece = piece_width // depth
    return jnp.bitwise_xor(index // per_piece, lax.axis_index("head")), index % per_piece * depth


def choose(offsets, pieces, depth, chosen_ref):
    for num, offset in enumerate(offsets):
        piece, start = place(offset, depth, pieces[0].shape[1])
        start = pl.multiple_of(start, 128)
        for index, ref in enumerate(pieces):

            @pl.when(piece == index)
            def _():
                chosen_ref[:, num * depth : (num + 1) * depth] = ref[:, pl.ds(start, depth)]


def extend_kernel(sizes, offsets, split, started, *refs):
    refs = list(refs)
    take = lambda count: [refs.pop(0) for _ in range(count)]
    groups = [take(size) for size in sizes]
    blocks = [take(split) for _ in offsets]
    totals = take(len(sizes)) if started else []
    out_refs, chosen_refs = take(len(sizes)), refs
    share, depth = blocks[0][0].shape
    for pieces, chosen_ref in zip(groups, chosen_refs):
        choose(offsets, pieces, depth, chosen_ref)
    step = min(256, share)
    for c0 in range(0, share * split, step):
        at = c0 % share
        left = jnp.concatenate(
            [block[c0 // share][at : at + step, :] for block in blocks], axis=1
        )
        for num, (out_ref, chosen_ref) in enumerate(zip(out_refs, chosen_refs)):
            total = dot_last(left, chosen_ref[...])
            if started:
                total = total + totals[num][c0 : c0 + step, :]
            out_ref[c0 : c0 + step, :] = total


def extend(totals, groups, parts):
    offsets = tuple(offset for offset, _ in parts)
    blocks = [half for _, block in parts for half in block]
    split = len(parts[0][1])
    share, depth = blocks[0].shape
    arrays = [*(piece for pieces in groups for piece in pieces), *blocks, *totals]
    rows = [pieces[0].shape[0] for pieces in groups]
    return pl.pallas_call(
        functools.partial(
            extend_kernel, [len(pieces) for pieces in groups], offsets, split, len(totals) > 0
        ),
        in_specs=[pl.BlockSpec(memory_space=pltpu.VMEM)] * len(arrays),
        out_shape=[pltpu.VMEM((share * split, count), F32) for count in rows],
        scratch_shapes=[pltpu.VMEM((count, depth * len(parts)), BF16) for count in rows],
        compiler_params=pltpu.CompilerParams(vmem_limit_bytes=12 << 20),
    )(*arrays)


def finish_kernel(piece_count, groups, offset, last_at, carried_at, final, head_size, *refs):
    last_count = len(last_at)
    refs = list(refs)
    take = lambda count: [refs.pop(0) for _ in range(count)]
    token_refs, sum_refs = take(piece_count), [take(piece_count) for _ in range(groups)]
    last_refs = take(last_count)
    value_ref, state_refs = refs.pop(0), take(groups)
    q_ref, w_ref, near_ref, score_ref = take(4)
    carried_refs = take(len(carried_at))
    width = value_ref.shape[0]
    step = min(256, width)
    columns = [(c0, None) for c0 in range(0, width, step)]
    if last_count:
        columns = [
            (start + c0, ref.at[c0 : c0 + step, :])
            for start, ref in zip(last_at, last_refs)
            for c0 in range(0, ref.shape[0], step)
        ]
    out_refs = take(1 if final else len(columns))
    stores = []
    if final:
        held_ref, sems = refs.pop(), refs.pop()

        def store(source, start):
            stores.append(
                pltpu.make_async_copy(
                    source, out_refs[0].at[:, start : start + step], sems.at[len(stores)]
                )
            )
            stores[-1].start()

        for start, ref in zip(carried_at, carried_refs):
            store(ref, start)
    length, state_rows = q_ref.shape
    near_levels = length.bit_length()
    far_levels = w_ref.shape[0] - near_levels
    rows = near_ref.shape[2]
    if last_count:
        token_chosen, *sum_chosen = refs
        depth = token_chosen.shape[1]
        choose([offset], token_refs, depth, token_chosen)
        for pieces, chosen in zip(sum_refs, sum_chosen):
            choose([offset], pieces, depth, chosen)
    mine = lax.axis_index("ctx")
    queries = q_ref[...]
    twice = jnp.concatenate([queries, queries], axis=1)
    for num, (c0, last_ref) in enumerate(columns):
        out_ref = held_ref.at[:, c0 : c0 + step] if final else out_refs[num]
        values = value_ref[c0 : c0 + step, :]
        states = [ref[c0 : c0 + step, :] for ref in state_refs]
        if last_count:
            left = last_ref[...]
            values = values + dot_last(left, token_chosen[...])
            states = [
                part + dot_last(left, chosen[...]) for part, chosen in zip(states, sum_chosen)
            ]
        values = values.astype(BF16)
        heads = range(c0 // head_size, (c0 + step) // head_size)

        def weight(level, low, high):
            return jnp.concatenate(
                [
                    spread_rows(
                        w_ref[level, head : head + 1, low:high] * level_scale(level), head_size
                    )
                    for head in heads
                ],
                axis=0,
            )

        far = None
        states = jnp.concatenate(states, axis=1)
        for far_num in range(far_levels):
            state = states[:, far_num * state_rows : (far_num + 1) * state_rows]
            state = jnp.where(jnp.right_shift(mine, far_num) % 2 == 1, state, jnp.zeros_like(state))
            high = state.astype(BF16)
            low = (state - high.astype(F32)).astype(BF16)
            reading = dot_last(jnp.concatenate([high, low], axis=1), twice)
            reading = weight(near_levels + far_num, 0, length) * reading
            far = reading if far is None else far + reading
        for t0 in range(0, length, rows):
            total = far[:, t0 : t0 + rows] + jnp.concatenate(
                [
                    jnp.dot(
                        values[head * head_size - c0 : (head + 1) * head_size - c0, t0 : t0 + rows],
                        near_ref[head, t0 : t0 + rows, :],
                        preferred_element_type=F32,
                    )
                    for head in heads
                ],
                axis=0,
            )
            for level in range(rows.bit_length(), near_levels):
                span = 1 << level - 1
                if t0 & span:
                    s0 = t0 // span * span - span
                    mixed = jnp.dot(
                        values[:, s0 : s0 + span],
                        score_ref[s0 : s0 + span, t0 : t0 + rows],
                        preferred_element_type=F32,
                    )
                    total = total + weight(level, t0, t0 + rows) * mixed
            out_ref[t0 : t0 + rows, :] = total.astype(BF16).T
        if final:
            store(out_ref, c0)
    for started in stores:
        started.wait()


def finish(
    values, states, offset, last, token_pieces, sum_pieces, queries, level_weight, near, head_size, carried, final
):
    width, length = values.shape
    step = min(256, width)
    flat_sums = [piece for pieces in sum_pieces for piece in pieces]
    parts = [part for _, part in last]
    held = [array for _, array in carried]
    arrays = [*token_pieces, *flat_sums, *parts, values, *states, queries, level_weight, *near, *held]
    scratch = []
    if last:
        depth = parts[0].shape[1]
        scratch = [pltpu.VMEM((rows, depth), BF16) for rows in [length, *(s.shape[1] for s in states)]]
    starts = [start + c0 for start, part in last for c0 in range(0, part.shape[0], step)]
    if final:
        scratch += [pltpu.SemaphoreType.DMA((max(1, width // step),)), pltpu.VMEM((length, width), BF16)]
        outs = dict(
            out_shape=jax.ShapeDtypeStruct((length, width), BF16),
            out_specs=pl.BlockSpec(memory_space=pltpu.HBM),
        )
    else:
        outs = dict(out_shape=[pltpu.VMEM((length, step), BF16)] * len(starts))
    out = pl.pallas_call(
        functools.partial(
            finish_kernel,
            len(token_pieces),
            len(states),
            offset,
            [start for start, _ in last],
            [start for start, _ in carried],
            final,
            head_size,
        ),
        in_specs=[pl.BlockSpec(memory_space=pltpu.VMEM)] * len(arrays),
        scratch_shapes=scratch,
        compiler_params=pltpu.CompilerParams(vmem_limit_bytes=24 << 20),
        name="finish",
        **outs,
    )(*arrays)
    return out if final else list(zip(starts, out))


def body(tokens, value_weight, queries, key_vectors, level_weight):
    _, width_feat = tokens.shape
    depth, width_local = value_weight.shape
    head_local = level_weight.shape[1]
    head_size = width_local // head_local
    ctx_count = lax.axis_size("ctx")
    dev_bits = ctx_count.bit_length() - 1
    near = prepare(queries, key_vectors, level_weight)

    running, sent, held, *turned = begin(key_vectors, tokens, value_weight, 2)
    level_sums = []
    for section_bit in range(dev_bits):
        if section_bit > 0:
            sent = running.astype(BF16)
        partner = from_partner(sent, "ctx", section_bit)
        level_sums.append(partner)
        running = running + partner.astype(F32)
    level_sums = jnp.concatenate(level_sums, axis=0)

    if depth % 256 or width_feat % depth:
        features = lax.all_gather(tokens, "head", axis=1, tiled=True)
        sums = lax.all_gather(level_sums, "head", axis=1, tiled=True)
        weight = lax.all_gather(value_weight, "ctx", axis=0, tiled=True)
        values = jnp.einsum("fc,tf->ct", weight, features, preferred_element_type=F32)
        states = jnp.einsum("fc,nf->cn", weight, sums, preferred_element_type=F32)
        return finish(
            values, [states], 0, [], [], [[]], queries, level_weight, near, head_size, [], True
        )

    order = ring_order(ctx_count)
    ahead = [(order[i], order[(i + 1) % ctx_count]) for i in range(ctx_count)]
    back = [(b, a) for a, b in ahead]
    half_count = ctx_count // 2
    token_pieces = on_chip(*gather_pieces(held, "head"))
    sum_pieces = on_chip(*gather_pieces(level_sums, "head"))
    cw = ccw = tuple(turned)
    steps = [[(0, cw)]]

    def move(part, route):
        return lax.ppermute(part, "ctx", route)

    for step in range(1, half_count):
        cw = tuple(move(part, ahead) for part in cw)
        ccw = tuple(move(part, back) for part in ccw)
        steps.append([(-step, on_chip(*cw)), (step, on_chip(*ccw))])
    share = width_local // 4
    parts = [*cut([cw[0]]), *cut([ccw[1]])]
    last = [
        [(num * share, move(parts[num], ahead)), ((2 + num) * share, move(parts[2 + num], back))]
        for num in range(2)
    ]
    values = extend([], [token_pieces], steps[0] + steps[1])
    for step in range(2, half_count - 1):
        values = extend(values, [token_pieces], steps[step])
    early = [part for parts in steps[:-1] for part in parts]
    low = extend([], [sum_pieces], early)
    values, low = extend([*values, *low], [token_pieces, sum_pieces], steps[-1])
    carried = []
    for num, parts in enumerate(last):
        starts = [start for start, _ in parts]
        done = finish(
            values,
            [low],
            half_count,
            list(zip(starts, on_chip(*(part for _, part in parts)))),
            token_pieces,
            [sum_pieces],
            queries,
            level_weight,
            near,
            head_size,
            carried,
            num == len(last) - 1,
        )
        carried = done
    return done


def solution(mesh):
    return jax.shard_map(
        body,
        mesh=mesh,
        in_specs=(
            P("ctx", "head"),
            P("ctx", "head"),
            P("ctx", None),
            P("ctx", None),
            P(None, "head", "ctx"),
        ),
        out_specs=P("ctx", "head"),
        check_vma=False,
    )
```

```python
import functools

import jax
import jax.numpy as jnp
from jax import lax
from jax.experimental import pallas as pl
from jax.experimental.pallas import tpu as pltpu
from jax.sharding import PartitionSpec as P


F32 = jnp.float32
BF16 = jnp.bfloat16


def from_partner(block, axis, distance):
    count = lax.axis_size(axis)
    route = []
    for low in range(count):
        high = low | 1 << distance
        if high != low and high < count:
            route += [(low, high), (high, low)]
    return lax.ppermute(block, axis, route)


def gather_pieces(block, axis):
    pieces = [block]
    masks = [0]
    for bit in reversed(range(lax.axis_size(axis).bit_length() - 1)):
        for mask, piece in zip(list(masks), list(pieces)):
            pieces.append(from_partner(piece, axis, bit))
            masks.append(mask | 1 << bit)
    return [piece for _, piece in sorted(zip(masks, pieces), key=lambda pair: pair[0])]


def level_scale(level_num):
    return 1.0 if level_num == 0 else 2.0 ** (-(level_num - 1) / 2.0)


def on_chip(*arrays):
    return [pltpu.with_memory_space_constraint(array, pltpu.VMEM) for array in arrays]


def off_chip(*arrays):
    return [pltpu.with_memory_space_constraint(array, pltpu.HBM) for array in arrays]


def dot_last(left, right):
    return lax.dot_general(left, right, (((1,), (1,)), ((), ())), preferred_element_type=F32)


def spread_rows(row, count):
    return jnp.broadcast_to(row, (count, row.shape[1]))


def prepare_kernel(q_hbm, k_hbm, w_hbm, near_ref, score_ref, row_ref, q_ref, k_ref, w_ref, sems):
    loads = [
        pltpu.make_async_copy(source, target, sems.at[num])
        for num, (source, target) in enumerate([(q_hbm, q_ref), (k_hbm, k_ref), (w_hbm, w_ref)])
    ]
    for load in loads:
        load.start()
    for load in loads:
        load.wait()
    length = q_ref.shape[0]
    heads, _, rows = near_ref.shape
    tile = min(128, length)
    sub = 8
    tile_levels = tile.bit_length() - 1
    sub_levels = sub.bit_length() - 1
    score_ref[...] = dot_last(k_ref[...], q_ref[...]).astype(BF16)
    for num in range(rows.bit_length()):
        for head in range(heads):
            row_ref[head, num : num + 1, :] = w_ref[num, head : head + 1, :] * level_scale(num)

    def grid_level(shape, shift):
        s_pos = lax.broadcasted_iota(jnp.int32, shape, 0)
        t_pos = jnp.right_shift(lax.broadcasted_iota(jnp.int32, shape, 1), shift)
        if shift == 0:
            t_pos = jnp.bitwise_and(t_pos, sub - 1)
        differ = jnp.bitwise_xor(s_pos, t_pos)
        level = jnp.zeros(shape, jnp.int32)
        for bit in range(tile_levels):
            level = level + (jnp.right_shift(differ, bit) > 0).astype(jnp.int32)
        return jnp.where(s_pos <= t_pos, level, -1)

    fine = grid_level((sub, tile), 0)
    coarse = grid_level((tile // sub, tile), sub_levels)
    near_diag = lax.broadcasted_iota(jnp.int32, (tile, tile), 0) // sub == (
        lax.broadcasted_iota(jnp.int32, (tile, tile), 1) // sub
    )

    def one_head(head, carry):
        for t0 in range(0, length, tile):
            base = t0 // rows * rows
            weight_rows = [
                row_ref[head, num : num + 1, t0 : t0 + tile] for num in range(rows.bit_length())
            ]
            for s0 in range(base, base + rows, tile):
                place_at = (head, pl.ds(s0, tile), pl.ds(t0 - base, tile))
                if s0 > t0:
                    near_ref[place_at] = jnp.zeros((tile, tile), BF16)
                    continue
                if s0 == t0:
                    small = jnp.zeros((sub, tile), F32)
                    for num in range(sub_levels + 1):
                        small = jnp.where(fine == num, spread_rows(weight_rows[num], sub), small)
                    big = jnp.zeros((tile // sub, tile), F32)
                    for num in range(sub_levels + 1, tile_levels + 1):
                        big = jnp.where(
                            coarse == num - sub_levels,
                            spread_rows(weight_rows[num], tile // sub),
                            big,
                        )
                    big = jnp.concatenate(
                        [spread_rows(big[row : row + 1], sub) for row in range(tile // sub)], axis=0
                    )
                    weight = jnp.where(near_diag, jnp.concatenate([small] * (tile // sub), 0), big)
                else:
                    num = tile_levels + (s0 // tile ^ t0 // tile).bit_length()
                    weight = spread_rows(weight_rows[num], tile)
                score = score_ref[s0 : s0 + tile, t0 : t0 + tile].astype(F32)
                near_ref[place_at] = (weight * score).astype(BF16)
        return carry

    lax.fori_loop(0, heads, one_head, 0)


def prepare(queries, key_vectors, level_weight):
    length = queries.shape[0]
    heads = level_weight.shape[1]
    rows = min(256, length)
    return pl.pallas_call(
        prepare_kernel,
        in_specs=[pl.BlockSpec(memory_space=pltpu.HBM)] * 3,
        out_shape=[
            pltpu.VMEM((heads, length, rows), BF16),
            pltpu.VMEM((length, length), BF16),
        ],
        scratch_shapes=[
            pltpu.VMEM((heads, rows.bit_length(), length), F32),
            pltpu.VMEM(queries.shape, queries.dtype),
            pltpu.VMEM(key_vectors.shape, key_vectors.dtype),
            pltpu.VMEM(level_weight.shape, level_weight.dtype),
            pltpu.SemaphoreType.DMA((3,)),
        ],
        compiler_params=pltpu.CompilerParams(vmem_limit_bytes=16 << 20),
        name="prepare",
    )(*off_chip(queries, key_vectors, level_weight))


def begin_kernel(k_hbm, token_hbm, weight_hbm, sum_ref, sent_ref, held_ref, *rest):
    part_refs, (k_ref, weight_ref, sems) = rest[:-3], rest[-3:]
    loads = [
        pltpu.make_async_copy(source, target, sems.at[num])
        for num, (source, target) in enumerate(
            [(k_hbm, k_ref), (token_hbm, held_ref), (weight_hbm, weight_ref)]
        )
    ]
    for load in loads:
        load.start()
    loads[0].wait()
    loads[1].wait()
    total = lax.dot_general(
        k_ref[...], held_ref[...], (((0,), (0,)), ((), ())), preferred_element_type=F32
    )
    sum_ref[...] = total
    sent_ref[...] = total.astype(BF16)
    loads[2].wait()
    share = part_refs[0].shape[0]
    for num, part_ref in enumerate(part_refs):
        part_ref[...] = weight_ref[:, num * share : (num + 1) * share].T


def begin(key_vectors, tokens, weight, split):
    depth, width = weight.shape
    shape = (key_vectors.shape[1], tokens.shape[1])
    return pl.pallas_call(
        begin_kernel,
        in_specs=[pl.BlockSpec(memory_space=pltpu.HBM)] * 3,
        out_shape=[
            pltpu.VMEM(shape, F32),
            pltpu.VMEM(shape, BF16),
            pltpu.VMEM(tokens.shape, tokens.dtype),
        ]
        + [pltpu.VMEM((width // split, depth), weight.dtype)] * split,
        scratch_shapes=[
            pltpu.VMEM(key_vectors.shape, key_vectors.dtype),
            pltpu.VMEM(weight.shape, weight.dtype),
            pltpu.SemaphoreType.DMA((3,)),
        ],
        compiler_params=pltpu.CompilerParams(vmem_limit_bytes=8 << 20),
        name="begin",
    )(*off_chip(key_vectors, tokens, weight))


def cut_kernel(count, *refs):
    for num in range(count):
        block_ref, parts = refs[num], refs[count + 2 * num :][:2]
        rows = parts[0].shape[0]
        parts[0][...] = block_ref[:rows, :]
        parts[1][...] = block_ref[rows:, :]


def cut(blocks):
    return pl.pallas_call(
        functools.partial(cut_kernel, len(blocks)),
        in_specs=[pl.BlockSpec(memory_space=pltpu.VMEM)] * len(blocks),
        out_shape=[
            pltpu.VMEM((block.shape[0] // 2, block.shape[1]), block.dtype)
            for block in blocks
            for _ in range(2)
        ],
        compiler_params=pltpu.CompilerParams(vmem_limit_bytes=4 << 20),
    )(*blocks)


def ring_order(count):
    return list(range(0, count, 2)) + list(range(1, count, 2))[::-1]


def place(offset, depth, piece_width):
    count = lax.axis_size("ctx")
    mine = lax.axis_index("ctx")
    pos = jnp.where(mine % 2 == 0, mine // 2, count - 1 - mine // 2)
    pos = (pos + offset + count) % count
    index = jnp.where(pos < count // 2, 2 * pos, 2 * (count - 1 - pos) + 1)
    per_piece = piece_width // depth
    return jnp.bitwise_xor(index // per_piece, lax.axis_index("head")), index % per_piece * depth


def choose(offsets, pieces, depth, chosen_ref):
    for num, offset in enumerate(offsets):
        piece, start = place(offset, depth, pieces[0].shape[1])
        start = pl.multiple_of(start, 128)
        for index, ref in enumerate(pieces):

            @pl.when(piece == index)
            def _():
                chosen_ref[:, num * depth : (num + 1) * depth] = ref[:, pl.ds(start, depth)]


def extend_kernel(sizes, offsets, split, started, *refs):
    refs = list(refs)
    take = lambda count: [refs.pop(0) for _ in range(count)]
    groups = [take(size) for size in sizes]
    blocks = [take(split) for _ in offsets]
    totals = take(len(sizes)) if started else []
    out_refs, chosen_refs = take(len(sizes)), refs
    share, depth = blocks[0][0].shape
    for pieces, chosen_ref in zip(groups, chosen_refs):
        choose(offsets, pieces, depth, chosen_ref)
    step = min(256, share)
    for c0 in range(0, share * split, step):
        at = c0 % share
        left = jnp.concatenate(
            [block[c0 // share][at : at + step, :] for block in blocks], axis=1
        )
        for num, (out_ref, chosen_ref) in enumerate(zip(out_refs, chosen_refs)):
            total = dot_last(left, chosen_ref[...])
            if started:
                total = total + totals[num][c0 : c0 + step, :]
            out_ref[c0 : c0 + step, :] = total


def extend(totals, groups, parts):
    offsets = tuple(offset for offset, _ in parts)
    blocks = [half for _, block in parts for half in block]
    split = len(parts[0][1])
    share, depth = blocks[0].shape
    arrays = [*(piece for pieces in groups for piece in pieces), *blocks, *totals]
    rows = [pieces[0].shape[0] for pieces in groups]
    return pl.pallas_call(
        functools.partial(
            extend_kernel, [len(pieces) for pieces in groups], offsets, split, len(totals) > 0
        ),
        in_specs=[pl.BlockSpec(memory_space=pltpu.VMEM)] * len(arrays),
        out_shape=[pltpu.VMEM((share * split, count), F32) for count in rows],
        scratch_shapes=[pltpu.VMEM((count, depth * len(parts)), BF16) for count in rows],
        compiler_params=pltpu.CompilerParams(vmem_limit_bytes=12 << 20),
    )(*arrays)


def finish_kernel(piece_count, groups, offset, last_at, carried_at, final, head_size, *refs):
    last_count = len(last_at)
    refs = list(refs)
    take = lambda count: [refs.pop(0) for _ in range(count)]
    token_refs, sum_refs = take(piece_count), [take(piece_count) for _ in range(groups)]
    last_refs = take(last_count)
    value_ref, state_refs = refs.pop(0), take(groups)
    q_ref, w_ref, near_ref, score_ref = take(4)
    carried_refs = take(len(carried_at))
    width = value_ref.shape[0]
    step = min(256, width)
    columns = [(c0, None) for c0 in range(0, width, step)]
    if last_count:
        columns = [
            (start + c0, ref.at[c0 : c0 + step, :])
            for start, ref in zip(last_at, last_refs)
            for c0 in range(0, ref.shape[0], step)
        ]
    out_refs = take(1 if final else len(columns))
    stores = []
    if final:
        held_ref, sems = refs.pop(), refs.pop()

        def store(source, start):
            stores.append(
                pltpu.make_async_copy(
                    source, out_refs[0].at[:, start : start + step], sems.at[len(stores)]
                )
            )
            stores[-1].start()

        for start, ref in zip(carried_at, carried_refs):
            store(ref, start)
    length, state_rows = q_ref.shape
    near_levels = length.bit_length()
    far_levels = w_ref.shape[0] - near_levels
    rows = near_ref.shape[2]
    if last_count:
        token_chosen, *sum_chosen = refs
        depth = token_chosen.shape[1]
        choose([offset], token_refs, depth, token_chosen)
        for pieces, chosen in zip(sum_refs, sum_chosen):
            choose([offset], pieces, depth, chosen)
    mine = lax.axis_index("ctx")
    queries = q_ref[...]
    twice = jnp.concatenate([queries, queries], axis=1)
    for num, (c0, last_ref) in enumerate(columns):
        out_ref = held_ref.at[:, c0 : c0 + step] if final else out_refs[num]
        values = value_ref[c0 : c0 + step, :]
        states = [ref[c0 : c0 + step, :] for ref in state_refs]
        if last_count:
            left = last_ref[...]
            values = values + dot_last(left, token_chosen[...])
            states = [
                part + dot_last(left, chosen[...]) for part, chosen in zip(states, sum_chosen)
            ]
        values = values.astype(BF16)
        heads = range(c0 // head_size, (c0 + step) // head_size)

        def weight(level, low, high):
            return jnp.concatenate(
                [
                    spread_rows(
                        w_ref[level, head : head + 1, low:high] * level_scale(level), head_size
                    )
                    for head in heads
                ],
                axis=0,
            )

        far = None
        states = jnp.concatenate(states, axis=1)
        for far_num in range(far_levels):
            state = states[:, far_num * state_rows : (far_num + 1) * state_rows]
            state = jnp.where(jnp.right_shift(mine, far_num) % 2 == 1, state, jnp.zeros_like(state))
            high = state.astype(BF16)
            low = (state - high.astype(F32)).astype(BF16)
            reading = dot_last(jnp.concatenate([high, low], axis=1), twice)
            reading = weight(near_levels + far_num, 0, length) * reading
            far = reading if far is None else far + reading
        for t0 in range(0, length, rows):
            total = far[:, t0 : t0 + rows] + jnp.concatenate(
                [
                    jnp.dot(
                        values[head * head_size - c0 : (head + 1) * head_size - c0, t0 : t0 + rows],
                        near_ref[head, t0 : t0 + rows, :],
                        preferred_element_type=F32,
                    )
                    for head in heads
                ],
                axis=0,
            )
            for level in range(rows.bit_length(), near_levels):
                span = 1 << level - 1
                if t0 & span:
                    s0 = t0 // span * span - span
                    mixed = jnp.dot(
                        values[:, s0 : s0 + span],
                        score_ref[s0 : s0 + span, t0 : t0 + rows],
                        preferred_element_type=F32,
                    )
                    total = total + weight(level, t0, t0 + rows) * mixed
            out_ref[t0 : t0 + rows, :] = total.astype(BF16).T
        if final:
            store(out_ref, c0)
    for started in stores:
        started.wait()


def finish(
    values, states, offset, last, token_pieces, sum_pieces, queries, level_weight, near, head_size, carried, final
):
    width, length = values.shape
    step = min(256, width)
    flat_sums = [piece for pieces in sum_pieces for piece in pieces]
    parts = [part for _, part in last]
    held = [array for _, array in carried]
    arrays = [*token_pieces, *flat_sums, *parts, values, *states, queries, level_weight, *near, *held]
    scratch = []
    if last:
        depth = parts[0].shape[1]
        scratch = [pltpu.VMEM((rows, depth), BF16) for rows in [length, *(s.shape[1] for s in states)]]
    starts = [start + c0 for start, part in last for c0 in range(0, part.shape[0], step)]
    if final:
        scratch += [pltpu.SemaphoreType.DMA((max(1, width // step),)), pltpu.VMEM((length, width), BF16)]
        outs = dict(
            out_shape=jax.ShapeDtypeStruct((length, width), BF16),
            out_specs=pl.BlockSpec(memory_space=pltpu.HBM),
        )
    else:
        outs = dict(out_shape=[pltpu.VMEM((length, step), BF16)] * len(starts))
    out = pl.pallas_call(
        functools.partial(
            finish_kernel,
            len(token_pieces),
            len(states),
            offset,
            [start for start, _ in last],
            [start for start, _ in carried],
            final,
            head_size,
        ),
        in_specs=[pl.BlockSpec(memory_space=pltpu.VMEM)] * len(arrays),
        scratch_shapes=scratch,
        compiler_params=pltpu.CompilerParams(vmem_limit_bytes=24 << 20),
        name="finish",
        **outs,
    )(*arrays)
    return out if final else list(zip(starts, out))


def body(tokens, value_weight, queries, key_vectors, level_weight):
    _, width_feat = tokens.shape
    depth, width_local = value_weight.shape
    head_local = level_weight.shape[1]
    head_size = width_local // head_local
    ctx_count = lax.axis_size("ctx")
    dev_bits = ctx_count.bit_length() - 1
    near = prepare(queries, key_vectors, level_weight)

    running, sent, held, *turned = begin(key_vectors, tokens, value_weight, 2)
    level_sums = []
    for section_bit in range(dev_bits):
        if section_bit > 0:
            sent = running.astype(BF16)
        if section_bit == dev_bits - 1 and dev_bits > 1:
            break
        partner = from_partner(sent, "ctx", section_bit)
        level_sums.append(partner)
        running = running + partner.astype(F32)
    if dev_bits > 1:
        unit = ctx_count // 4
        for hop in range(2):
            route = [((1 + hop) * unit + num, (2 + hop) * unit + num) for num in range(unit)]
            sent = lax.ppermute(sent, "ctx", route)
            top = sent if hop == 0 else top + sent
        level_sums.append(top)
    low_sums = jnp.concatenate(level_sums[:-1] or level_sums, axis=0)
    top_sums = level_sums[-1:] if dev_bits > 1 else []

    if depth % 256 or width_feat % depth:
        features = lax.all_gather(tokens, "head", axis=1, tiled=True)
        level_sums = jnp.concatenate([low_sums, *top_sums], axis=0)
        sums = lax.all_gather(level_sums, "head", axis=1, tiled=True)
        weight = lax.all_gather(value_weight, "ctx", axis=0, tiled=True)
        values = jnp.einsum("fc,tf->ct", weight, features, preferred_element_type=F32)
        states = jnp.einsum("fc,nf->cn", weight, sums, preferred_element_type=F32)
        return finish(
            values, [states], 0, [], [], [[]], queries, level_weight, near, head_size, [], True
        )

    order = ring_order(ctx_count)
    ahead = [(order[i], order[(i + 1) % ctx_count]) for i in range(ctx_count)]
    back = [(b, a) for a, b in ahead]
    half_count = ctx_count // 2
    token_pieces = on_chip(*gather_pieces(held, "head"))
    sum_pieces = [on_chip(*gather_pieces(low_sums, "head"))]
    sum_pieces += [on_chip(*gather_pieces(sums, "head")) for sums in top_sums]
    cw = ccw = tuple(turned)
    steps = [[(0, cw)]]

    def move(part, route):
        return lax.ppermute(part, "ctx", route)

    for step in range(1, half_count):
        cw = tuple(move(part, ahead) for part in cw)
        ccw = tuple(move(part, back) for part in ccw)
        steps.append([(-step, on_chip(*cw)), (step, on_chip(*ccw))])
    share = width_local // 4
    parts = [*cut([cw[0]]), *cut([ccw[1]])]
    last = [
        [(num * share, move(parts[num], ahead)), ((2 + num) * share, move(parts[2 + num], back))]
        for num in range(2)
    ]
    values = extend([], [token_pieces], steps[0] + steps[1])
    for step in range(2, half_count - 1):
        values = extend(values, [token_pieces], steps[step])
    early = [part for parts in steps[:-1] for part in parts]
    low = extend([], sum_pieces[:1], early)
    values, low = extend([*values, *low], [token_pieces, sum_pieces[0]], steps[-1])
    top = [extend([], [pieces], early + steps[-1])[0] for pieces in sum_pieces[1:]]
    states = [low, *top]
    carried = []
    for num, parts in enumerate(last):
        starts = [start for start, _ in parts]
        done = finish(
            values,
            states,
            half_count,
            list(zip(starts, on_chip(*(part for _, part in parts)))),
            token_pieces,
            sum_pieces,
            queries,
            level_weight,
            near,
            head_size,
            carried,
            num == len(last) - 1,
        )
        carried = done
    return done


def solution(mesh):
    return jax.shard_map(
        body,
        mesh=mesh,
        in_specs=(
            P("ctx", "head"),
            P("ctx", "head"),
            P("ctx", None),
            P("ctx", None),
            P(None, "head", "ctx"),
        ),
        out_specs=P("ctx", "head"),
        check_vma=False,
    )
```

```python
import functools

import jax
import jax.numpy as jnp
from jax import lax
from jax.experimental import pallas as pl
from jax.experimental.pallas import tpu as pltpu
from jax.sharding import PartitionSpec as P


F32 = jnp.float32
BF16 = jnp.bfloat16


def from_partner(block, axis, distance):
    count = lax.axis_size(axis)
    route = []
    for low in range(count):
        high = low | 1 << distance
        if high != low and high < count:
            route += [(low, high), (high, low)]
    return lax.ppermute(block, axis, route)


def gather_pieces(block, axis):
    pieces = [block]
    masks = [0]
    for bit in reversed(range(lax.axis_size(axis).bit_length() - 1)):
        for mask, piece in zip(list(masks), list(pieces)):
            pieces.append(from_partner(piece, axis, bit))
            masks.append(mask | 1 << bit)
    return [piece for _, piece in sorted(zip(masks, pieces), key=lambda pair: pair[0])]


def level_scale(level_num):
    return 1.0 if level_num == 0 else 2.0 ** (-(level_num - 1) / 2.0)


def on_chip(*arrays):
    return [pltpu.with_memory_space_constraint(array, pltpu.VMEM) for array in arrays]


def off_chip(*arrays):
    return [pltpu.with_memory_space_constraint(array, pltpu.HBM) for array in arrays]


def dot_last(left, right):
    return lax.dot_general(left, right, (((1,), (1,)), ((), ())), preferred_element_type=F32)


def spread_rows(row, count):
    return jnp.broadcast_to(row, (count, row.shape[1]))


def prepare_kernel(q_hbm, k_hbm, w_hbm, near_ref, score_ref, row_ref, q_ref, k_ref, w_ref, sems):
    loads = [
        pltpu.make_async_copy(source, target, sems.at[num])
        for num, (source, target) in enumerate([(q_hbm, q_ref), (k_hbm, k_ref), (w_hbm, w_ref)])
    ]
    for load in loads:
        load.start()
    for load in loads:
        load.wait()
    length = q_ref.shape[0]
    heads, _, rows = near_ref.shape
    tile = min(128, length)
    sub = 8
    tile_levels = tile.bit_length() - 1
    sub_levels = sub.bit_length() - 1
    score_ref[...] = dot_last(k_ref[...], q_ref[...]).astype(BF16)
    for num in range(rows.bit_length()):
        for head in range(heads):
            row_ref[head, num : num + 1, :] = w_ref[num, head : head + 1, :] * level_scale(num)

    def grid_level(shape, shift):
        s_pos = lax.broadcasted_iota(jnp.int32, shape, 0)
        t_pos = jnp.right_shift(lax.broadcasted_iota(jnp.int32, shape, 1), shift)
        if shift == 0:
            t_pos = jnp.bitwise_and(t_pos, sub - 1)
        differ = jnp.bitwise_xor(s_pos, t_pos)
        level = jnp.zeros(shape, jnp.int32)
        for bit in range(tile_levels):
            level = level + (jnp.right_shift(differ, bit) > 0).astype(jnp.int32)
        return jnp.where(s_pos <= t_pos, level, -1)

    fine = grid_level((sub, tile), 0)
    coarse = grid_level((tile // sub, tile), sub_levels)
    near_diag = lax.broadcasted_iota(jnp.int32, (tile, tile), 0) // sub == (
        lax.broadcasted_iota(jnp.int32, (tile, tile), 1) // sub
    )

    def one_head(head, carry):
        for t0 in range(0, length, tile):
            base = t0 // rows * rows
            weight_rows = [
                row_ref[head, num : num + 1, t0 : t0 + tile] for num in range(rows.bit_length())
            ]
            for s0 in range(base, base + rows, tile):
                place_at = (head, pl.ds(s0, tile), pl.ds(t0 - base, tile))
                if s0 > t0:
                    near_ref[place_at] = jnp.zeros((tile, tile), BF16)
                    continue
                if s0 == t0:
                    small = jnp.zeros((sub, tile), F32)
                    for num in range(sub_levels + 1):
                        small = jnp.where(fine == num, spread_rows(weight_rows[num], sub), small)
                    big = jnp.zeros((tile // sub, tile), F32)
                    for num in range(sub_levels + 1, tile_levels + 1):
                        big = jnp.where(
                            coarse == num - sub_levels,
                            spread_rows(weight_rows[num], tile // sub),
                            big,
                        )
                    big = jnp.concatenate(
                        [spread_rows(big[row : row + 1], sub) for row in range(tile // sub)], axis=0
                    )
                    weight = jnp.where(near_diag, jnp.concatenate([small] * (tile // sub), 0), big)
                else:
                    num = tile_levels + (s0 // tile ^ t0 // tile).bit_length()
                    weight = spread_rows(weight_rows[num], tile)
                score = score_ref[s0 : s0 + tile, t0 : t0 + tile].astype(F32)
                near_ref[place_at] = (weight * score).astype(BF16)
        return carry

    lax.fori_loop(0, heads, one_head, 0)


def prepare(queries, key_vectors, level_weight):
    length = queries.shape[0]
    heads = level_weight.shape[1]
    rows = min(256, length)
    return pl.pallas_call(
        prepare_kernel,
        in_specs=[pl.BlockSpec(memory_space=pltpu.HBM)] * 3,
        out_shape=[
            pltpu.VMEM((heads, length, rows), BF16),
            pltpu.VMEM((length, length), BF16),
        ],
        scratch_shapes=[
            pltpu.VMEM((heads, rows.bit_length(), length), F32),
            pltpu.VMEM(queries.shape, queries.dtype),
            pltpu.VMEM(key_vectors.shape, key_vectors.dtype),
            pltpu.VMEM(level_weight.shape, level_weight.dtype),
            pltpu.SemaphoreType.DMA((3,)),
        ],
        compiler_params=pltpu.CompilerParams(vmem_limit_bytes=16 << 20),
        name="prepare",
    )(*off_chip(queries, key_vectors, level_weight))


def begin_kernel(k_hbm, token_hbm, weight_hbm, sum_ref, sent_ref, held_ref, *rest):
    part_refs, (k_ref, weight_ref, sems) = rest[:-3], rest[-3:]
    loads = [
        pltpu.make_async_copy(source, target, sems.at[num])
        for num, (source, target) in enumerate(
            [(k_hbm, k_ref), (token_hbm, held_ref), (weight_hbm, weight_ref)]
        )
    ]
    for load in loads:
        load.start()
    loads[0].wait()
    loads[1].wait()
    total = lax.dot_general(
        k_ref[...], held_ref[...], (((0,), (0,)), ((), ())), preferred_element_type=F32
    )
    sum_ref[...] = total
    sent_ref[...] = total.astype(BF16)
    loads[2].wait()
    share = part_refs[0].shape[0]
    for num, part_ref in enumerate(part_refs):
        part_ref[...] = weight_ref[:, num * share : (num + 1) * share].T


def begin(key_vectors, tokens, weight, split):
    depth, width = weight.shape
    shape = (key_vectors.shape[1], tokens.shape[1])
    return pl.pallas_call(
        begin_kernel,
        in_specs=[pl.BlockSpec(memory_space=pltpu.HBM)] * 3,
        out_shape=[
            pltpu.VMEM(shape, F32),
            pltpu.VMEM(shape, BF16),
            pltpu.VMEM(tokens.shape, tokens.dtype),
        ]
        + [pltpu.VMEM((width // split, depth), weight.dtype)] * split,
        scratch_shapes=[
            pltpu.VMEM(key_vectors.shape, key_vectors.dtype),
            pltpu.VMEM(weight.shape, weight.dtype),
            pltpu.SemaphoreType.DMA((3,)),
        ],
        compiler_params=pltpu.CompilerParams(vmem_limit_bytes=8 << 20),
        name="begin",
    )(*off_chip(key_vectors, tokens, weight))


def cut_kernel(count, *refs):
    for num in range(count):
        block_ref, parts = refs[num], refs[count + 2 * num :][:2]
        rows = parts[0].shape[0]
        parts[0][...] = block_ref[:rows, :]
        parts[1][...] = block_ref[rows:, :]


def cut(blocks):
    return pl.pallas_call(
        functools.partial(cut_kernel, len(blocks)),
        in_specs=[pl.BlockSpec(memory_space=pltpu.VMEM)] * len(blocks),
        out_shape=[
            pltpu.VMEM((block.shape[0] // 2, block.shape[1]), block.dtype)
            for block in blocks
            for _ in range(2)
        ],
        compiler_params=pltpu.CompilerParams(vmem_limit_bytes=4 << 20),
    )(*blocks)


def ring_order(count):
    return list(range(0, count, 2)) + list(range(1, count, 2))[::-1]


def place(offset, depth, piece_width):
    count = lax.axis_size("ctx")
    mine = lax.axis_index("ctx")
    pos = jnp.where(mine % 2 == 0, mine // 2, count - 1 - mine // 2)
    pos = (pos + offset + count) % count
    index = jnp.where(pos < count // 2, 2 * pos, 2 * (count - 1 - pos) + 1)
    per_piece = piece_width // depth
    return jnp.bitwise_xor(index // per_piece, lax.axis_index("head")), index % per_piece * depth


def choose(offsets, pieces, depth, chosen_ref):
    for num, offset in enumerate(offsets):
        piece, start = place(offset, depth, pieces[0].shape[1])
        start = pl.multiple_of(start, 128)
        for index, ref in enumerate(pieces):

            @pl.when(piece == index)
            def _():
                chosen_ref[:, num * depth : (num + 1) * depth] = ref[:, pl.ds(start, depth)]


def extend_kernel(sizes, offsets, split, started, *refs):
    refs = list(refs)
    take = lambda count: [refs.pop(0) for _ in range(count)]
    groups = [take(size) for size in sizes]
    blocks = [take(split) for _ in offsets]
    totals = take(len(sizes)) if started else []
    out_refs, chosen_refs = take(len(sizes)), refs
    share, depth = blocks[0][0].shape
    for pieces, chosen_ref in zip(groups, chosen_refs):
        choose(offsets, pieces, depth, chosen_ref)
    step = min(256, share)
    for c0 in range(0, share * split, step):
        at = c0 % share
        left = jnp.concatenate(
            [block[c0 // share][at : at + step, :] for block in blocks], axis=1
        )
        for num, (out_ref, chosen_ref) in enumerate(zip(out_refs, chosen_refs)):
            total = dot_last(left, chosen_ref[...])
            if started:
                total = total + totals[num][c0 : c0 + step, :]
            out_ref[c0 : c0 + step, :] = total


def extend(totals, groups, parts):
    offsets = tuple(offset for offset, _ in parts)
    blocks = [half for _, block in parts for half in block]
    split = len(parts[0][1])
    share, depth = blocks[0].shape
    arrays = [*(piece for pieces in groups for piece in pieces), *blocks, *totals]
    rows = [pieces[0].shape[0] for pieces in groups]
    return pl.pallas_call(
        functools.partial(
            extend_kernel, [len(pieces) for pieces in groups], offsets, split, len(totals) > 0
        ),
        in_specs=[pl.BlockSpec(memory_space=pltpu.VMEM)] * len(arrays),
        out_shape=[pltpu.VMEM((share * split, count), F32) for count in rows],
        scratch_shapes=[pltpu.VMEM((count, depth * len(parts)), BF16) for count in rows],
        compiler_params=pltpu.CompilerParams(vmem_limit_bytes=12 << 20),
    )(*arrays)


def finish_kernel(piece_count, groups, offset, last_at, carried_at, final, head_size, *refs):
    last_count = len(last_at)
    refs = list(refs)
    take = lambda count: [refs.pop(0) for _ in range(count)]
    token_refs, sum_refs = take(piece_count), [take(piece_count) for _ in range(groups)]
    last_refs = take(last_count)
    value_ref, state_refs = refs.pop(0), take(groups)
    q_ref, w_ref, near_ref, score_ref = take(4)
    carried_refs = take(len(carried_at))
    width = value_ref.shape[0]
    step = min(256, width)
    columns = [(c0, None) for c0 in range(0, width, step)]
    if last_count:
        columns = [
            (start + c0, ref.at[c0 : c0 + step, :])
            for start, ref in zip(last_at, last_refs)
            for c0 in range(0, ref.shape[0], step)
        ]
    out_refs = take(1 if final else len(columns))
    stores = []
    if final:
        held_ref, sems = refs.pop(), refs.pop()

        def store(source, start):
            stores.append(
                pltpu.make_async_copy(
                    source, out_refs[0].at[:, start : start + step], sems.at[len(stores)]
                )
            )
            stores[-1].start()

        for start, ref in zip(carried_at, carried_refs):
            store(ref, start)
    length, state_rows = q_ref.shape
    near_levels = length.bit_length()
    far_levels = w_ref.shape[0] - near_levels
    rows = near_ref.shape[2]
    if last_count:
        token_chosen, *sum_chosen = refs
        depth = token_chosen.shape[1]
        choose([offset], token_refs, depth, token_chosen)
        for pieces, chosen in zip(sum_refs, sum_chosen):
            choose([offset], pieces, depth, chosen)
    mine = lax.axis_index("ctx")
    queries = q_ref[...]
    twice = jnp.concatenate([queries, queries], axis=1)
    for num, (c0, last_ref) in enumerate(columns):
        out_ref = held_ref.at[:, c0 : c0 + step] if final else out_refs[num]
        values = value_ref[c0 : c0 + step, :]
        states = [ref[c0 : c0 + step, :] for ref in state_refs]
        if last_count:
            left = last_ref[...]
            values = values + dot_last(left, token_chosen[...])
            states = [
                part + dot_last(left, chosen[...]) for part, chosen in zip(states, sum_chosen)
            ]
        values = values.astype(BF16)
        heads = range(c0 // head_size, (c0 + step) // head_size)

        def weight(level, low, high):
            return jnp.concatenate(
                [
                    spread_rows(
                        w_ref[level, head : head + 1, low:high] * level_scale(level), head_size
                    )
                    for head in heads
                ],
                axis=0,
            )

        far = None
        states = jnp.concatenate(states, axis=1)
        for far_num in range(far_levels):
            state = states[:, far_num * state_rows : (far_num + 1) * state_rows]
            state = jnp.where(jnp.right_shift(mine, far_num) % 2 == 1, state, jnp.zeros_like(state))
            high = state.astype(BF16)
            low = (state - high.astype(F32)).astype(BF16)
            reading = dot_last(jnp.concatenate([high, low], axis=1), twice)
            reading = weight(near_levels + far_num, 0, length) * reading
            far = reading if far is None else far + reading
        for t0 in range(0, length, rows):
            total = far[:, t0 : t0 + rows] + jnp.concatenate(
                [
                    jnp.dot(
                        values[head * head_size - c0 : (head + 1) * head_size - c0, t0 : t0 + rows],
                        near_ref[head, t0 : t0 + rows, :],
                        preferred_element_type=F32,
                    )
                    for head in heads
                ],
                axis=0,
            )
            for level in range(rows.bit_length(), near_levels):
                span = 1 << level - 1
                if t0 & span:
                    s0 = t0 // span * span - span
                    mixed = jnp.dot(
                        values[:, s0 : s0 + span],
                        score_ref[s0 : s0 + span, t0 : t0 + rows],
                        preferred_element_type=F32,
                    )
                    total = total + weight(level, t0, t0 + rows) * mixed
            out_ref[t0 : t0 + rows, :] = total.astype(BF16).T
        if final:
            store(out_ref, c0)
    for started in stores:
        started.wait()


def finish(
    values, states, offset, last, token_pieces, sum_pieces, queries, level_weight, near, head_size, carried, final
):
    width, length = values.shape
    step = min(256, width)
    flat_sums = [piece for pieces in sum_pieces for piece in pieces]
    parts = [part for _, part in last]
    held = [array for _, array in carried]
    arrays = [*token_pieces, *flat_sums, *parts, values, *states, queries, level_weight, *near, *held]
    scratch = []
    if last:
        depth = parts[0].shape[1]
        scratch = [pltpu.VMEM((rows, depth), BF16) for rows in [length, *(s.shape[1] for s in states)]]
    starts = [start + c0 for start, part in last for c0 in range(0, part.shape[0], step)]
    if final:
        scratch += [pltpu.SemaphoreType.DMA((max(1, width // step),)), pltpu.VMEM((length, width), BF16)]
        outs = dict(
            out_shape=jax.ShapeDtypeStruct((length, width), BF16),
            out_specs=pl.BlockSpec(memory_space=pltpu.HBM),
        )
    else:
        outs = dict(out_shape=[pltpu.VMEM((length, step), BF16)] * len(starts))
    out = pl.pallas_call(
        functools.partial(
            finish_kernel,
            len(token_pieces),
            len(states),
            offset,
            [start for start, _ in last],
            [start for start, _ in carried],
            final,
            head_size,
        ),
        in_specs=[pl.BlockSpec(memory_space=pltpu.VMEM)] * len(arrays),
        scratch_shapes=scratch,
        compiler_params=pltpu.CompilerParams(vmem_limit_bytes=24 << 20),
        name="finish",
        **outs,
    )(*arrays)
    return out if final else list(zip(starts, out))


def body(tokens, value_weight, queries, key_vectors, level_weight):
    _, width_feat = tokens.shape
    depth, width_local = value_weight.shape
    head_local = level_weight.shape[1]
    head_size = width_local // head_local
    ctx_count = lax.axis_size("ctx")
    dev_bits = ctx_count.bit_length() - 1
    near = prepare(queries, key_vectors, level_weight)

    running, sent, held, *turned = begin(key_vectors, tokens, value_weight, 2)
    level_sums = []
    for section_bit in range(dev_bits):
        if section_bit > 0:
            sent = running.astype(BF16)
        if section_bit == dev_bits - 1 and dev_bits > 1:
            break
        partner = from_partner(sent, "ctx", section_bit)
        level_sums.append(partner)
        running = running + partner.astype(F32)
    if dev_bits > 1:
        unit = ctx_count // 4
        for hop in range(2):
            route = [((1 + hop) * unit + num, (2 + hop) * unit + num) for num in range(unit)]
            sent = lax.ppermute(sent, "ctx", route)
            top = sent if hop == 0 else top + sent
        level_sums.append(top)
    low_sums = jnp.concatenate(level_sums[:-1] or level_sums, axis=0)
    top_sums = level_sums[-1:] if dev_bits > 1 else []

    if depth % 256 or width_feat % depth:
        features = lax.all_gather(tokens, "head", axis=1, tiled=True)
        level_sums = jnp.concatenate([low_sums, *top_sums], axis=0)
        sums = lax.all_gather(level_sums, "head", axis=1, tiled=True)
        weight = lax.all_gather(value_weight, "ctx", axis=0, tiled=True)
        values = jnp.einsum("fc,tf->ct", weight, features, preferred_element_type=F32)
        states = jnp.einsum("fc,nf->cn", weight, sums, preferred_element_type=F32)
        return finish(
            values, [states], 0, [], [], [[]], queries, level_weight, near, head_size, [], True
        )

    order = ring_order(ctx_count)
    ahead = [(order[i], order[(i + 1) % ctx_count]) for i in range(ctx_count)]
    back = [(b, a) for a, b in ahead]
    half_count = ctx_count // 2
    token_pieces = on_chip(*gather_pieces(held, "head"))
    sum_pieces = [on_chip(*gather_pieces(low_sums, "head"))]
    sum_pieces += [on_chip(*gather_pieces(sums, "head")) for sums in top_sums]
    cw = ccw = tuple(turned)
    steps = [[(0, cw)]]

    def move(part, route):
        return lax.ppermute(part, "ctx", route)

    for step in range(1, half_count):
        cw = tuple(move(part, ahead) for part in cw)
        ccw = tuple(move(part, back) for part in ccw)
        steps.append([(-step, on_chip(*cw)), (step, on_chip(*ccw))])
    share = width_local // 4
    parts = [*cut([cw[0]]), *cut([ccw[1]])]
    last = [
        [(num * share, move(parts[num], ahead)), ((2 + num) * share, move(parts[2 + num], back))]
        for num in range(2)
    ]
    values = extend([], [token_pieces], steps[0] + steps[1])
    for step in range(2, half_count - 1):
        values = extend(values, [token_pieces], steps[step])
    early = [part for parts in steps[:-1] for part in parts]
    low = extend([], sum_pieces[:1], early)
    top = [extend([], [pieces], early)[0] for pieces in sum_pieces[1:]]
    values, *states = extend([*values, *low, *top], [token_pieces, *sum_pieces], steps[-1])
    carried = []
    for num, parts in enumerate(last):
        starts = [start for start, _ in parts]
        done = finish(
            values,
            states,
            half_count,
            list(zip(starts, on_chip(*(part for _, part in parts)))),
            token_pieces,
            sum_pieces,
            queries,
            level_weight,
            near,
            head_size,
            carried,
            num == len(last) - 1,
        )
        carried = done
    return done


def solution(mesh):
    return jax.shard_map(
        body,
        mesh=mesh,
        in_specs=(
            P("ctx", "head"),
            P("ctx", "head"),
            P("ctx", None),
            P("ctx", None),
            P(None, "head", "ctx"),
        ),
        out_specs=P("ctx", "head"),
        check_vma=False,
    )
```
